32 devices in a mesh: replica: 2 (over core), shard: 16 (over z, y, x).
Axes of the slice: x: 2, y: 2, z: 4, core: 2. Of those that a mesh axis runs over, the one named last changes fastest.
Arguments:
- inputs: bfloat16 [32768, 768], P(('replica', 'shard')), may hold values from -6 to 6
- cotangent: bfloat16 [32768, 768], P(('replica', 'shard')), may hold values from -6 to 6
- block_ids: int32 [32, 1024], P(('replica', 'shard')), may hold values from 0 to 3, never falling along the last dimension, each value on 1 to 512 neighbouring positions
- buckets: int32 [2047], replicated, may hold values from 0 to 31
- early_gain: float32 [768], replicated, may hold values from 0.25 to 1.75
- query_weight: bfloat16 [768, 768], P('shard'), may hold values from -0.109375 to 0.109375
- key_weight: bfloat16 [768, 768], P('shard'), may hold values from -0.109375 to 0.109375
- value_weight: bfloat16 [768, 768], P('shard'), may hold values from -0.21875 to 0.21875
- mixing_weight: bfloat16 [768, 768], P('shard'), may hold values from -0.875 to 0.875
- relative_table: float32 [32, 12], replicated, may hold values from -4 to 4
- later_gain: float32 [768], replicated, may hold values from 0.25 to 1.75
- up_weight: bfloat16 [768, 3072], P('shard'), may hold values from -0.21875 to 0.21875
- down_weight: bfloat16 [3072, 768], P('shard'), may hold values from -0.109375 to 0.109375
Outputs:
- layer_output: bfloat16 [32768, 768], P(('replica', 'shard'))
- input_gradient: bfloat16 [32768, 768], P(('replica', 'shard'))
- early_gradient: float32 [768], replicated
- query_gradient: float32 [768, 768], P('shard')
- key_gradient: float32 [768, 768], P('shard')
- value_gradient: float32 [768, 768], P('shard')
- mixing_gradient: float32 [768, 768], P('shard')
- table_gradient: float32 [32, 12], replicated
- later_gradient: float32 [768], replicated
- up_gradient: float32 [768, 3072], P('shard')
- down_gradient: float32 [3072, 768], P('shard')
The draws below stay inside these ranges and needn't reach their ends.
Inputs may be any that keep to these rules, and one draw needn't show every extreme that they name: `block_ids`: along the positions of each sequence the passage numbers never fall; a passage holds at most 512 tokens.
All inputs are finite; a program needn't handle non-finite values.
Results may differ from the reference program's by a relative error of at most 0.019.
Values may be sent and summed in bfloat16 or wider, within the bound.
No kernel may reach another device: no remote copies, remote signals or barrier semaphores. Data moves between devices by JAX's collectives and lax.ppermute only.
A program may use at most 192 MiB of HBM per device.

```python
import math
import jax
import jax.numpy as jnp
import numpy as np
from jax import lax

D = 768
HEADS = 12
HEAD_DIM = 64
FF = 3072
BUCKETS = 32
LEN = 1024
PASSAGE = 256
SEQS = 32
TOKENS = 32768
OFFSETS = 2047


def with_ends(drawn, rng, low, high):
    spot = [jax.random.randint(jax.random.fold_in(rng, axis), (), 0, length) for axis, length in enumerate(drawn.shape)]
    main_axis = drawn.shape.index(max(drawn.shape))
    neighbour = spot[:main_axis] + [(spot[main_axis] + 1) % drawn.shape[main_axis]] + spot[main_axis + 1:]
    return drawn.at[tuple(spot)].set(low).at[tuple(neighbour)].set(high)


def strengthened(array, stream_key, source, target, parts, factor):
    owner, partner = [(jnp.arange(array.shape[axis_at]) // (array.shape[axis_at] // parts)).reshape([-1 if axis == axis_at else 1 for axis in range(array.ndim)]) for axis_at in (source, target)]
    chosen = jax.random.permutation(stream_key, parts)[partner]
    strong = (owner == chosen) | (owner == (partner + parts // 2) % parts)
    return jnp.where(strong, factor * array, array)


def level_of(key, extent, pieces, smallest, top_value):
    def one(position, shards_of):
        steps = jax.random.uniform(jax.random.fold_in(jax.random.fold_in(key, 6), position), (shards_of,), jnp.float32, smallest / len(pieces), top_value / len(pieces))
        return jnp.repeat(jnp.exp(steps), extent[position] // shards_of).reshape((-1,) + (1,) * (len(extent) - position - 1))

    factor_of = one(*pieces[0])
    for cut in pieces[1:]:
        factor_of = factor_of * one(*cut)
    return factor_of


def length_profile(count, total, reach, skew):
    portions = [(1 << 20) // math.isqrt(grade ** skew) + 1 for grade in range(2, count + 1)]
    surplus, holding = total - reach - (count - 1), [1] * (count - 1)
    while surplus > 0:
        candidates = [i for i in range(count - 1) if holding[i] < reach]
        whole, budget = sum([portions[i] for i in candidates]), surplus
        for i in candidates:
            extra = min(reach - holding[i], max(1, budget * portions[i] // whole), surplus)
            holding[i] = holding[i] + extra
            surplus = surplus - extra
    return np.array([reach] + holding)


def uneven(stream_key, number_of, total, reach, lean):
    if number_of == 2:
        one = jax.random.randint(stream_key, (), max(1, total - reach), min(reach, total - 1) + 1)
        return jnp.stack([one, total - one])
    lengths = jnp.asarray(length_profile(number_of, total, reach, lean), jnp.int32)
    couples = (number_of - 1) // 2
    giver, sink = lengths[1:1 + 2 * couples:2], lengths[2:2 + 2 * couples:2]
    room = jnp.minimum(giver - 1, reach - sink)
    passed = jax.random.randint(jax.random.fold_in(stream_key, 1), (couples,), 0, 1 << 20) % (room + 1)
    lengths = lengths.at[1:1 + 2 * couples:2].set(giver - passed).at[2:2 + 2 * couples:2].set(sink + passed)
    return lengths[jax.random.permutation(jax.random.fold_in(stream_key, 2), number_of)]


def centred(stream_key, shape, deviation, limit, split=(), kind=jnp.bfloat16):
    factor_of = level_of(stream_key, shape, split, -0.22, 0.18) if split else 1.0
    values = jax.random.normal(stream_key, shape, jnp.float32) * deviation * factor_of
    return jnp.minimum(jnp.maximum(values, -limit), limit).astype(kind)


def gaussian_with(own_key, shape, spread, bound, pieces, heavy, kind=jnp.bfloat16):
    array = spread * jax.random.normal(own_key, shape, jnp.float32)
    if pieces:
        array = array * level_of(own_key, shape, pieces, -0.22, 0.18)
    return jnp.clip(strengthened(array, jax.random.fold_in(own_key, 3), *heavy), -bound, bound).astype(kind)


def setup_inputs(seed: int = 0) -> dict:
    key_list = jax.random.split(jax.random.key(seed), 14)
    inputs = gaussian_with(key_list[0], (TOKENS, D), 1.0, 6.0, ((0, 32),), (0, 1, 32, 2.75))
    cotangent = centred(key_list[1], (TOKENS, D), 1.0, 6.0, ((0, 32),))
    block_ids = jax.vmap(lambda own: jnp.searchsorted(jnp.cumsum(uneven(own, LEN // PASSAGE, LEN, 2 * PASSAGE, 2)), jnp.arange(LEN), side="right"))(jax.random.split(key_list[2], SEQS)).reshape((SEQS, LEN)).astype(jnp.int32)
    buckets = with_ends(jax.random.randint(key_list[3], (OFFSETS,), 0, BUCKETS), jax.random.fold_in(key_list[3], 1), 0, BUCKETS - 1).astype(jnp.int32)
    early_gain = jnp.clip(1.0 + 0.15 * jax.random.normal(key_list[4], (D,), jnp.float32), 0.25, 1.75)
    query_weight = centred(key_list[5], (D, D), (4 * D) ** -0.5, 0.109375, ((0, 16),))
    key_weight = centred(key_list[6], (D, D), (4 * D) ** -0.5, 0.109375, ((0, 16),))
    value_weight = centred(key_list[7], (D, D), D ** -0.5, 0.21875, ((0, 16),))
    mixing_weight = centred(key_list[8], (D, D), (D // 16) ** -0.5, 0.875, ((0, 16),))
    relative_table = centred(key_list[9], (BUCKETS, HEADS), 1.0, 4.0, (), jnp.float32)
    later_gain = jnp.clip(1.0 + 0.15 * jax.random.normal(key_list[10], (D,), jnp.float32), 0.25, 1.75)
    up_weight = centred(key_list[11], (D, FF), D ** -0.5, 0.21875, ((0, 16),))
    down_weight = centred(key_list[12], (FF, D), FF ** -0.5, 0.109375, ((0, 16),))
    return dict(inputs=inputs, cotangent=cotangent, block_ids=block_ids, buckets=buckets, early_gain=early_gain, query_weight=query_weight, key_weight=key_weight, value_weight=value_weight, mixing_weight=mixing_weight, relative_table=relative_table, later_gain=later_gain, up_weight=up_weight, down_weight=down_weight)


EPS = 1e-06
HIGH = lax.Precision.HIGHEST

@jax.custom_vjp
def low(v):
    return lax.optimization_barrier(v.astype(jnp.bfloat16)).astype(jnp.float32)

@jax.custom_vjp
def low_back(v):
    return v

def low_keep(v):
    return (low(v), None)

def low_pass(kept, grad):
    return (grad,)

def back_keep(v):
    return (v, None)

def back_low(kept, grad):
    return (low(grad),)
low.defvjp(low_keep, low_pass)
low_back.defvjp(back_keep, back_low)

def rounded_both(v):
    return low(low_back(v))

def smooth_gate(v):
    return jax.nn.gelu(v, approximate=True)

def matmul(left, right):
    return jnp.dot(left, right, precision=HIGH, preferred_element_type=left.dtype)

def rms_scale(values, gain):
    scale = lax.rsqrt(lax.optimization_barrier(jnp.mean(values * values, axis=-1, keepdims=True)) + EPS)
    return values * scale * gain

def attend(query_seq, key_seq, value_seq, ids, bias):
    scores = jnp.einsum('qhd,khd->hqk', query_seq, key_seq, precision=HIGH)
    scores = low_back(scores) + bias
    allowed = (ids[None, :] <= ids[:, None])[None]
    masked = jnp.where(allowed, scores, -1000000000.0)
    peak = lax.optimization_barrier(jnp.max(masked, axis=-1, keepdims=True))
    weights = jnp.where(allowed, jnp.exp(masked - peak), 0.0)
    probs = low(weights / lax.optimization_barrier(jnp.sum(weights, axis=-1, keepdims=True)))
    return jnp.einsum('hqk,khd->qhd', probs, value_seq, precision=HIGH)

def layer(block_ids, bucket_grid, values, early, wq, wk, wv, wm, table, later, wup, wdown):
    count = values.shape[0]
    normed = low(rms_scale(values, early))
    queries = rounded_both(matmul(normed, wq))
    key_rows = rounded_both(matmul(normed, wk))
    value_rows = rounded_both(matmul(normed, wv))
    bias = jnp.transpose(jnp.take(table, bucket_grid, axis=0), (2, 0, 1))

    def one_sequence(item):
        query_seq, key_seq, value_seq, ids = item
        return attend(query_seq, key_seq, value_seq, ids, bias)
    shape = (count // LEN, LEN, HEADS, HEAD_DIM)
    attended = lax.map(jax.checkpoint(one_sequence), (queries.reshape(shape), key_rows.reshape(shape), value_rows.reshape(shape), block_ids))
    attended = rounded_both(attended.reshape(count, D))
    state = values + low_back(matmul(attended, wm))
    later_normed = low(rms_scale(state, later))
    activated = low(smooth_gate(low_back(matmul(later_normed, wup))))
    return state + low_back(matmul(activated, wdown))

def reference(inputs, cotangent, block_ids, buckets, early_gain, query_weight, key_weight, value_weight, mixing_weight, relative_table, later_gain, up_weight, down_weight):
    positions = jnp.arange(LEN, dtype=jnp.int32)
    offsets = (positions[None, :] - positions[:, None] + jnp.int32(LEN - 1)).astype(jnp.int32)
    bucket_grid = jnp.take(buckets.astype(jnp.int32), offsets, axis=0).astype(jnp.int32)
    ids = block_ids.astype(jnp.int32)
    floats = (inputs.astype(jnp.float32), early_gain.astype(jnp.float32), query_weight.astype(jnp.float32), key_weight.astype(jnp.float32), value_weight.astype(jnp.float32), mixing_weight.astype(jnp.float32), relative_table.astype(jnp.float32), later_gain.astype(jnp.float32), up_weight.astype(jnp.float32), down_weight.astype(jnp.float32))

    def forward(*params):
        return layer(ids, bucket_grid, *params)
    result, pullback = jax.vjp(forward, *floats)
    grads = pullback(cotangent.astype(jnp.float32))
    return (result.astype(jnp.bfloat16), grads[0].astype(jnp.bfloat16), grads[1], grads[2], grads[3], grads[4], grads[5], grads[6], grads[7], grads[8], grads[9])
```

```python
import functools
import jax
import jax.numpy as jnp
from jax import lax
from jax.experimental import pallas as pl
from jax.experimental.pallas import tpu as pltpu
from jax.sharding import PartitionSpec as P

HEAD_DIM = 64
SLAB = 128
TILE = 256
NEG = -1e30


def nt(left, right):
    return lax.dot_general(left, right, (((1,), (1,)), ((), ())), preferred_element_type=jnp.float32)


def nn(left, right):
    return lax.dot_general(left, right, (((1,), (0,)), ((), ())), preferred_element_type=jnp.float32)


def tn(left, right):
    return lax.dot_general(left, right, (((0,), (0,)), ((), ())), preferred_element_type=jnp.float32)


def skew_kernel(rows_ref, out_ref):
    width = rows_ref.shape[-1]
    keep = out_ref.shape[-1]
    for k in range(rows_ref.shape[0]):
        spread = jnp.broadcast_to(rows_ref[k], (SLAB, width))
        moved = pltpu.roll(spread, width - SLAB + 1, 1, stride=1, stride_axis=0)
        out_ref[k] = moved[:, :keep]


def skew(rows, length):
    count, width = rows.shape
    keep = 2 * length - SLAB
    return pl.pallas_call(
        skew_kernel,
        grid=(count // 2,),
        in_specs=[pl.BlockSpec((2, 1, width), lambda i: (i, 0, 0))],
        out_specs=pl.BlockSpec((2, SLAB, keep), lambda i: (i, 0, 0)),
        out_shape=jax.ShapeDtypeStruct((count, SLAB, keep), jnp.float32),
        compiler_params=pltpu.CompilerParams(vmem_limit_bytes=32 << 20),
    )(rows.reshape(count, 1, width))


def bias_tile(table_ref, k, offset):
    return jnp.concatenate(
        [
            table_ref[k, :, pl.ds(offset, TILE)],
            table_ref[k, :, pl.ds(offset - SLAB, TILE)],
        ],
        axis=0,
    )


def forward_kernel(counts_ref, q_ref, k_ref, v_ref, ends_ref, table_ref, out_ref, log_ref):
    length = q_ref.shape[0]
    tiles = length // TILE
    low = lax.broadcasted_iota(jnp.int32, (TILE, 2 * HEAD_DIM), 1) < HEAD_DIM

    def block(i, n):
        first = pl.multiple_of(i * TILE, TILE)
        query = q_ref[pl.ds(first, TILE), :]
        ends = ends_ref[pl.ds(first, TILE), :]
        keys = k_ref[0 : n * TILE, :]
        values = v_ref[0 : n * TILE, :]
        columns = lax.broadcasted_iota(jnp.int32, (TILE, n * TILE), 1)
        allowed = columns < ends
        outs = []
        zero = jnp.zeros_like(query)
        for k in range(2):
            mine = jnp.where(low, query, zero) if k == 0 else jnp.where(low, zero, query)
            offset = pl.multiple_of((tiles - 1 - i) * TILE + SLAB, SLAB)
            bias = jnp.concatenate(
                [
                    table_ref[k, :, pl.ds(offset, n * TILE)],
                    table_ref[k, :, pl.ds(pl.multiple_of(offset - SLAB, SLAB), n * TILE)],
                ],
                axis=0,
            )
            scores = jnp.where(allowed, nt(mine, keys) + bias, NEG)
            peak = jnp.max(scores, axis=1, keepdims=True)
            weights = jnp.exp(scores - peak)
            total = jnp.sum(weights, axis=1, keepdims=True)
            scaled = nn(weights.astype(jnp.bfloat16), values)
            outs.append(scaled / total)
            logs = jnp.broadcast_to(peak + jnp.log(total), (TILE, SLAB))
            log_ref[0, k : k + 1, pl.ds(first, TILE)] = logs.T[0:1, :]
        out_ref[pl.ds(first, TILE), :] = jnp.where(low, outs[0], outs[1]).astype(out_ref.dtype)

    def step(i, carry):
        count = counts_ref[i]
        for n in range(1, tiles + 1):
            @pl.when(count == n)
            def _():
                block(i, n)
        return carry

    lax.fori_loop(0, tiles, step, 0)


def attend_forward(qkv, ends, counts, table, heads, first_pair, pairs):
    length = qkv.shape[0]
    half = heads // 2
    width = 2 * HEAD_DIM
    keep = table.shape[-1]
    return pl.pallas_call(
        forward_kernel,
        grid_spec=pltpu.PrefetchScalarGridSpec(
            num_scalar_prefetch=1,
            grid=(pairs,),
            in_specs=[
                pl.BlockSpec((length, width), lambda p, c: (0, first_pair + p)),
                pl.BlockSpec((length, width), lambda p, c: (0, half + first_pair + p)),
                pl.BlockSpec((length, width), lambda p, c: (0, 2 * half + first_pair + p)),
                pl.BlockSpec((length, 1), lambda p, c: (0, 0)),
                pl.BlockSpec((2, SLAB, keep), lambda p, c: (first_pair + p, 0, 0)),
            ],
            out_specs=[
                pl.BlockSpec((length, width), lambda p, c: (0, p)),
                pl.BlockSpec((1, 2, length), lambda p, c: (p, 0, 0)),
            ],
        ),
        out_shape=[
            jax.ShapeDtypeStruct((length, pairs * width), jnp.bfloat16),
            jax.ShapeDtypeStruct((pairs, 2, length), jnp.float32),
        ],
        compiler_params=pltpu.CompilerParams(vmem_limit_bytes=48 << 20),
        cost_estimate=pl.CostEstimate(
            flops=pairs * 2 * 4 * length * length * HEAD_DIM * 2,
            bytes_accessed=pairs * (4 * length * width * 2 + 2 * SLAB * keep * 4),
            transcendentals=pairs * 2 * length * length,
        ),
    )(counts, qkv, qkv, qkv, ends, table)


def backward_kernel(
    tiles_ref, q_ref, k_ref, v_ref, out_ref, grad_ref, ends_ref, log_ref, table_ref,
    dq_ref, dk_ref, dv_ref, diag_ref,
    qm, km, gm, dq_acc, dk_acc, dv_acc, skewed, delta,
):
    length = q_ref.shape[0]
    tiles = length // TILE
    width = 2 * HEAD_DIM
    low = lax.broadcasted_iota(jnp.int32, (length, width), 1) < HEAD_DIM
    query, keys, grads = q_ref[...], k_ref[...], grad_ref[...]
    zero = jnp.zeros_like(query)
    for k in range(2):
        pick = low if k == 0 else jnp.logical_not(low)
        qm[k] = jnp.where(pick, query, zero)
        km[k] = jnp.where(pick, keys, zero)
        gm[k] = jnp.where(pick, grads, zero)
    dq_acc[...] = jnp.zeros_like(dq_acc)
    dk_acc[...] = jnp.zeros_like(dk_acc)
    dv_acc[...] = jnp.zeros_like(dv_acc)
    skewed[...] = jnp.zeros_like(skewed)
    product = grads.astype(jnp.float32) * out_ref[...].astype(jnp.float32)
    high = product.astype(jnp.bfloat16)
    rest = (product - high.astype(jnp.float32)).astype(jnp.bfloat16)
    lane = lax.broadcasted_iota(jnp.int32, (16, width), 1)
    row = lax.broadcasted_iota(jnp.int32, (16, width), 0)
    chooser = jnp.where(lane // HEAD_DIM == row, 1.0, 0.0).astype(jnp.bfloat16)
    delta[...] = nt(chooser, high) + nt(chooser, rest)

    def tile(t, carry):
        kb = tiles_ref[1 + 2 * t]
        qb = tiles_ref[2 + 2 * t]
        kf = pl.multiple_of(kb * TILE, TILE)
        qf = pl.multiple_of(qb * TILE, TILE)
        offset = pl.multiple_of((tiles - 1 + qb - kb) * TILE + SLAB, SLAB)
        before = pl.multiple_of(offset - SLAB, SLAB)
        rows = lax.broadcasted_iota(jnp.int32, (TILE, TILE), 0) + kf
        allowed = rows < ends_ref[:, pl.ds(qf, TILE)]
        q_tile = q_ref[pl.ds(qf, TILE), :]
        v_tile = v_ref[pl.ds(kf, TILE), :]
        dk_part = dk_acc[pl.ds(kf, TILE), :]
        dv_part = dv_acc[pl.ds(kf, TILE), :]
        dq_part = dq_acc[pl.ds(qf, TILE), :]
        for k in range(2):
            k_tile = km[k, pl.ds(kf, TILE), :]
            g_tile = gm[k, pl.ds(qf, TILE), :]
            bias = jnp.concatenate(
                [table_ref[k, :, pl.ds(offset, TILE)], table_ref[k, :, pl.ds(before, TILE)]], axis=0
            )
            scores = nt(k_tile, q_tile) + bias - log_ref[0, k : k + 1, pl.ds(qf, TILE)]
            probs = jnp.where(allowed, jnp.exp(scores), 0.0)
            above = nt(v_tile, g_tile) - delta[k : k + 1, pl.ds(qf, TILE)]
            grad = probs * above
            skewed[k, :, pl.ds(offset, TILE)] += grad[:SLAB]
            skewed[k, :, pl.ds(before, TILE)] += grad[SLAB:]
            probs_low = probs.astype(jnp.bfloat16)
            grad_low = grad.astype(jnp.bfloat16)
            dv_part = dv_part + nn(probs_low, g_tile)
            dk_part = dk_part + nn(grad_low, qm[k, pl.ds(qf, TILE), :])
            dq_part = dq_part + tn(grad_low, k_tile)
        dk_acc[pl.ds(kf, TILE), :] = dk_part
        dv_acc[pl.ds(kf, TILE), :] = dv_part
        dq_acc[pl.ds(qf, TILE), :] = dq_part
        return carry

    lax.fori_loop(0, tiles_ref[0], tile, 0)
    dq_ref[...] = dq_acc[...].astype(dq_ref.dtype)
    dk_ref[...] = dk_acc[...].astype(dk_ref.dtype)
    dv_ref[...] = dv_acc[...].astype(dv_ref.dtype)
    lanes = skewed.shape[-1]
    group = lax.broadcasted_iota(jnp.int32, (SLAB, lanes), 0)
    for k in range(2):
        held = skewed[k]
        shift = 1
        while shift < SLAB:
            moved = pltpu.roll(held, shift, 1)
            held = jnp.where(((SLAB - 1 - group) & shift) != 0, moved, held)
            shift *= 2
        diag_ref[0, k : k + 1, :] = jnp.sum(held, axis=0, keepdims=True)


def attend_backward(qkv, out, grad, ends, logs, tile_list, table, heads, first_pair, pairs):
    length = qkv.shape[0]
    half = heads // 2
    width = 2 * HEAD_DIM
    keep = table.shape[-1]
    lanes = 2 * length
    piece = pl.BlockSpec((length, width), lambda p, c: (0, p))
    return pl.pallas_call(
        backward_kernel,
        grid_spec=pltpu.PrefetchScalarGridSpec(
            num_scalar_prefetch=1,
            grid=(pairs,),
            in_specs=[
                pl.BlockSpec((length, width), lambda p, c: (0, first_pair + p)),
                pl.BlockSpec((length, width), lambda p, c: (0, half + first_pair + p)),
                pl.BlockSpec((length, width), lambda p, c: (0, 2 * half + first_pair + p)),
                pl.BlockSpec((length, width), lambda p, c: (0, first_pair + p)),
                pl.BlockSpec((length, width), lambda p, c: (0, first_pair + p)),
                pl.BlockSpec((1, length), lambda p, c: (0, 0)),
                pl.BlockSpec((1, 2, length), lambda p, c: (first_pair + p, 0, 0)),
                pl.BlockSpec((2, SLAB, keep), lambda p, c: (first_pair + p, 0, 0)),
            ],
            out_specs=[piece, piece, piece, pl.BlockSpec((1, 2, lanes), lambda p, c: (p, 0, 0))],
            scratch_shapes=[
                pltpu.VMEM((2, length, width), jnp.bfloat16),
                pltpu.VMEM((2, length, width), jnp.bfloat16),
                pltpu.VMEM((2, length, width), jnp.bfloat16),
                pltpu.VMEM((length, width), jnp.float32),
                pltpu.VMEM((length, width), jnp.float32),
                pltpu.VMEM((length, width), jnp.float32),
                pltpu.VMEM((2, SLAB, lanes), jnp.float32),
                pltpu.VMEM((16, length), jnp.float32),
            ],
        ),
        out_shape=[jax.ShapeDtypeStruct((length, pairs * width), jnp.bfloat16)] * 3
        + [jax.ShapeDtypeStruct((pairs, 2, lanes), jnp.float32)],
        compiler_params=pltpu.CompilerParams(vmem_limit_bytes=48 << 20),
        cost_estimate=pl.CostEstimate(
            flops=pairs * 2 * 10 * length * length * HEAD_DIM * 2,
            bytes_accessed=pairs * (8 * length * width * 2 + 2 * SLAB * keep * 4),
            transcendentals=pairs * 2 * length * length,
        ),
    )(tile_list, qkv, qkv, qkv, out, grad, ends, logs, table)


EPS = 1e-06
HIGH = lax.Precision.HIGHEST
EVERY = ("shard", "replica")


def smooth_gate(v):
    return jax.nn.gelu(v, approximate=True)


def rms_forward(values, gain):
    scale = lax.rsqrt(jnp.mean(values * values, axis=1, keepdims=True) + EPS)
    return (scale, (values * scale * gain).astype(jnp.bfloat16))


def rms_backward(values, scale, gain, upstream):
    gain_part = jnp.sum(upstream * values * scale, axis=0)
    scaled = upstream * gain
    inner = jnp.mean(scaled * values, axis=1, keepdims=True)
    return (scale * (scaled - values * scale * scale * inner), gain_part)


def gather_rows(shard_rows, copies):
    part = shard_rows.shape[0] // copies
    own = lax.dynamic_slice_in_dim(shard_rows, lax.axis_index("replica") * part, part, 0)
    return lax.all_gather(own, EVERY, axis=0, tiled=True)


def scatter_rows(partial):
    part = lax.psum_scatter(partial.astype(jnp.bfloat16), EVERY, scatter_dimension=0, tiled=True)
    return lax.all_gather(part, "replica", axis=0, tiled=True).astype(jnp.float32)


def exchange_rows(partial, copies, shards):
    rows, columns = partial.shape
    wide = columns // copies
    if copies == 2:
        me = lax.axis_index("replica")
        own = lax.dynamic_slice_in_dim(partial, me * wide, wide, 1)
        sent = lax.dynamic_slice_in_dim(partial, (1 - me) * wide, wide, 1).astype(jnp.bfloat16)
        other = lax.ppermute(sent, "replica", [(0, 1), (1, 0)])
        both = own + other.astype(jnp.float32)
    else:
        pieces = partial.astype(jnp.bfloat16).reshape(rows, copies, wide)
        both = lax.all_to_all(pieces, "replica", 1, 0).astype(jnp.float32).sum(axis=0)
    pieces = both.astype(jnp.bfloat16).reshape(shards, rows // shards, wide)
    summed = lax.all_to_all(pieces, "shard", 0, 0).astype(jnp.float32).sum(axis=0)
    return lax.all_gather(summed, "replica", axis=1, tiled=True)


def body(
    copies,
    shards,
    inputs,
    cotangent,
    block_ids,
    buckets,
    early_gain,
    query_weight,
    key_weight,
    value_weight,
    mixing_weight,
    relative_table,
    later_gain,
    up_weight,
    down_weight,
):
    length, width = inputs.shape
    bucket_count, heads = relative_table.shape
    hidden = up_weight.shape[1]
    pairs = heads // 2
    offsets = buckets.shape[0]
    qkv_weight = gather_rows(jnp.concatenate([query_weight, key_weight, value_weight], axis=1), copies)
    mixing_up = gather_rows(jnp.concatenate([mixing_weight, up_weight], axis=1), copies)
    mixing_full, up_full = mixing_up[:, :width], mixing_up[:, width:]
    down_full = gather_rows(down_weight, copies)

    ids = block_ids.reshape(length)
    ends = jnp.sum((ids[None, :] <= ids[:, None]).astype(jnp.int32), axis=1)
    tiles = length // TILE
    last = ends.reshape(tiles, TILE)[:, TILE - 1]
    counts = (last + TILE - 1) // TILE
    key_block = jnp.repeat(jnp.arange(tiles, dtype=jnp.int32), tiles)
    query_block = jnp.tile(jnp.arange(tiles, dtype=jnp.int32), tiles)
    active = (key_block.reshape(tiles, tiles) * TILE < last[None, :]).reshape(-1)
    slot = jnp.arange(tiles * tiles, dtype=jnp.int32)
    place = jnp.sum((slot[None, :] < slot[:, None]) & active[None, :], axis=1, dtype=jnp.int32)
    hit = ((place[None, :] == slot[:, None]) & active[None, :]).astype(jnp.int32)
    listed = jnp.stack(
        [jnp.sum(hit * key_block[None, :], axis=1), jnp.sum(hit * query_block[None, :], axis=1)], axis=1
    ).reshape(-1)
    tile_list = jnp.concatenate([jnp.sum(active.astype(jnp.int32))[None], listed])

    onehot = (buckets[:, None] == jnp.arange(bucket_count, dtype=jnp.int32)[None, :]).astype(jnp.float32)
    bias_rows = jnp.dot(onehot, relative_table, precision=HIGH).T
    spare = ((0, 0), (0, 2 * length - offsets))
    forward_table = skew(jnp.pad(bias_rows, spare), length)
    backward_table = skew(jnp.pad(bias_rows[:, ::-1], spare), length)

    values = inputs.astype(jnp.float32)
    early_scale, normed = rms_forward(values, early_gain)
    qkv = nn(normed, qkv_weight).astype(jnp.bfloat16)
    attended, logs = attend_forward(qkv, ends[:, None], counts, forward_table, heads, 0, pairs)
    state = values + nn(attended, mixing_full)
    later_scale, later_normed = rms_forward(state, later_gain)
    pre_act = nn(later_normed, up_full)
    gate_values, gate_pull = jax.vjp(smooth_gate, pre_act)
    activated = gate_values.astype(jnp.bfloat16)
    layer_output = (state + nn(activated, down_full)).astype(jnp.bfloat16)
    down_share = scatter_rows(tn(activated, cotangent))
    pre_grad = gate_pull(nt(cotangent, down_full))[0].astype(jnp.bfloat16)
    up_grad = tn(later_normed, pre_grad)
    later_normed_grad = nt(pre_grad, up_full)
    state_part, later_part = rms_backward(state, later_scale, later_gain, later_normed_grad)
    state_grad = cotangent.astype(jnp.float32) + state_part
    branch_grad = state_grad.astype(jnp.bfloat16)
    mixing_grad = tn(attended, branch_grad)
    mixing_up_share = scatter_rows(jnp.concatenate([mixing_grad, up_grad], axis=1))
    attended_grad = nt(branch_grad, mixing_full).astype(jnp.bfloat16)
    query_low, key_low, value_low, diagonals = attend_backward(
        qkv, attended, attended_grad, ends[None, :], logs, tile_list, backward_table, heads, 0, pairs
    )
    low = jnp.concatenate([query_low, key_low, value_low], axis=1)
    qkv_share = exchange_rows(tn(normed, low), copies, shards)
    normed_grad = nt(low, qkv_weight)
    input_part, early_part = rms_backward(values, early_scale, early_gain, normed_grad)
    input_gradient = (state_grad + input_part).astype(jnp.bfloat16)
    diagonals = diagonals.reshape(heads, 2 * length)[:, :offsets][:, ::-1]
    table_part = lax.dot_general(onehot, diagonals, (((0,), (1,)), ((), ())), precision=HIGH)
    early_total, later_total, table_total = lax.psum(
        (early_part, later_part, table_part), ("replica", "shard")
    )
    return (
        layer_output,
        input_gradient,
        early_total,
        qkv_share[:, :width],
        qkv_share[:, width : 2 * width],
        qkv_share[:, 2 * width :],
        mixing_up_share[:, :width],
        table_total,
        later_total,
        mixing_up_share[:, width:],
        down_share,
    )


def solution(mesh):
    rows = P(("replica", "shard"), None)
    split = P("shard", None)
    same = P()
    return jax.shard_map(
        functools.partial(body, mesh.shape["replica"], mesh.shape["shard"]),
        mesh=mesh,
        in_specs=(rows, rows, rows, same, same, split, split, split, split, same, same, split, split),
        out_specs=(rows, rows, same, split, split, split, split, same, same, split, split),
        check_vma=False,
    )
```

```python
import functools
import math

import jax
import jax.numpy as jnp
from jax import lax
from jax.experimental import pallas as pl
from jax.experimental.pallas import tpu as pltpu
from jax.sharding import PartitionSpec as P

EPS = 1e-06
HIGH = lax.Precision.HIGHEST
HEAD_DIM = 64
PAIR = 2 * HEAD_DIM
TRIPLE = 3 * PAIR
SLAB = 128
TILE = 256
CHUNKS = 3
INNER = 4
ROWS = 256
NEG = -1e30
CURVE = math.sqrt(2 / math.pi)
CUBE = 0.044715
MIB = 1 << 20


def nt(left, right):
    return lax.dot_general(left, right, (((1,), (1,)), ((), ())), preferred_element_type=jnp.float32)


def nn(left, right):
    return lax.dot_general(left, right, (((1,), (0,)), ((), ())), preferred_element_type=jnp.float32)


def tn(left, right):
    return lax.dot_general(left, right, (((0,), (0,)), ((), ())), preferred_element_type=jnp.float32)


def low(values):
    return values.astype(jnp.bfloat16)


def wide(values):
    return values.astype(jnp.float32)


def skew_kernel(rows_ref, out_ref):
    width = rows_ref.shape[-1]
    keep = out_ref.shape[-1]
    for k in range(rows_ref.shape[0]):
        spread = jnp.broadcast_to(rows_ref[k], (SLAB, width))
        moved = pltpu.roll(spread, width - SLAB + 1, 1, stride=1, stride_axis=0)
        out_ref[k] = moved[:, :keep]


def skew(rows, length):
    count, width = rows.shape
    keep = 2 * length - SLAB
    return pl.pallas_call(
        skew_kernel,
        grid=(count // 2,),
        in_specs=[pl.BlockSpec((2, 1, width), lambda i: (i, 0, 0))],
        out_specs=pl.BlockSpec((2, SLAB, keep), lambda i: (i, 0, 0)),
        out_shape=jax.ShapeDtypeStruct((count, SLAB, keep), jnp.float32),
        compiler_params=pltpu.CompilerParams(vmem_limit_bytes=32 * MIB),
        cost_estimate=pl.CostEstimate(
            flops=count * SLAB * width, bytes_accessed=count * SLAB * keep * 4, transcendentals=0
        ),
        name="skew",
    )(rows.reshape(count, 1, width))


def shard_at(relative, meta_ref, m, k):
    return (meta_ref[2] ^ k) * INNER + (meta_ref[1] ^ m) if relative else k * INNER + m


def row_span(relative, shard, rows):
    return pl.ds(pl.multiple_of(shard * rows, 16) if relative else shard * rows, rows)


def forward_kernel(
    relative, meta_ref, normed_ref, own_ref, other_ref, ends_ref, table_ref, qkv_ref, out_ref, log_ref, weight_ref
):
    length = normed_ref.shape[0]
    tiles = length // TILE
    inner, outer, rows, _ = own_ref.shape
    mine = pl.program_id(0) == 0
    for m in range(inner):
        for k in range(outer):
            span = row_span(relative, shard_at(relative, meta_ref, m, k), rows)
            weight_ref[0, span, :] = jnp.where(mine, own_ref[m, k], other_ref[m, k])
    qkv_ref[0] = low(nn(normed_ref[...], weight_ref[0]))
    left = lax.broadcasted_iota(jnp.int32, (TILE, PAIR), 1) < HEAD_DIM

    def block(i, n):
        first = pl.multiple_of(i * TILE, TILE)
        query = qkv_ref[0, pl.ds(first, TILE), :PAIR]
        keys = qkv_ref[0, : n * TILE, PAIR : 2 * PAIR]
        values = qkv_ref[0, : n * TILE, 2 * PAIR :]
        ends = ends_ref[pl.ds(first, TILE), :]
        columns = lax.broadcasted_iota(jnp.int32, (TILE, n * TILE), 1)
        allowed = columns < ends
        outs = []
        zero = jnp.zeros_like(query)
        offset = pl.multiple_of((tiles - 1 - i) * TILE + SLAB, SLAB)
        before = pl.multiple_of(offset - SLAB, SLAB)
        for k in range(2):
            mine = jnp.where(left, query, zero) if k == 0 else jnp.where(left, zero, query)
            bias = jnp.concatenate(
                [table_ref[k, :, pl.ds(offset, n * TILE)], table_ref[k, :, pl.ds(before, n * TILE)]], axis=0
            )
            scores = jnp.where(allowed, nt(mine, keys) + bias, NEG)
            peak = jnp.max(scores, axis=1, keepdims=True)
            weights = jnp.exp(scores - peak)
            total = jnp.sum(weights, axis=1, keepdims=True)
            outs.append(nn(low(weights), values) / total)
            logs = jnp.broadcast_to(peak + jnp.log(total), (TILE, SLAB))
            log_ref[0, k : k + 1, pl.ds(first, TILE)] = logs.T[0:1, :]
        out_ref[0, pl.ds(first, TILE), :] = low(jnp.where(left, outs[0], outs[1]))

    def step(i, carry):
        count = meta_ref[3 + i]
        for n in range(1, tiles + 1):
            @pl.when(count == n)
            def _():
                block(i, n)
        return carry

    lax.fori_loop(0, tiles, step, 0)


def attend_forward(chunk, relative, meta, normed, own, other, ends, table):
    length, width = normed.shape
    pieces = pl.BlockSpec(own.shape[:2] + (None,) + own.shape[3:], lambda p, m: (0, 0, chunk, 0, 0))
    keep = table.shape[-1]
    turn = lambda p, m: (p, 0, 0)
    same = lambda p, m: (0, 0)
    return pl.pallas_call(
        functools.partial(forward_kernel, relative),
        grid_spec=pltpu.PrefetchScalarGridSpec(
            num_scalar_prefetch=1,
            grid=(2,),
            in_specs=[
                pl.BlockSpec((length, width), same),
                pieces,
                pieces,
                pl.BlockSpec((length, 1), same),
                pl.BlockSpec((2, SLAB, keep), lambda p, m: (chunk + CHUNKS * ((p + m[0]) % 2), 0, 0)),
            ],
            out_specs=[
                pl.BlockSpec((1, length, TRIPLE), turn),
                pl.BlockSpec((1, length, PAIR), turn),
                pl.BlockSpec((1, 2, length), turn),
                pl.BlockSpec((1, width, TRIPLE), turn),
            ],
        ),
        out_shape=[
            jax.ShapeDtypeStruct((2, length, TRIPLE), jnp.bfloat16),
            jax.ShapeDtypeStruct((2, length, PAIR), jnp.bfloat16),
            jax.ShapeDtypeStruct((2, 2, length), jnp.float32),
            jax.ShapeDtypeStruct((2, width, TRIPLE), jnp.bfloat16),
        ],
        compiler_params=pltpu.CompilerParams(vmem_limit_bytes=48 * MIB),
        cost_estimate=pl.CostEstimate(
            flops=16 * length * length * HEAD_DIM * 2,
            bytes_accessed=2 * length * (width + 2 * TRIPLE) + 4 * SLAB * keep * 4,
            transcendentals=4 * length * length,
        ),
        name="attend_forward",
    )(meta, normed, own, other, ends, table)


def backward_kernel(
    relative, meta_ref, qkv_ref, out_ref, grad_ref, ends_ref, log_ref, table_ref, turned_ref,
    dqkv_ref, own_ref, other_ref, diag_ref,
    qm, km, gm, dq_acc, dk_acc, dv_acc, skewed, delta, summed,
):
    length = qkv_ref.shape[1]
    tiles = length // TILE
    left = lax.broadcasted_iota(jnp.int32, (length, PAIR), 1) < HEAD_DIM
    query, keys, grads = qkv_ref[0, :, :PAIR], qkv_ref[0, :, PAIR : 2 * PAIR], grad_ref[0, 0]
    zero = jnp.zeros_like(query)
    for k in range(2):
        pick = left if k == 0 else jnp.logical_not(left)
        qm[k] = jnp.where(pick, query, zero)
        km[k] = jnp.where(pick, keys, zero)
        gm[k] = jnp.where(pick, grads, zero)
    dq_acc[...] = jnp.zeros_like(dq_acc)
    dk_acc[...] = jnp.zeros_like(dk_acc)
    dv_acc[...] = jnp.zeros_like(dv_acc)
    skewed[...] = jnp.zeros_like(skewed)
    product = wide(grads) * wide(out_ref[0])
    high = low(product)
    rest = low(product - wide(high))
    lane = lax.broadcasted_iota(jnp.int32, (16, PAIR), 1)
    row = lax.broadcasted_iota(jnp.int32, (16, PAIR), 0)
    chooser = low(jnp.where(lane // HEAD_DIM == row, 1.0, 0.0))
    delta[...] = nt(chooser, high) + nt(chooser, rest)

    def tile(t, carry):
        kb = meta_ref[4 + 2 * t]
        qb = meta_ref[5 + 2 * t]
        kf = pl.multiple_of(kb * TILE, TILE)
        qf = pl.multiple_of(qb * TILE, TILE)
        offset = pl.multiple_of((tiles - 1 + qb - kb) * TILE + SLAB, SLAB)
        before = pl.multiple_of(offset - SLAB, SLAB)
        rows = lax.broadcasted_iota(jnp.int32, (TILE, TILE), 0) + kf
        allowed = rows < ends_ref[:, pl.ds(qf, TILE)]
        q_tile = qkv_ref[0, pl.ds(qf, TILE), :PAIR]
        v_tile = qkv_ref[0, pl.ds(kf, TILE), 2 * PAIR :]
        dk_part = dk_acc[pl.ds(kf, TILE), :]
        dv_part = dv_acc[pl.ds(kf, TILE), :]
        dq_part = dq_acc[pl.ds(qf, TILE), :]
        for k in range(2):
            k_tile = km[k, pl.ds(kf, TILE), :]
            g_tile = gm[k, pl.ds(qf, TILE), :]
            bias = jnp.concatenate(
                [table_ref[k, :, pl.ds(offset, TILE)], table_ref[k, :, pl.ds(before, TILE)]], axis=0
            )
            scores = nt(k_tile, q_tile) + bias - log_ref[0, k : k + 1, pl.ds(qf, TILE)]
            probs = jnp.where(allowed, jnp.exp(scores), 0.0)
            above = nt(v_tile, g_tile) - delta[k : k + 1, pl.ds(qf, TILE)]
            grad = probs * above
            skewed[k, :, pl.ds(offset, TILE)] += grad[:SLAB]
            skewed[k, :, pl.ds(before, TILE)] += grad[SLAB:]
            probs_low = low(probs)
            grad_low = low(grad)
            dv_part = dv_part + nn(probs_low, g_tile)
            dk_part = dk_part + nn(grad_low, qm[k, pl.ds(qf, TILE), :])
            dq_part = dq_part + tn(grad_low, k_tile)
        dk_acc[pl.ds(kf, TILE), :] = dk_part
        dv_acc[pl.ds(kf, TILE), :] = dv_part
        dq_acc[pl.ds(qf, TILE), :] = dq_part
        return carry

    lax.fori_loop(0, meta_ref[3], tile, 0)
    dqkv_ref[0, :, :PAIR] = low(dq_acc[...])
    dqkv_ref[0, :, PAIR : 2 * PAIR] = low(dk_acc[...])
    dqkv_ref[0, :, 2 * PAIR :] = low(dv_acc[...])
    summed[...] = low(nn(turned_ref[...], dqkv_ref[0]))
    inner, outer, rows, _ = own_ref.shape

    def place(ref):
        for m in range(inner):
            for k in range(outer):
                ref[m, k] = summed[row_span(relative, shard_at(relative, meta_ref, m, k), rows), :]

    @pl.when(pl.program_id(0) == 0)
    def _():
        place(own_ref)

    @pl.when(pl.program_id(0) == 1)
    def _():
        place(other_ref)

    lanes = skewed.shape[-1]
    group = lax.broadcasted_iota(jnp.int32, (SLAB, lanes), 0)
    for k in range(2):
        held = skewed[k]
        shift = 1
        while shift < SLAB:
            moved = pltpu.roll(held, shift, 1)
            held = jnp.where(((SLAB - 1 - group) & shift) != 0, moved, held)
            shift *= 2
        diag_ref[0, k : k + 1, :] = jnp.sum(held, axis=0, keepdims=True)


def attend_backward(chunk, relative, shards, meta, qkv, out, grad, ends, logs, table, turned):
    length = qkv.shape[1]
    width = turned.shape[0]
    keep = table.shape[-1]
    lanes = 2 * length
    turn = lambda p, m: (p, 0, 0)
    same = lambda p, m: (0, 0)
    piece = (INNER, shards // INNER, width // shards, TRIPLE)
    pieces = pl.BlockSpec(piece, lambda p, m: (0, 0, 0, 0))
    return pl.pallas_call(
        functools.partial(backward_kernel, relative),
        grid_spec=pltpu.PrefetchScalarGridSpec(
            num_scalar_prefetch=1,
            grid=(2,),
            in_specs=[
                pl.BlockSpec((1, length, TRIPLE), turn),
                pl.BlockSpec((1, length, PAIR), turn),
                pl.BlockSpec((1, 1, length, PAIR), lambda p, m: (chunk, p, 0, 0)),
                pl.BlockSpec((1, length), same),
                pl.BlockSpec((1, 2, length), turn),
                pl.BlockSpec((2, SLAB, keep), lambda p, m: (chunk + CHUNKS * ((p + m[0]) % 2), 0, 0)),
                pl.BlockSpec((width, length), same),
            ],
            out_specs=[
                pl.BlockSpec((1, length, TRIPLE), turn),
                pieces,
                pieces,
                pl.BlockSpec((1, 2, lanes), turn),
            ],
            scratch_shapes=[
                pltpu.VMEM((2, length, PAIR), jnp.bfloat16),
                pltpu.VMEM((2, length, PAIR), jnp.bfloat16),
                pltpu.VMEM((2, length, PAIR), jnp.bfloat16),
                pltpu.VMEM((length, PAIR), jnp.float32),
                pltpu.VMEM((length, PAIR), jnp.float32),
                pltpu.VMEM((length, PAIR), jnp.float32),
                pltpu.VMEM((2, SLAB, lanes), jnp.float32),
                pltpu.VMEM((16, length), jnp.float32),
                pltpu.VMEM((width, TRIPLE), jnp.bfloat16),
            ],
        ),
        out_shape=[
            jax.ShapeDtypeStruct((2, length, TRIPLE), jnp.bfloat16),
            jax.ShapeDtypeStruct(piece, jnp.bfloat16),
            jax.ShapeDtypeStruct(piece, jnp.bfloat16),
            jax.ShapeDtypeStruct((2, 2, lanes), jnp.float32),
        ],
        compiler_params=pltpu.CompilerParams(vmem_limit_bytes=48 * MIB),
        cost_estimate=pl.CostEstimate(
            flops=48 * length * length * HEAD_DIM * 2,
            bytes_accessed=2 * length * (width + 4 * TRIPLE) + 4 * SLAB * keep * 4,
            transcendentals=4 * length * length,
        ),
        name="attend_backward",
    )(meta, qkv, out, grad, ends, logs, table, turned)


def feed_kernel(
    relative, meta_ref, x_ref, cot_ref, att0_ref, att1_ref, att2_ref, gain_ref, mix_ref, up_ref, down_ref,
    out_ref, sgrad_ref, agrad_ref, later_ref, own_ref, other_ref,
    state, scale, normed, turned, total, upstream, act, pre, mixing, attended, branch,
):
    block = pl.program_id(0)
    blocks = pl.num_programs(0)
    me = meta_ref[0]
    length, width = x_ref.shape
    half = width // 2
    shards, _, rows, _ = mix_ref.shape
    count = length // ROWS

    @pl.when(block == 0)
    def _():
        for c in range(2):
            mixing[:, c * half : (c + 1) * half] = mix_ref[:, c].reshape(width, half)
        for i, ref in enumerate((att0_ref, att1_ref, att2_ref)):
            for p in range(2):
                spot = pl.multiple_of((i + CHUNKS * ((p + me) % 2)) * PAIR, PAIR)
                attended[:, pl.ds(spot, PAIR)] = ref[p]

        def start(n, carry):
            spot = pl.ds(pl.multiple_of(n * ROWS, ROWS), ROWS)
            held = wide(x_ref[spot, :]) + nn(attended[spot, :], mixing[...])
            state[spot, :] = held
            found = lax.rsqrt(jnp.mean(held * held, axis=1, keepdims=True) + EPS)
            scale[spot, :] = jnp.broadcast_to(found, (ROWS, SLAB))
            normed[spot, :] = low(held * found * gain_ref[...])
            return carry

        lax.fori_loop(0, count, start, 0)
        turned[...] = normed[...].T
        total[...] = jnp.zeros_like(total)
        upstream[...] = jnp.zeros_like(upstream)

    up = up_ref[...].reshape(width, half)
    down = jnp.concatenate([down_ref[:, c].reshape(half, half) for c in range(2)], axis=1)

    def middle(n, carry):
        spot = pl.ds(pl.multiple_of(n * ROWS, ROWS), ROWS)
        v = nn(normed[spot, :], up)
        square = v * v
        bent = jnp.tanh(v * (CURVE + (CURVE * CUBE) * square))
        gate = 0.5 + 0.5 * bent
        slope = gate + (0.5 * v) * (1.0 - bent * bent) * (CURVE + (3 * CURVE * CUBE) * square)
        active = low(v * gate)
        act[spot, :] = active
        total[spot, :] += nn(active, down)
        changed = low(nt(cot_ref[spot, :], down) * slope)
        pre[spot, :] = changed
        upstream[spot, :] += nt(changed, up)
        return carry

    lax.fori_loop(0, count, middle, 0)
    inner, outer = own_ref.shape[:2]
    long = down_ref.shape[2]
    per = half // long
    groups = blocks // 2

    def place(shard):
        if relative:
            return (shard % inner) ^ meta_ref[1], (shard // inner) ^ meta_ref[2]
        return shard % inner, shard // inner

    def halves(values):
        left, right = values[:, :half], values[:, half:]
        first = me == 0
        return jnp.where(first, left, right), jnp.where(first, right, left)

    kept, sent = halves(low(tn(act[...], cot_ref[...])))
    for s in range(per):
        m, k = place(block * per + s)
        own_ref[m, k, :long] = kept[s * long : (s + 1) * long]
        other_ref[m, k, :long] = sent[s * long : (s + 1) * long]
    dup = low(nn(turned[...], pre[...]))
    start = pl.multiple_of(long + rows + block % groups * rows, 16 if relative else 8)

    def put(ref):
        for s in range(shards):
            m, k = place(s)
            ref[m, k, pl.ds(start, rows)] = dup[s * rows : (s + 1) * rows]

    @pl.when(block // groups == me)
    def _():
        put(own_ref)

    @pl.when(block // groups != me)
    def _():
        put(other_ref)

    @pl.when(block == blocks - 1)
    def _():
        gain = gain_ref[...]

        def finish(n, parts):
            spot = pl.ds(pl.multiple_of(n * ROWS, ROWS), ROWS)
            held = state[spot, :]
            found = scale[spot, :][:, :1]
            out_ref[spot, :] = low(held + total[spot, :])
            grads = upstream[spot, :]
            parts = parts + jnp.sum(grads * held * found, axis=0, keepdims=True)
            scaled = grads * gain
            mean = jnp.mean(scaled * held, axis=1, keepdims=True)
            result = wide(cot_ref[spot, :]) + found * (scaled - held * (found * found * mean))
            sgrad_ref[spot, :] = result
            rounded = low(result)
            branch[spot, :] = rounded
            back = low(nt(rounded, mixing[...]))
            for pair in range(width // PAIR):
                agrad_ref[pair % CHUNKS, (pair // CHUNKS + me) % 2, spot, :] = back[
                    :, pair * PAIR : (pair + 1) * PAIR
                ]
            return parts

        later_ref[...] = lax.fori_loop(0, count, finish, jnp.zeros((1, width), jnp.float32))
        kept, sent = halves(low(tn(attended[...], branch[...])))
        for s in range(shards):
            m, k = place(s)
            own_ref[m, k, long : long + rows] = kept[s * rows : (s + 1) * rows]
            other_ref[m, k, long : long + rows] = sent[s * rows : (s + 1) * rows]


def feed_forward(relative, meta, inputs, cotangent, attended, gain, gathered):
    length, width = inputs.shape
    half = width // 2
    shards, _, every, _ = gathered.shape
    rows = width // shards
    groups = (every - rows) // (2 * rows)
    long = groups * rows
    per = half // long
    blocks = 2 * groups
    outer = shards // INNER
    same = lambda b, m: (0, 0)
    full = pl.BlockSpec((length, width), same)
    pair = pl.BlockSpec((2, length, PAIR), lambda b, m: (0, 0, 0))
    return pl.pallas_call(
        functools.partial(feed_kernel, relative),
        grid_spec=pltpu.PrefetchScalarGridSpec(
            num_scalar_prefetch=1,
            grid=(blocks,),
            in_specs=[
                full, full, pair, pair, pair,
                pl.BlockSpec((1, width), same),
                pl.BlockSpec((shards, 2, rows, half), lambda b, m: (0, 0, groups, 0)),
                pl.BlockSpec((shards, 1, rows, half), lambda b, m: (0, b // groups, groups + 1 + b % groups, 0)),
                pl.BlockSpec((per, 2, long, half), lambda b, m: (b, 0, 0, 0)),
            ],
            out_specs=[
                full, full,
                pl.BlockSpec((CHUNKS, 2, length, PAIR), lambda b, m: (0, 0, 0, 0)),
                pl.BlockSpec((1, width), same),
                pl.BlockSpec((INNER, outer, every, half), lambda b, m: (0, 0, 0, 0)),
                pl.BlockSpec((INNER, outer, every, half), lambda b, m: (0, 0, 0, 0)),
            ],
            scratch_shapes=[
                pltpu.VMEM((length, width), jnp.float32),
                pltpu.VMEM((length, SLAB), jnp.float32),
                pltpu.VMEM((length, width), jnp.bfloat16),
                pltpu.VMEM((width, length), jnp.bfloat16),
                pltpu.VMEM((length, width), jnp.float32),
                pltpu.VMEM((length, width), jnp.float32),
                pltpu.VMEM((length, half), jnp.bfloat16),
                pltpu.VMEM((length, half), jnp.bfloat16),
                pltpu.VMEM((width, width), jnp.bfloat16),
                pltpu.VMEM((length, width), jnp.bfloat16),
                pltpu.VMEM((length, width), jnp.bfloat16),
            ],
        ),
        out_shape=[
            jax.ShapeDtypeStruct((length, width), jnp.bfloat16),
            jax.ShapeDtypeStruct((length, width), jnp.float32),
            jax.ShapeDtypeStruct((CHUNKS, 2, length, PAIR), jnp.bfloat16),
            jax.ShapeDtypeStruct((1, width), jnp.float32),
            jax.ShapeDtypeStruct((INNER, outer, every, half), jnp.bfloat16),
            jax.ShapeDtypeStruct((INNER, outer, every, half), jnp.bfloat16),
        ],
        compiler_params=pltpu.CompilerParams(vmem_limit_bytes=60 * MIB),
        cost_estimate=pl.CostEstimate(
            flops=12 * length * width * half * blocks + 6 * length * width * width,
            bytes_accessed=14 * length * width + 8 * width * half * blocks,
            transcendentals=length * half * blocks,
        ),
        name="feed_forward",
    )(meta, inputs, cotangent, *attended, gain.reshape(1, width), gathered, gathered, gathered)


def last_kernel(x_ref, scale_ref, gain_ref, sgrad_ref, *refs):
    grads, weights = refs[:CHUNKS], refs[CHUNKS : 2 * CHUNKS]
    out_ref, early_ref = refs[2 * CHUNKS :]
    x = wide(x_ref[...])
    found = scale_ref[...]
    upstream = jnp.zeros(x.shape, jnp.float32)
    for i in range(CHUNKS):
        upstream = upstream + nt(grads[i][0], weights[i][0]) + nt(grads[i][1], weights[i][1])
    part = jnp.sum(upstream * x * found, axis=0, keepdims=True)
    scaled = upstream * gain_ref[...]
    mean = jnp.mean(scaled * x, axis=1, keepdims=True)
    out_ref[...] = low(sgrad_ref[...] + found * (scaled - x * (found * found * mean)))

    @pl.when(pl.program_id(0) == 0)
    def _():
        early_ref[...] = part

    @pl.when(pl.program_id(0) > 0)
    def _():
        early_ref[...] += part


def last(inputs, scale, gain, state_grad, grads, weights):
    length, width = inputs.shape
    step = lambda i: (i, 0)
    same = lambda i: (0, 0)
    return pl.pallas_call(
        last_kernel,
        grid=(length // ROWS,),
        in_specs=[
            pl.BlockSpec((ROWS, width), step),
            pl.BlockSpec((ROWS, 1), step),
            pl.BlockSpec((1, width), same),
            pl.BlockSpec((ROWS, width), step),
        ]
        + [pl.BlockSpec((2, ROWS, TRIPLE), lambda i: (0, i, 0))] * CHUNKS
        + [pl.BlockSpec((2, width, TRIPLE), lambda i: (0, 0, 0))] * CHUNKS,
        out_specs=[pl.BlockSpec((ROWS, width), step), pl.BlockSpec((1, width), same)],
        out_shape=[
            jax.ShapeDtypeStruct((length, width), jnp.bfloat16),
            jax.ShapeDtypeStruct((1, width), jnp.float32),
        ],
        compiler_params=pltpu.CompilerParams(vmem_limit_bytes=48 * MIB),
        cost_estimate=pl.CostEstimate(
            flops=6 * length * width * width,
            bytes_accessed=14 * length * width + 6 * width * width,
            transcendentals=0,
        ),
        name="last",
    )(inputs, scale, gain.reshape(1, width), state_grad, *grads, *weights)


def swap(values):
    return lax.ppermute(values, "replica", [(0, 1), (1, 0)])


def shift(values, shards, distance):
    return lax.ppermute(values, "shard", [(i, i ^ distance) for i in range(shards)])


def tie(values, *before):
    return lax.optimization_barrier((values,) + before)[0]


def gather_relative(own, shards, *before):
    line = jnp.stack([own] + [shift(own, shards, k * INNER) for k in range(1, shards // INNER)])
    came = [shift(line, shards, m) for m in range(1, INNER)]
    return jnp.stack([line] + [tie(c, *before) for c in came])


def cross(own, came):
    return [low(wide(own[m]) + wide(came[m])) for m in range(INNER)]


def plane(places, shards):
    return [places[0]] + [shift(places[m], shards, m) for m in range(1, INNER)]


def column(line, shards):
    return [line[0]] + [shift(line[k], shards, k * INNER) for k in range(1, shards // INNER)]


def total_of(parts):
    total = wide(parts[0])
    for part in parts[1:]:
        total = total + wide(part)
    return total


def natural_halves(own):
    other = swap(own)
    first = lax.axis_index("replica") == 0
    return jnp.where(first, own, other), jnp.where(first, other, own)


def scatter_halves(own, other):
    halves = []
    for part in (own, other):
        whole = jnp.swapaxes(part, 0, 1).reshape((-1,) + part.shape[2:])
        halves.append(wide(lax.psum_scatter(whole, "shard", scatter_dimension=0, tiled=True))[0])
    return lax.psum(tuple(halves), "replica")


def body(
    copies,
    shards,
    inputs,
    cotangent,
    block_ids,
    buckets,
    early_gain,
    query_weight,
    key_weight,
    value_weight,
    mixing_weight,
    relative_table,
    later_gain,
    up_weight,
    down_weight,
):
    length, width = inputs.shape
    half = width // 2
    bucket_count, heads = relative_table.shape
    hidden = up_weight.shape[1]
    offsets = buckets.shape[0]
    relative = copies == 2 and width // shards % 16 == 0 and shards & (shards - 1) == 0
    me = lax.axis_index("replica") if relative else jnp.int32(0)
    spot = lax.axis_index("shard") if relative else jnp.int32(0)

    def parts_of(h):
        column = lambda w, c: lax.dynamic_slice_in_dim(w, c, half, 1)
        groups = up_weight.shape[1] // width
        return jnp.concatenate(
            [column(down_weight, h * half), column(mixing_weight, h * half)]
            + [column(up_weight, (h * groups + j) * half) for j in range(groups)],
            axis=0,
        )

    def triples_of(h):
        weights = (query_weight, key_weight, value_weight)
        starts = [(chunk + CHUNKS * h) * PAIR for chunk in range(CHUNKS)]
        return jnp.stack(
            [
                jnp.concatenate([lax.dynamic_slice_in_dim(w, at, PAIR, 1) for w in weights], axis=1)
                for at in starts
            ]
        )

    outer = shards // INNER
    if relative:
        gathered = lax.all_gather(parts_of(me), ("shard", "replica"), axis=0, tiled=True)
    else:
        gathered = lax.all_gather(jnp.stack([parts_of(0), parts_of(1)]), "shard", axis=0, tiled=True)
    gathered = gathered.reshape(shards, 2, -1, half)

    ids = block_ids.reshape(length)
    ends = jnp.sum((ids[None, :] <= ids[:, None]).astype(jnp.int32), axis=1)
    tiles = length // TILE
    final = ends.reshape(tiles, TILE)[:, TILE - 1]
    counts = (final + TILE - 1) // TILE
    key_block = jnp.repeat(jnp.arange(tiles, dtype=jnp.int32), tiles)
    query_block = jnp.tile(jnp.arange(tiles, dtype=jnp.int32), tiles)
    active = (key_block.reshape(tiles, tiles) * TILE < final[None, :]).reshape(-1)
    slot = jnp.arange(tiles * tiles, dtype=jnp.int32)
    place = jnp.sum((slot[None, :] < slot[:, None]) & active[None, :], axis=1, dtype=jnp.int32)
    hit = ((place[None, :] == slot[:, None]) & active[None, :]).astype(jnp.int32)
    listed = jnp.stack(
        [jnp.sum(hit * key_block[None, :], axis=1), jnp.sum(hit * query_block[None, :], axis=1)], axis=1
    ).reshape(-1)
    place_of = jnp.stack([me, spot % INNER, spot // INNER])
    forward_meta = jnp.concatenate([place_of, counts]).astype(jnp.int32)
    backward_meta = jnp.concatenate(
        [place_of, jnp.sum(active.astype(jnp.int32))[None], listed]
    ).astype(jnp.int32)

    onehot = (buckets[:, None] == jnp.arange(bucket_count, dtype=jnp.int32)[None, :]).astype(jnp.float32)
    mirrored = (buckets[::-1][:, None] == jnp.arange(bucket_count, dtype=jnp.int32)[None, :]).astype(jnp.float32)
    spare = ((0, 0), (0, 2 * length - offsets))
    forward_table, backward_table = [
        skew(jnp.pad(jnp.dot(hot, relative_table, precision=HIGH).T, spare), length) for hot in (onehot, mirrored)
    ]

    def natural(values):
        every = lax.all_gather(values, "shard", axis=0)
        return jnp.swapaxes(every.reshape((outer, INNER) + values.shape), 0, 1)

    if relative:
        own = gather_relative(triples_of(me), shards, forward_table, backward_table)
        other = swap(own)
    else:
        own, other = natural(triples_of(0)), natural(triples_of(1))

    values = wide(inputs)
    early_scale = lax.rsqrt(jnp.mean(values * values, axis=1, keepdims=True) + EPS)
    normed = low(values * early_scale * early_gain)
    turned = normed.T

    held = [
        attend_forward(c, relative, forward_meta, normed, own, other, ends[:, None], forward_table)
        for c in range(CHUNKS)
    ]
    layer_output, state_grad, attended_grad, later_part, feed_own, feed_other = feed_forward(
        relative, forward_meta, inputs, cotangent, [h[1] for h in held], later_gain, gathered
    )

    def backward(c, grad):
        qkv, attended, logs, _ = held[c]
        return attend_backward(
            c, relative, shards, backward_meta, qkv, attended, grad, ends[None, :], logs, backward_table, turned
        )

    def finish(grads, *before):
        scale = tie(early_scale, *before)
        return last(inputs, scale, early_gain, state_grad, grads, [h[3] for h in held])

    if relative:
        feed_came = swap(feed_other)
        grad0, own0, other0, diag0 = backward(0, attended_grad)
        came0 = swap(other0)
        feed_places = cross(feed_own, tie(feed_came, diag0))
        feed_plane = [shift(feed_places[m], shards, m) for m in (1, 2)]
        grad1, own1, other1, diag1 = backward(1, tie(attended_grad, *feed_places))
        came1 = swap(other1)
        feed_plane = [tie(p, diag1) for p in feed_plane]
        places0 = cross(own0, tie(came0, diag1))
        feed_plane.append(shift(tie(feed_places[3], diag1), shards, 3))
        plane0 = plane(places0, shards)
        grad2, own2, other2, diag2 = backward(2, tie(attended_grad, *places0, *feed_plane[:2]))
        came2 = swap(other2)
        feed_line = low(total_of([feed_places[0]] + [tie(p, diag2) for p in feed_plane]))
        line0 = low(total_of([tie(p, diag2) for p in plane0]))
        early_column = column(jnp.concatenate([feed_line, line0], axis=1), shards)
        places1 = cross(own1, tie(came1, diag2))
        places2 = cross(own2, came2)
        late_places = [jnp.concatenate(p, axis=1) for p in zip(places1, places2, strict=True)]
        late_plane = plane(late_places, shards)
        input_gradient, early_part = finish([grad0, grad1, grad2], early_column[0], *late_places)
        late_column = column(low(total_of([late_plane[0]] + [tie(p, early_part) for p in late_plane[1:]])), shards)
        rows = width // shards
        early = natural_halves(total_of([tie(p, late_column[0]) for p in early_column]))
        late = natural_halves(total_of(late_column))
        share = [h[:-rows] for h in early]
        shares = [[h[-rows:] for h in early], [h[:rows] for h in late], [h[rows:] for h in late]]
    else:
        grad0, own0, other0, diag0 = backward(0, attended_grad)
        grad1, own1, other1, diag1 = backward(1, attended_grad)
        grad2, own2, other2, diag2 = backward(2, attended_grad)
        input_gradient, early_part = finish([grad0, grad1, grad2])
        share = scatter_halves(feed_own, feed_other)
        shares = [scatter_halves(a, b) for a, b in ((own0, other0), (own1, other1), (own2, other2))]
    diagonals = [diag0, diag1, diag2]

    stacked = jnp.stack(diagonals)
    stacked = jnp.where(me == 0, stacked, stacked[:, ::-1])
    stacked = jnp.swapaxes(stacked, 0, 1).reshape(heads, 2 * length)[:, :offsets]
    table_part = lax.dot_general(mirrored, stacked, (((0,), (1,)), ((), ())), precision=HIGH)
    small = jnp.concatenate([early_part.reshape(-1), later_part.reshape(-1), table_part.reshape(-1)])
    size = small.shape[0]
    small = jnp.pad(small, (0, -size % 1024)).reshape(8, -1)
    everyone = copies * shards
    small = lax.all_to_all(
        jnp.broadcast_to(small[None], (everyone,) + small.shape), ("replica", "shard"), 0, 0
    )
    small = jnp.sum(small, axis=0).reshape(-1)
    early_total, later_total = small[:width], small[width : 2 * width]
    table_total = small[2 * width : size].reshape(bucket_count, heads)

    rows = width // shards
    long = hidden // shards
    groups = hidden // width
    down_share = jnp.concatenate([share[0][:long], share[1][:long]], axis=1)
    mixing_share = jnp.concatenate([share[0][long : long + rows], share[1][long : long + rows]], axis=1)
    up_share = jnp.concatenate(
        [share[h][long + rows * (1 + j) : long + rows * (2 + j)] for h in range(2) for j in range(groups)], axis=1
    )
    triples = [
        jnp.concatenate(
            [shares[c][h][:, n * PAIR : (n + 1) * PAIR] for h in range(2) for c in range(CHUNKS)], axis=1
        )
        for n in range(3)
    ]
    return (
        layer_output,
        input_gradient,
        early_total,
        triples[0],
        triples[1],
        triples[2],
        mixing_share,
        table_total,
        later_total,
        up_share,
        down_share,
    )


def solution(mesh):
    rows = P(("replica", "shard"), None)
    split = P("shard", None)
    same = P()
    return jax.shard_map(
        functools.partial(body, mesh.shape["replica"], mesh.shape["shard"]),
        mesh=mesh,
        in_specs=(rows, rows, rows, same, same, split, split, split, split, same, same, split, split),
        out_specs=(rows, rows, same, split, split, split, split, same, same, split, split),
        check_vma=False,
    )
```

```python
import functools
import math

import jax
import jax.numpy as jnp
from jax import lax
from jax.experimental import pallas as pl
from jax.experimental.pallas import tpu as pltpu
from jax.sharding import PartitionSpec as P

EPS = 1e-06
HIGH = lax.Precision.HIGHEST
HEAD_DIM = 64
PAIR = 2 * HEAD_DIM
TRIPLE = 3 * PAIR
SLAB = 128
TILE = 256
CHUNKS = 3
INNER = 4
ROWS = 512
NEG = -1e30
CURVE = math.sqrt(2 / math.pi)
CUBE = 0.044715
MIB = 1 << 20


def nt(left, right):
    return lax.dot_general(left, right, (((1,), (1,)), ((), ())), preferred_element_type=jnp.float32)


def nn(left, right):
    return lax.dot_general(left, right, (((1,), (0,)), ((), ())), preferred_element_type=jnp.float32)


def tn(left, right):
    return lax.dot_general(left, right, (((0,), (0,)), ((), ())), preferred_element_type=jnp.float32)


def low(values):
    return values.astype(jnp.bfloat16)


def wide(values):
    return values.astype(jnp.float32)


def skew_kernel(rows_ref, out_ref):
    width = rows_ref.shape[-1]
    keep = out_ref.shape[-1]
    for k in range(rows_ref.shape[0]):
        spread = jnp.broadcast_to(rows_ref[k], (SLAB, width))
        moved = pltpu.roll(spread, width - SLAB + 1, 1, stride=1, stride_axis=0)
        out_ref[k] = moved[:, :keep]


def skew(rows, length):
    count, width = rows.shape
    keep = 2 * length - SLAB
    return pl.pallas_call(
        skew_kernel,
        grid=(count // 2,),
        in_specs=[pl.BlockSpec((2, 1, width), lambda i: (i, 0, 0))],
        out_specs=pl.BlockSpec((2, SLAB, keep), lambda i: (i, 0, 0)),
        out_shape=jax.ShapeDtypeStruct((count, SLAB, keep), jnp.float32),
        compiler_params=pltpu.CompilerParams(vmem_limit_bytes=32 * MIB),
        cost_estimate=pl.CostEstimate(
            flops=count * SLAB * width, bytes_accessed=count * SLAB * keep * 4, transcendentals=0
        ),
        name="skew",
    )(rows.reshape(count, 1, width))


def shard_at(relative, meta_ref, m, k):
    return (meta_ref[2] ^ k) * INNER + (meta_ref[1] ^ m) if relative else k * INNER + m


def row_span(relative, shard, rows):
    return pl.ds(pl.multiple_of(shard * rows, 16) if relative else shard * rows, rows)


def forward_kernel(
    relative, meta_ref, normed_ref, own_ref, other_ref, ends_ref, table_ref, qkv_ref, out_ref, log_ref, weight_ref
):
    length = normed_ref.shape[0]
    tiles = length // TILE
    inner, outer, rows, _ = own_ref.shape
    mine = pl.program_id(0) == 0
    for m in range(inner):
        for k in range(outer):
            span = row_span(relative, shard_at(relative, meta_ref, m, k), rows)
            weight_ref[0, span, :] = jnp.where(mine, own_ref[m, k], other_ref[m, k])
    qkv_ref[0] = low(nn(normed_ref[...], weight_ref[0]))
    left = lax.broadcasted_iota(jnp.int32, (TILE, PAIR), 1) < HEAD_DIM

    def block(i, n):
        first = pl.multiple_of(i * TILE, TILE)
        query = qkv_ref[0, pl.ds(first, TILE), :PAIR]
        keys = qkv_ref[0, : n * TILE, PAIR : 2 * PAIR]
        values = qkv_ref[0, : n * TILE, 2 * PAIR :]
        ends = ends_ref[pl.ds(first, TILE), :]
        columns = lax.broadcasted_iota(jnp.int32, (TILE, n * TILE), 1)
        allowed = columns < ends
        outs = []
        zero = jnp.zeros_like(query)
        offset = pl.multiple_of((tiles - 1 - i) * TILE + SLAB, SLAB)
        before = pl.multiple_of(offset - SLAB, SLAB)
        for k in range(2):
            mine = jnp.where(left, query, zero) if k == 0 else jnp.where(left, zero, query)
            bias = jnp.concatenate(
                [table_ref[k, :, pl.ds(offset, n * TILE)], table_ref[k, :, pl.ds(before, n * TILE)]], axis=0
            )
            scores = jnp.where(allowed, nt(mine, keys) + bias, NEG)
            peak = jnp.max(scores, axis=1, keepdims=True)
            weights = jnp.exp(scores - peak)
            total = jnp.sum(weights, axis=1, keepdims=True)
            outs.append(nn(low(weights), values) / total)
            logs = jnp.broadcast_to(peak + jnp.log(total), (TILE, SLAB))
            log_ref[0, k : k + 1, pl.ds(first, TILE)] = logs.T[0:1, :]
        out_ref[0, pl.ds(first, TILE), :] = low(jnp.where(left, outs[0], outs[1]))

    def step(i, carry):
        count = meta_ref[3 + i]
        for n in range(1, tiles + 1):
            @pl.when(count == n)
            def _():
                block(i, n)
        return carry

    lax.fori_loop(0, tiles, step, 0)


def attend_forward(chunk, relative, meta, normed, own, other, ends, table):
    length, width = normed.shape
    pieces = pl.BlockSpec(own.shape[:2] + (None,) + own.shape[3:], lambda p, m: (0, 0, chunk, 0, 0))
    keep = table.shape[-1]
    turn = lambda p, m: (p, 0, 0)
    same = lambda p, m: (0, 0)
    return pl.pallas_call(
        functools.partial(forward_kernel, relative),
        grid_spec=pltpu.PrefetchScalarGridSpec(
            num_scalar_prefetch=1,
            grid=(2,),
            in_specs=[
                pl.BlockSpec((length, width), same),
                pieces,
                pieces,
                pl.BlockSpec((length, 1), same),
                pl.BlockSpec((2, SLAB, keep), lambda p, m: (chunk + CHUNKS * ((p + m[0]) % 2), 0, 0)),
            ],
            out_specs=[
                pl.BlockSpec((1, length, TRIPLE), turn),
                pl.BlockSpec((1, length, PAIR), turn),
                pl.BlockSpec((1, 2, length), turn),
                pl.BlockSpec((1, width, TRIPLE), turn),
            ],
        ),
        out_shape=[
            jax.ShapeDtypeStruct((2, length, TRIPLE), jnp.bfloat16),
            jax.ShapeDtypeStruct((2, length, PAIR), jnp.bfloat16),
            jax.ShapeDtypeStruct((2, 2, length), jnp.float32),
            jax.ShapeDtypeStruct((2, width, TRIPLE), jnp.bfloat16),
        ],
        compiler_params=pltpu.CompilerParams(vmem_limit_bytes=48 * MIB),
        cost_estimate=pl.CostEstimate(
            flops=16 * length * length * HEAD_DIM * 2,
            bytes_accessed=2 * length * (width + 2 * TRIPLE) + 4 * SLAB * keep * 4,
            transcendentals=4 * length * length,
        ),
        name="attend_forward",
    )(meta, normed, own, other, ends, table)


def backward_kernel(
    relative, meta_ref, qkv_ref, out_ref, grad_ref, ends_ref, log_ref, table_ref, turned_ref,
    dqkv_ref, own_ref, other_ref, diag_ref,
    qm, gm, kt, dq_acc, skewed, delta, summed,
):
    length = qkv_ref.shape[1]
    tiles = length // TILE
    left = lax.broadcasted_iota(jnp.int32, (length, PAIR), 1) < HEAD_DIM
    query, grads = qkv_ref[0, :, :PAIR], grad_ref[0, 0]
    zero = jnp.zeros_like(query)
    for k in range(2):
        pick = left if k == 0 else jnp.logical_not(left)
        qm[k] = jnp.where(pick, query, zero)
        gm[k] = jnp.where(pick, grads, zero)
    kt[...] = qkv_ref[0, :, PAIR : 2 * PAIR].T
    dq_acc[...] = jnp.zeros_like(dq_acc)
    skewed[...] = jnp.zeros_like(skewed)
    product = wide(grads) * wide(out_ref[0])
    high = low(product)
    rest = low(product - wide(high))
    lane = lax.broadcasted_iota(jnp.int32, (16, PAIR), 1)
    row = lax.broadcasted_iota(jnp.int32, (16, PAIR), 0)
    chooser = low(jnp.where(lane // HEAD_DIM == row, 1.0, 0.0))
    delta[...] = nt(chooser, high) + nt(chooser, rest)

    def block(kb, n):
        kf = pl.multiple_of(kb * TILE, TILE)
        qf = length - n * TILE
        span = n * TILE
        offset = pl.multiple_of((2 * tiles - 1 - n - kb) * TILE + SLAB, SLAB)
        before = pl.multiple_of(offset - SLAB, SLAB)
        rows = lax.broadcasted_iota(jnp.int32, (TILE, span), 0) + kf
        allowed = rows < ends_ref[:, qf:]
        k_tile = qkv_ref[0, pl.ds(kf, TILE), PAIR : 2 * PAIR]
        v_tile = qkv_ref[0, pl.ds(kf, TILE), 2 * PAIR :]
        dk = jnp.zeros((TILE, PAIR), jnp.float32)
        dv = jnp.zeros((TILE, PAIR), jnp.float32)
        for k in range(2):
            q_part = qm[k, qf:, :]
            g_part = gm[k, qf:, :]
            bias = jnp.concatenate(
                [table_ref[k, :, pl.ds(offset, span)], table_ref[k, :, pl.ds(before, span)]], axis=0
            )
            scores = nt(k_tile, q_part) + bias - log_ref[0, k : k + 1, qf:]
            probs = jnp.where(allowed, jnp.exp(scores), 0.0)
            above = nt(v_tile, g_part) - delta[k : k + 1, qf:]
            grad = probs * above
            skewed[k, :, pl.ds(offset, span)] += grad[:SLAB]
            skewed[k, :, pl.ds(before, span)] += grad[SLAB:]
            grad_low = low(grad)
            dv = dv + nn(low(probs), g_part)
            dk = dk + nn(grad_low, q_part)
            head = slice(k * HEAD_DIM, (k + 1) * HEAD_DIM)
            dq_acc[head, qf:] += nn(kt[head, pl.ds(kf, TILE)], grad_low)
        dqkv_ref[0, pl.ds(kf, TILE), PAIR : 2 * PAIR] = low(dk)
        dqkv_ref[0, pl.ds(kf, TILE), 2 * PAIR :] = low(dv)

    def step(kb, carry):
        count = meta_ref[3 + tiles + kb]
        for n in range(1, tiles + 1):
            @pl.when(count == n)
            def _():
                block(kb, n)
        return carry

    lax.fori_loop(0, tiles, step, 0)
    dqkv_ref[0, :, :PAIR] = low(dq_acc[...].T)
    summed[...] = low(nn(turned_ref[...], dqkv_ref[0]))
    inner, outer, rows, _ = own_ref.shape

    def place(ref):
        for m in range(inner):
            for k in range(outer):
                ref[m, k] = summed[row_span(relative, shard_at(relative, meta_ref, m, k), rows), :]

    @pl.when(pl.program_id(0) == 0)
    def _():
        place(own_ref)

    @pl.when(pl.program_id(0) == 1)
    def _():
        place(other_ref)

    group = lax.broadcasted_iota(jnp.int32, (8, skewed.shape[-1]), 0)
    for k in range(2):
        held = skewed[k, SLAB - 8 :, :]
        for a in range(SLAB // 8 - 1):
            held = held + pltpu.roll(skewed[k, a * 8 : (a + 1) * 8, :], SLAB - 8 * (a + 1), 1)
        for bit in (1, 2, 4):
            held = jnp.where(((7 - group) & bit) != 0, pltpu.roll(held, bit, 1), held)
        diag_ref[0, k : k + 1, :] = jnp.sum(held, axis=0, keepdims=True)


def attend_backward(chunk, relative, shards, meta, qkv, out, grad, ends, logs, table, turned):
    length = qkv.shape[1]
    width = turned.shape[0]
    keep = table.shape[-1]
    lanes = 2 * length
    turn = lambda p, m: (p, 0, 0)
    same = lambda p, m: (0, 0)
    piece = (INNER, shards // INNER, width // shards, TRIPLE)
    pieces = pl.BlockSpec(piece, lambda p, m: (0, 0, 0, 0))
    return pl.pallas_call(
        functools.partial(backward_kernel, relative),
        grid_spec=pltpu.PrefetchScalarGridSpec(
            num_scalar_prefetch=1,
            grid=(2,),
            in_specs=[
                pl.BlockSpec((1, length, TRIPLE), turn),
                pl.BlockSpec((1, length, PAIR), turn),
                pl.BlockSpec((1, 1, length, PAIR), lambda p, m: (chunk, p, 0, 0)),
                pl.BlockSpec((1, length), same),
                pl.BlockSpec((1, 2, length), turn),
                pl.BlockSpec((2, SLAB, keep), lambda p, m: (chunk + CHUNKS * ((p + m[0]) % 2), 0, 0)),
                pl.BlockSpec((width, length), same),
            ],
            out_specs=[
                pl.BlockSpec((1, length, TRIPLE), turn),
                pieces,
                pieces,
                pl.BlockSpec((1, 2, lanes), turn),
            ],
            scratch_shapes=[
                pltpu.VMEM((2, length, PAIR), jnp.bfloat16),
                pltpu.VMEM((2, length, PAIR), jnp.bfloat16),
                pltpu.VMEM((PAIR, length), jnp.bfloat16),
                pltpu.VMEM((PAIR, length), jnp.float32),
                pltpu.VMEM((2, SLAB, lanes), jnp.float32),
                pltpu.VMEM((16, length), jnp.float32),
                pltpu.VMEM((width, TRIPLE), jnp.bfloat16),
            ],
        ),
        out_shape=[
            jax.ShapeDtypeStruct((2, length, TRIPLE), jnp.bfloat16),
            jax.ShapeDtypeStruct(piece, jnp.bfloat16),
            jax.ShapeDtypeStruct(piece, jnp.bfloat16),
            jax.ShapeDtypeStruct((2, 2, lanes), jnp.float32),
        ],
        compiler_params=pltpu.CompilerParams(vmem_limit_bytes=48 * MIB),
        cost_estimate=pl.CostEstimate(
            flops=48 * length * length * HEAD_DIM * 2,
            bytes_accessed=2 * length * (width + 4 * TRIPLE) + 4 * SLAB * keep * 4,
            transcendentals=4 * length * length,
        ),
        name="attend_backward",
    )(meta, qkv, out, grad, ends, logs, table, turned)


def feed_kernel(
    relative, meta_ref, x_ref, cot_ref, att0_ref, att1_ref, att2_ref, gain_ref, mix_ref, up0_ref, up1_ref, down_ref,
    out_ref, sgrad_ref, agrad_ref, later_ref, own_ref, other_ref,
    state, scale, normed, turned, total, upstream, act, pre, mixing, attended, branch, up, down,
):
    block = pl.program_id(0)
    blocks = pl.num_programs(0)
    me = meta_ref[0]
    length, width = x_ref.shape
    half = width // 2
    shards, _, rows, _ = mix_ref.shape
    count = length // ROWS

    @pl.when(block == 0)
    def _():
        for c in range(2):
            mixing[:, c * half : (c + 1) * half] = mix_ref[:, c].reshape(width, half)
        for i, ref in enumerate((att0_ref, att1_ref, att2_ref)):
            for p in range(2):
                spot = pl.multiple_of((i + CHUNKS * ((p + me) % 2)) * PAIR, PAIR)
                attended[:, pl.ds(spot, PAIR)] = ref[p]

        def start(n, carry):
            spot = pl.ds(pl.multiple_of(n * ROWS, ROWS), ROWS)
            held = wide(x_ref[spot, :]) + nn(attended[spot, :], mixing[...])
            state[spot, :] = held
            found = lax.rsqrt(jnp.mean(held * held, axis=1, keepdims=True) + EPS)
            scale[spot, :] = jnp.broadcast_to(found, (ROWS, SLAB))
            normed[spot, :] = low(held * found * gain_ref[...])
            return carry

        lax.fori_loop(0, count, start, 0)
        turned[...] = normed[...].T
        total[...] = jnp.zeros_like(total)
        upstream[...] = jnp.zeros_like(upstream)

    for c, ref in enumerate((up0_ref, up1_ref)):
        up[:, c * half : (c + 1) * half] = ref[...].reshape(width, half)
        down[:, c * half : (c + 1) * half] = down_ref[:, c].reshape(width, half)

    def middle(n, carry):
        spot = pl.ds(n * ROWS, ROWS)
        v = nn(normed[spot, :], up[...])
        square = v * v
        bent = jnp.tanh(v * (CURVE + (CURVE * CUBE) * square))
        gate = 0.5 + 0.5 * bent
        slope = gate + (0.5 * v) * (1.0 - bent * bent) * (CURVE + (3 * CURVE * CUBE) * square)
        active = low(v * gate)
        act[spot, :] = active
        total[spot, :] += nn(active, down[...])
        changed = low(nt(cot_ref[spot, :], down[...]) * slope)
        pre[spot, :] = changed
        upstream[spot, :] += nt(changed, up[...])
        return carry

    for n in range(count):
        middle(n, 0)
    inner, outer = own_ref.shape[:2]
    long = down_ref.shape[2]
    per = width // long
    steps = blocks // 2

    def place(shard):
        if relative:
            return (shard % inner) ^ meta_ref[1], (shard // inner) ^ meta_ref[2]
        return shard % inner, shard // inner

    def halves(values):
        left, right = values[:, :half], values[:, half:]
        first = me == 0
        return jnp.where(first, left, right), jnp.where(first, right, left)

    kept, sent = halves(low(tn(act[...], cot_ref[...])))
    for s in range(per):
        m, k = place(block * per + s)
        own_ref[m, k, :long] = kept[s * long : (s + 1) * long]
        other_ref[m, k, :long] = sent[s * long : (s + 1) * long]
    dup = low(nn(turned[...], pre[...]))

    def put(ref):
        for c in range(2):
            start = pl.multiple_of(long + rows + (block % steps * 2 + c) * rows, 16 if relative else 8)
            for s in range(shards):
                m, k = place(s)
                ref[m, k, pl.ds(start, rows)] = dup[s * rows : (s + 1) * rows, c * half : (c + 1) * half]

    @pl.when(block // steps == me)
    def _():
        put(own_ref)

    @pl.when(block // steps != me)
    def _():
        put(other_ref)

    @pl.when(block == blocks - 1)
    def _():
        gain = gain_ref[...]

        def finish(n, parts):
            spot = pl.ds(pl.multiple_of(n * ROWS, ROWS), ROWS)
            held = state[spot, :]
            found = scale[spot, :][:, :1]
            out_ref[spot, :] = low(held + total[spot, :])
            grads = upstream[spot, :]
            parts = parts + jnp.sum(grads * held * found, axis=0, keepdims=True)
            scaled = grads * gain
            mean = jnp.mean(scaled * held, axis=1, keepdims=True)
            result = wide(cot_ref[spot, :]) + found * (scaled - held * (found * found * mean))
            sgrad_ref[spot, :] = result
            rounded = low(result)
            branch[spot, :] = rounded
            back = low(nt(rounded, mixing[...]))
            for pair in range(width // PAIR):
                agrad_ref[pair % CHUNKS, (pair // CHUNKS + me) % 2, spot, :] = back[
                    :, pair * PAIR : (pair + 1) * PAIR
                ]
            return parts

        later_ref[...] = lax.fori_loop(0, count, finish, jnp.zeros((1, width), jnp.float32))
        kept, sent = halves(low(tn(attended[...], branch[...])))
        for s in range(shards):
            m, k = place(s)
            own_ref[m, k, long : long + rows] = kept[s * rows : (s + 1) * rows]
            other_ref[m, k, long : long + rows] = sent[s * rows : (s + 1) * rows]


def feed_forward(relative, meta, inputs, cotangent, attended, gain, gathered):
    length, width = inputs.shape
    half = width // 2
    shards, _, every, _ = gathered.shape
    rows = width // shards
    groups = (every - rows) // (2 * rows)
    long = groups * rows
    per = width // long
    steps = groups // 2
    blocks = 2 * steps
    outer = shards // INNER
    same = lambda b, m: (0, 0)
    full = pl.BlockSpec((length, width), same)
    pair = pl.BlockSpec((2, length, PAIR), lambda b, m: (0, 0, 0))
    return pl.pallas_call(
        functools.partial(feed_kernel, relative),
        grid_spec=pltpu.PrefetchScalarGridSpec(
            num_scalar_prefetch=1,
            grid=(blocks,),
            in_specs=[
                full, full, pair, pair, pair,
                pl.BlockSpec((1, width), same),
                pl.BlockSpec((shards, 2, rows, half), lambda b, m: (0, 0, groups, 0)),
                pl.BlockSpec((shards, 1, rows, half), lambda b, m: (0, b // steps, groups + 1 + 2 * (b % steps), 0)),
                pl.BlockSpec((shards, 1, rows, half), lambda b, m: (0, b // steps, groups + 2 + 2 * (b % steps), 0)),
                pl.BlockSpec((per, 2, long, half), lambda b, m: (b, 0, 0, 0)),
            ],
            out_specs=[
                full, full,
                pl.BlockSpec((CHUNKS, 2, length, PAIR), lambda b, m: (0, 0, 0, 0)),
                pl.BlockSpec((1, width), same),
                pl.BlockSpec((INNER, outer, every, half), lambda b, m: (0, 0, 0, 0)),
                pl.BlockSpec((INNER, outer, every, half), lambda b, m: (0, 0, 0, 0)),
            ],
            scratch_shapes=[
                pltpu.VMEM((length, width), jnp.float32),
                pltpu.VMEM((length, SLAB), jnp.float32),
                pltpu.VMEM((length, width), jnp.bfloat16),
                pltpu.VMEM((width, length), jnp.bfloat16),
                pltpu.VMEM((length, width), jnp.float32),
                pltpu.VMEM((length, width), jnp.float32),
                pltpu.VMEM((length, width), jnp.bfloat16),
                pltpu.VMEM((length, width), jnp.bfloat16),
                pltpu.VMEM((width, width), jnp.bfloat16),
                pltpu.VMEM((length, width), jnp.bfloat16),
                pltpu.VMEM((length, width), jnp.bfloat16),
                pltpu.VMEM((width, width), jnp.bfloat16),
                pltpu.VMEM((width, width), jnp.bfloat16),
            ],
        ),
        out_shape=[
            jax.ShapeDtypeStruct((length, width), jnp.bfloat16),
            jax.ShapeDtypeStruct((length, width), jnp.float32),
            jax.ShapeDtypeStruct((CHUNKS, 2, length, PAIR), jnp.bfloat16),
            jax.ShapeDtypeStruct((1, width), jnp.float32),
            jax.ShapeDtypeStruct((INNER, outer, every, half), jnp.bfloat16),
            jax.ShapeDtypeStruct((INNER, outer, every, half), jnp.bfloat16),
        ],
        compiler_params=pltpu.CompilerParams(vmem_limit_bytes=60 * MIB),
        cost_estimate=pl.CostEstimate(
            flops=12 * length * width * width * blocks + 6 * length * width * width,
            bytes_accessed=14 * length * width + 8 * width * width * blocks,
            transcendentals=length * width * blocks,
        ),
        name="feed_forward",
    )(meta, inputs, cotangent, *attended, gain.reshape(1, width), *[gathered] * 4)


def last_kernel(x_ref, scale_ref, gain_ref, sgrad_ref, *refs):
    grads, weights = refs[:CHUNKS], refs[CHUNKS : 2 * CHUNKS]
    out_ref, early_ref = refs[2 * CHUNKS :]
    x = wide(x_ref[...])
    found = scale_ref[...]
    upstream = jnp.zeros(x.shape, jnp.float32)
    for i in range(CHUNKS):
        upstream = upstream + nt(grads[i][0], weights[i][0]) + nt(grads[i][1], weights[i][1])
    part = jnp.sum(upstream * x * found, axis=0, keepdims=True)
    scaled = upstream * gain_ref[...]
    mean = jnp.mean(scaled * x, axis=1, keepdims=True)
    out_ref[...] = low(sgrad_ref[...] + found * (scaled - x * (found * found * mean)))

    @pl.when(pl.program_id(0) == 0)
    def _():
        early_ref[...] = part

    @pl.when(pl.program_id(0) > 0)
    def _():
        early_ref[...] += part


def last(inputs, scale, gain, state_grad, grads, weights):
    length, width = inputs.shape
    step = lambda i: (i, 0)
    same = lambda i: (0, 0)
    return pl.pallas_call(
        last_kernel,
        grid=(length // ROWS,),
        in_specs=[
            pl.BlockSpec((ROWS, width), step),
            pl.BlockSpec((ROWS, 1), step),
            pl.BlockSpec((1, width), same),
            pl.BlockSpec((ROWS, width), step),
        ]
        + [pl.BlockSpec((2, ROWS, TRIPLE), lambda i: (0, i, 0))] * CHUNKS
        + [pl.BlockSpec((2, width, TRIPLE), lambda i: (0, 0, 0))] * CHUNKS,
        out_specs=[pl.BlockSpec((ROWS, width), step), pl.BlockSpec((1, width), same)],
        out_shape=[
            jax.ShapeDtypeStruct((length, width), jnp.bfloat16),
            jax.ShapeDtypeStruct((1, width), jnp.float32),
        ],
        compiler_params=pltpu.CompilerParams(vmem_limit_bytes=48 * MIB),
        cost_estimate=pl.CostEstimate(
            flops=6 * length * width * width,
            bytes_accessed=14 * length * width + 6 * width * width,
            transcendentals=0,
        ),
        name="last",
    )(inputs, scale, gain.reshape(1, width), state_grad, *grads, *weights)


def swap(values):
    return lax.ppermute(values, "replica", [(0, 1), (1, 0)])


def shift(values, shards, distance):
    return lax.ppermute(values, "shard", [(i, i ^ distance) for i in range(shards)])


def tie(values, *before):
    return lax.optimization_barrier((values,) + before)[0]


def gather_relative(own, shards, *before):
    line = jnp.stack([own] + [shift(own, shards, k * INNER) for k in range(1, shards // INNER)])
    came = [shift(line, shards, m) for m in range(1, INNER)]
    return jnp.stack([line] + [tie(c, *before) for c in came])


def cross(own, came):
    return [low(wide(own[m]) + wide(came[m])) for m in range(INNER)]


def plane(places, shards):
    return [places[0]] + [shift(places[m], shards, m) for m in range(1, INNER)]


def column(line, shards):
    return [line[0]] + [shift(line[k], shards, k * INNER) for k in range(1, shards // INNER)]


def total_of(parts):
    total = wide(parts[0])
    for part in parts[1:]:
        total = total + wide(part)
    return total


def natural_halves(own):
    other = swap(own)
    first = lax.axis_index("replica") == 0
    return jnp.where(first, own, other), jnp.where(first, other, own)


def scatter_halves(own, other):
    halves = []
    for part in (own, other):
        whole = jnp.swapaxes(part, 0, 1).reshape((-1,) + part.shape[2:])
        halves.append(wide(lax.psum_scatter(whole, "shard", scatter_dimension=0, tiled=True))[0])
    return lax.psum(tuple(halves), "replica")


def body(
    copies,
    shards,
    inputs,
    cotangent,
    block_ids,
    buckets,
    early_gain,
    query_weight,
    key_weight,
    value_weight,
    mixing_weight,
    relative_table,
    later_gain,
    up_weight,
    down_weight,
):
    length, width = inputs.shape
    half = width // 2
    bucket_count, heads = relative_table.shape
    hidden = up_weight.shape[1]
    offsets = buckets.shape[0]
    relative = copies == 2 and width // shards % 16 == 0 and shards & (shards - 1) == 0
    me = lax.axis_index("replica") if relative else jnp.int32(0)
    spot = lax.axis_index("shard") if relative else jnp.int32(0)

    def parts_of(h):
        column = lambda w, c: lax.dynamic_slice_in_dim(w, c, half, 1)
        groups = up_weight.shape[1] // width
        return jnp.concatenate(
            [column(down_weight, h * half), column(mixing_weight, h * half)]
            + [column(up_weight, (h * groups + j) * half) for j in range(groups)],
            axis=0,
        )

    def triples_of(h):
        weights = (query_weight, key_weight, value_weight)
        starts = [(chunk + CHUNKS * h) * PAIR for chunk in range(CHUNKS)]
        return jnp.stack(
            [
                jnp.concatenate([lax.dynamic_slice_in_dim(w, at, PAIR, 1) for w in weights], axis=1)
                for at in starts
            ]
        )

    outer = shards // INNER
    if relative:
        gathered = lax.all_gather(parts_of(me), ("shard", "replica"), axis=0, tiled=True)
    else:
        gathered = lax.all_gather(jnp.stack([parts_of(0), parts_of(1)]), "shard", axis=0, tiled=True)
    gathered = gathered.reshape(shards, 2, -1, half)

    ids = block_ids.reshape(length)
    ends = jnp.sum((ids[None, :] <= ids[:, None]).astype(jnp.int32), axis=1)
    tiles = length // TILE
    final = ends.reshape(tiles, TILE)[:, TILE - 1]
    counts = (final + TILE - 1) // TILE
    starts = jnp.arange(tiles, dtype=jnp.int32) * TILE
    uses = jnp.sum((starts[:, None] < final[None, :]).astype(jnp.int32), axis=1)
    place_of = jnp.stack([me, spot % INNER, spot // INNER])
    meta = jnp.concatenate([place_of, counts, uses]).astype(jnp.int32)

    onehot = (buckets[:, None] == jnp.arange(bucket_count, dtype=jnp.int32)[None, :]).astype(jnp.float32)
    mirrored = (buckets[::-1][:, None] == jnp.arange(bucket_count, dtype=jnp.int32)[None, :]).astype(jnp.float32)
    spare = ((0, 0), (0, 2 * length - offsets))
    forward_table, backward_table = [
        skew(jnp.pad(jnp.dot(hot, relative_table, precision=HIGH).T, spare), length) for hot in (onehot, mirrored)
    ]

    def natural(values):
        every = lax.all_gather(values, "shard", axis=0)
        return jnp.swapaxes(every.reshape((outer, INNER) + values.shape), 0, 1)

    if relative:
        own = gather_relative(triples_of(me), shards, forward_table, backward_table)
        other = swap(own)
    else:
        own, other = natural(triples_of(0)), natural(triples_of(1))

    values = wide(inputs)
    early_scale = lax.rsqrt(jnp.mean(values * values, axis=1, keepdims=True) + EPS)
    normed = low(values * early_scale * early_gain)
    turned = normed.T

    held = [
        attend_forward(c, relative, meta, normed, own, other, ends[:, None], forward_table)
        for c in range(CHUNKS)
    ]
    layer_output, state_grad, attended_grad, later_part, feed_own, feed_other = feed_forward(
        relative, meta, inputs, cotangent, [h[1] for h in held], later_gain, gathered
    )

    def backward(c, grad):
        qkv, attended, logs, _ = held[c]
        return attend_backward(
            c, relative, shards, meta, qkv, attended, grad, ends[None, :], logs, backward_table, turned
        )

    def finish(grads, *before):
        scale = tie(early_scale, *before)
        return last(inputs, scale, early_gain, state_grad, grads, [h[3] for h in held])

    if relative:
        feed_came = swap(feed_other)
        grad0, own0, other0, diag0 = backward(0, attended_grad)
        came0 = swap(other0)
        feed_places = cross(feed_own, tie(feed_came, diag0))
        feed_plane = [shift(feed_places[m], shards, m) for m in (1, 2)]
        grad1, own1, other1, diag1 = backward(1, tie(attended_grad, *feed_places))
        came1 = swap(other1)
        feed_plane = [tie(p, diag1) for p in feed_plane]
        places0 = cross(own0, tie(came0, diag1))
        feed_plane.append(shift(tie(feed_places[3], diag1), shards, 3))
        plane0 = plane(places0, shards)
        grad2, own2, other2, diag2 = backward(2, tie(attended_grad, *places0, *feed_plane[:2]))
        came2 = swap(other2)
        feed_line = low(total_of([feed_places[0]] + [tie(p, diag2) for p in feed_plane]))
        line0 = low(total_of([tie(p, diag2) for p in plane0]))
        early_column = column(jnp.concatenate([feed_line, line0], axis=1), shards)
        places1 = cross(own1, tie(came1, diag2))
        places2 = cross(own2, came2)
        late_places = [jnp.concatenate(p, axis=1) for p in zip(places1, places2, strict=True)]
        late_plane = plane(late_places, shards)
        input_gradient, early_part = finish([grad0, grad1, grad2], early_column[0], *late_places)
        late_column = column(low(total_of([late_plane[0]] + [tie(p, early_part) for p in late_plane[1:]])), shards)
        rows = width // shards
        early = natural_halves(total_of([tie(p, late_column[0]) for p in early_column]))
        late = natural_halves(total_of(late_column))
        share = [h[:-rows] for h in early]
        shares = [[h[-rows:] for h in early], [h[:rows] for h in late], [h[rows:] for h in late]]
    else:
        grad0, own0, other0, diag0 = backward(0, attended_grad)
        grad1, own1, other1, diag1 = backward(1, attended_grad)
        grad2, own2, other2, diag2 = backward(2, attended_grad)
        input_gradient, early_part = finish([grad0, grad1, grad2])
        share = scatter_halves(feed_own, feed_other)
        shares = [scatter_halves(a, b) for a, b in ((own0, other0), (own1, other1), (own2, other2))]
    diagonals = [diag0, diag1, diag2]

    stacked = jnp.stack(diagonals)
    stacked = jnp.where(me == 0, stacked, stacked[:, ::-1])
    stacked = jnp.swapaxes(stacked, 0, 1).reshape(heads, 2 * length)[:, :offsets]
    table_part = lax.dot_general(mirrored, stacked, (((0,), (1,)), ((), ())), precision=HIGH)
    small = jnp.concatenate([early_part.reshape(-1), later_part.reshape(-1), table_part.reshape(-1)])
    size = small.shape[0]
    small = jnp.pad(small, (0, -size % 1024)).reshape(8, -1)
    everyone = copies * shards
    small = lax.all_to_all(
        jnp.broadcast_to(small[None], (everyone,) + small.shape), ("replica", "shard"), 0, 0
    )
    small = jnp.sum(small, axis=0).reshape(-1)
    early_total, later_total = small[:width], small[width : 2 * width]
    table_total = small[2 * width : size].reshape(bucket_count, heads)

    rows = width // shards
    long = hidden // shards
    groups = hidden // width
    down_share = jnp.concatenate([share[0][:long], share[1][:long]], axis=1)
    mixing_share = jnp.concatenate([share[0][long : long + rows], share[1][long : long + rows]], axis=1)
    up_share = jnp.concatenate(
        [share[h][long + rows * (1 + j) : long + rows * (2 + j)] for h in range(2) for j in range(groups)], axis=1
    )
    triples = [
        jnp.concatenate(
            [shares[c][h][:, n * PAIR : (n + 1) * PAIR] for h in range(2) for c in range(CHUNKS)], axis=1
        )
        for n in range(3)
    ]
    return (
        layer_output,
        input_gradient,
        early_total,
        triples[0],
        triples[1],
        triples[2],
        mixing_share,
        table_total,
        later_total,
        up_share,
        down_share,
    )


def solution(mesh):
    rows = P(("replica", "shard"), None)
    split = P("shard", None)
    same = P()
    return jax.shard_map(
        functools.partial(body, mesh.shape["replica"], mesh.shape["shard"]),
        mesh=mesh,
        in_specs=(rows, rows, rows, same, same, split, split, split, split, same, same, split, split),
        out_specs=(rows, rows, same, split, split, split, split, same, same, split, split),
        check_vma=False,
    )
```

```python
import functools
import math

import jax
import jax.numpy as jnp
from jax import lax
from jax.experimental import pallas as pl
from jax.experimental.pallas import tpu as pltpu
from jax.sharding import PartitionSpec as P

EPS = 1e-06
HIGH = lax.Precision.HIGHEST
HEAD_DIM = 64
PAIR = 2 * HEAD_DIM
TRIPLE = 3 * PAIR
SLAB = 128
TILE = 256
CHUNKS = 3
INNER = 4
ROWS = 512
SMALL = 8
NEG = -1e30
CURVE = math.sqrt(2 / math.pi)
CUBE = 0.044715
MIB = 1 << 20


def nt(left, right):
    return lax.dot_general(left, right, (((1,), (1,)), ((), ())), preferred_element_type=jnp.float32)


def nn(left, right):
    return lax.dot_general(left, right, (((1,), (0,)), ((), ())), preferred_element_type=jnp.float32)


def tn(left, right):
    return lax.dot_general(left, right, (((0,), (0,)), ((), ())), preferred_element_type=jnp.float32)


def low(values):
    return values.astype(jnp.bfloat16)


def wide(values):
    return values.astype(jnp.float32)


def in_hbm(shape, dtype):
    return pltpu.HBM(shape, dtype)


def from_hbm(*arrays):
    return [pltpu.with_memory_space_constraint(a, pltpu.HBM) for a in arrays]


def skew_kernel(rows_ref, out_ref):
    width = rows_ref.shape[-1]
    keep = out_ref.shape[-1]
    for k in range(rows_ref.shape[0]):
        spread = jnp.broadcast_to(rows_ref[k], (SLAB, width))
        moved = pltpu.roll(spread, width - SLAB + 1, 1, stride=1, stride_axis=0)
        out_ref[k] = moved[:, :keep]


def skew(rows, length):
    count, width = rows.shape
    keep = 2 * length - SLAB
    return pl.pallas_call(
        skew_kernel,
        grid=(count // 2,),
        in_specs=[pl.BlockSpec((2, 1, width), lambda i: (i, 0, 0))],
        out_specs=pl.BlockSpec((2, SLAB, keep), lambda i: (i, 0, 0)),
        out_shape=in_hbm((count, SLAB, keep), jnp.float32),
        compiler_params=pltpu.CompilerParams(vmem_limit_bytes=32 * MIB),
        cost_estimate=pl.CostEstimate(
            flops=count * SLAB * width, bytes_accessed=count * SLAB * keep * 4, transcendentals=0
        ),
        name="skew",
    )(rows.reshape(count, 1, width))


def shard_at(relative, meta_ref, m, k):
    return (meta_ref[2] ^ k) * INNER + (meta_ref[1] ^ m) if relative else k * INNER + m


def row_span(relative, shard, rows):
    return pl.ds(pl.multiple_of(shard * rows, 16) if relative else shard * rows, rows)


def forward_kernel(
    relative, meta_ref, normed_ref, own_ref, other_ref, ends_ref, table_ref, qkv_ref, out_ref, log_ref, weight_ref
):
    length = normed_ref.shape[0]
    tiles = length // TILE
    inner, outer, rows, _ = own_ref.shape
    mine = pl.program_id(0) == 0
    for m in range(inner):
        for k in range(outer):
            span = row_span(relative, shard_at(relative, meta_ref, m, k), rows)
            weight_ref[0, span, :] = jnp.where(mine, own_ref[m, k], other_ref[m, k])
    qkv_ref[0] = low(nn(normed_ref[...], weight_ref[0]))
    left = lax.broadcasted_iota(jnp.int32, (TILE, PAIR), 1) < HEAD_DIM

    def block(i, n):
        first = pl.multiple_of(i * TILE, TILE)
        query = qkv_ref[0, pl.ds(first, TILE), :PAIR]
        keys = qkv_ref[0, : n * TILE, PAIR : 2 * PAIR]
        values = qkv_ref[0, : n * TILE, 2 * PAIR :]
        ends = ends_ref[pl.ds(first, TILE), :]
        columns = lax.broadcasted_iota(jnp.int32, (TILE, n * TILE), 1)
        allowed = columns < ends
        outs = []
        zero = jnp.zeros_like(query)
        offset = pl.multiple_of((tiles - 1 - i) * TILE + SLAB, SLAB)
        before = pl.multiple_of(offset - SLAB, SLAB)
        for k in range(2):
            mine = jnp.where(left, query, zero) if k == 0 else jnp.where(left, zero, query)
            bias = jnp.concatenate(
                [table_ref[k, :, pl.ds(offset, n * TILE)], table_ref[k, :, pl.ds(before, n * TILE)]], axis=0
            )
            scores = jnp.where(allowed, nt(mine, keys) + bias, NEG)
            peak = jnp.max(scores, axis=1, keepdims=True)
            weights = jnp.exp(scores - peak)
            total = jnp.sum(weights, axis=1, keepdims=True)
            outs.append(nn(low(weights), values) / total)
            logs = jnp.broadcast_to(peak + jnp.log(total), (TILE, SLAB))
            log_ref[0, k : k + 1, pl.ds(first, TILE)] = logs.T[0:1, :]
        out_ref[0, pl.ds(first, TILE), :] = low(jnp.where(left, outs[0], outs[1]))

    def step(i, carry):
        count = meta_ref[3 + i]
        for n in range(1, tiles + 1):
            @pl.when(count == n)
            def _():
                block(i, n)
        return carry

    lax.fori_loop(0, tiles, step, 0)


def attend_forward(chunk, relative, meta, normed, own, other, ends, table):
    length, width = normed.shape
    pieces = pl.BlockSpec(own.shape[:2] + (None,) + own.shape[3:], lambda p, m: (0, 0, chunk, 0, 0))
    keep = table.shape[-1]
    turn = lambda p, m: (p, 0, 0)
    same = lambda p, m: (0, 0)
    return pl.pallas_call(
        functools.partial(forward_kernel, relative),
        grid_spec=pltpu.PrefetchScalarGridSpec(
            num_scalar_prefetch=1,
            grid=(2,),
            in_specs=[
                pl.BlockSpec((length, width), same),
                pieces,
                pieces,
                pl.BlockSpec((length, 1), same),
                pl.BlockSpec((2, SLAB, keep), lambda p, m: (chunk + CHUNKS * ((p + m[0]) % 2), 0, 0)),
            ],
            out_specs=[
                pl.BlockSpec((1, length, TRIPLE), turn),
                pl.BlockSpec((1, length, PAIR), turn),
                pl.BlockSpec((1, 2, length), turn),
                pl.BlockSpec((1, width, TRIPLE), turn),
            ],
        ),
        out_shape=[
            in_hbm((2, length, TRIPLE), jnp.bfloat16),
            in_hbm((2, length, PAIR), jnp.bfloat16),
            in_hbm((2, 2, length), jnp.float32),
            in_hbm((2, width, TRIPLE), jnp.bfloat16),
        ],
        compiler_params=pltpu.CompilerParams(vmem_limit_bytes=48 * MIB),
        cost_estimate=pl.CostEstimate(
            flops=16 * length * length * HEAD_DIM * 2,
            bytes_accessed=2 * length * (width + 2 * TRIPLE) + 4 * SLAB * keep * 4,
            transcendentals=4 * length * length,
        ),
        name="attend_forward",
    )(meta, normed, own, other, ends, *from_hbm(table))


def backward_kernel(
    relative, side, meta_ref, qkv_ref, out_ref, grad_ref, ends_ref, log_ref, table_ref, turned_ref, matrix_ref,
    dqkv_ref, weight_ref, diag_ref, gain_ref,
    qm, gm, kt, dq_acc, skewed, delta, summed, turned, matrix, sems,
):
    fetches = [
        pltpu.make_async_copy(turned_ref, turned, sems.at[0]),
        pltpu.make_async_copy(matrix_ref.at[side], matrix, sems.at[1]),
    ]
    for fetch in fetches:
        fetch.start()
    length = qkv_ref.shape[1]
    tiles = length // TILE
    left = lax.broadcasted_iota(jnp.int32, (length, PAIR), 1) < HEAD_DIM
    query, grads = qkv_ref[0, :, :PAIR], grad_ref[0, 0]
    zero = jnp.zeros_like(query)
    for k in range(2):
        pick = left if k == 0 else jnp.logical_not(left)
        qm[k] = jnp.where(pick, query, zero)
        gm[k] = jnp.where(pick, grads, zero)
    kt[...] = qkv_ref[0, :, PAIR : 2 * PAIR].T
    dq_acc[...] = jnp.zeros_like(dq_acc)
    skewed[...] = jnp.zeros_like(skewed)
    product = wide(grads) * wide(out_ref[0])
    high = low(product)
    rest = low(product - wide(high))
    lane = lax.broadcasted_iota(jnp.int32, (16, PAIR), 1)
    row = lax.broadcasted_iota(jnp.int32, (16, PAIR), 0)
    chooser = low(jnp.where(lane // HEAD_DIM == row, 1.0, 0.0))
    delta[...] = nt(chooser, high) + nt(chooser, rest)

    def block(kb, n):
        kf = pl.multiple_of(kb * TILE, TILE)
        qf = length - n * TILE
        span = n * TILE
        offset = pl.multiple_of((2 * tiles - 1 - n - kb) * TILE + SLAB, SLAB)
        before = pl.multiple_of(offset - SLAB, SLAB)
        rows = lax.broadcasted_iota(jnp.int32, (TILE, span), 0) + kf
        allowed = rows < ends_ref[:, qf:]
        k_tile = qkv_ref[0, pl.ds(kf, TILE), PAIR : 2 * PAIR]
        v_tile = qkv_ref[0, pl.ds(kf, TILE), 2 * PAIR :]
        dk = jnp.zeros((TILE, PAIR), jnp.float32)
        dv = jnp.zeros((TILE, PAIR), jnp.float32)
        for k in range(2):
            q_part = qm[k, qf:, :]
            g_part = gm[k, qf:, :]
            bias = jnp.concatenate(
                [table_ref[k, :, pl.ds(offset, span)], table_ref[k, :, pl.ds(before, span)]], axis=0
            )
            scores = nt(k_tile, q_part) + bias - log_ref[0, k : k + 1, qf:]
            probs = jnp.where(allowed, jnp.exp(scores), 0.0)
            above = nt(v_tile, g_part) - delta[k : k + 1, qf:]
            grad = probs * above
            skewed[k, :, pl.ds(offset, span)] += grad[:SLAB]
            skewed[k, :, pl.ds(before, span)] += grad[SLAB:]
            grad_low = low(grad)
            dv = dv + nn(low(probs), g_part)
            dk = dk + nn(grad_low, q_part)
            head = slice(k * HEAD_DIM, (k + 1) * HEAD_DIM)
            dq_acc[head, qf:] += nn(kt[head, pl.ds(kf, TILE)], grad_low)
        dqkv_ref[pl.ds(kf, TILE), PAIR : 2 * PAIR] = low(dk)
        dqkv_ref[pl.ds(kf, TILE), 2 * PAIR :] = low(dv)

    def step(kb, carry):
        count = meta_ref[3 + tiles + kb]
        for n in range(1, tiles + 1):
            @pl.when(count == n)
            def _():
                block(kb, n)
        return carry

    lax.fori_loop(0, tiles, step, 0)
    dqkv_ref[:, :PAIR] = low(dq_acc[...].T)
    for fetch in fetches:
        fetch.wait()
    exact = nn(turned[...], dqkv_ref[...])
    summed[...] = low(exact)
    by_row = jnp.sum(exact * wide(matrix[...]), axis=1, keepdims=True)
    gain_ref[...] = jnp.broadcast_to(by_row, (by_row.shape[0], SLAB)).T[0:1, :]
    inner, outer, rows, _ = weight_ref.shape
    for m in range(inner):
        for k in range(outer):
            weight_ref[m, k] = summed[row_span(relative, shard_at(relative, meta_ref, m, k), rows), :]

    group = lax.broadcasted_iota(jnp.int32, (8, skewed.shape[-1]), 0)
    for k in range(2):
        held = skewed[k, SLAB - 8 :, :]
        for a in range(SLAB // 8 - 1):
            held = held + pltpu.roll(skewed[k, a * 8 : (a + 1) * 8, :], SLAB - 8 * (a + 1), 1)
        for bit in (1, 2, 4):
            held = jnp.where(((7 - group) & bit) != 0, pltpu.roll(held, bit, 1), held)
        diag_ref[k : k + 1, :] = jnp.sum(held, axis=0, keepdims=True)


def attend_backward(chunk, side, relative, shards, meta, qkv, out, grad, ends, logs, table, turned, matrices):
    length = qkv.shape[1]
    width = turned.shape[0]
    keep = table.shape[-1]
    lanes = 2 * length
    turn = lambda i, m: (side, 0, 0)
    same = lambda i, m: (0, 0)
    piece = (INNER, shards // INNER, width // shards, TRIPLE)
    return pl.pallas_call(
        functools.partial(backward_kernel, relative, side),
        grid_spec=pltpu.PrefetchScalarGridSpec(
            num_scalar_prefetch=1,
            grid=(1,),
            in_specs=[
                pl.BlockSpec((1, length, TRIPLE), turn),
                pl.BlockSpec((1, length, PAIR), turn),
                pl.BlockSpec((1, 1, length, PAIR), lambda i, m: (chunk, side, 0, 0)),
                pl.BlockSpec((1, length), same),
                pl.BlockSpec((1, 2, length), turn),
                pl.BlockSpec((2, SLAB, keep), lambda i, m: (chunk + CHUNKS * ((side + m[0]) % 2), 0, 0)),
                pl.BlockSpec(memory_space=pl.ANY),
                pl.BlockSpec(memory_space=pl.ANY),
            ],
            out_specs=[
                pl.BlockSpec((length, TRIPLE), same),
                pl.BlockSpec(piece, lambda i, m: (0, 0, 0, 0)),
                pl.BlockSpec((2, lanes), same),
                pl.BlockSpec((1, width), same),
            ],
            scratch_shapes=[
                pltpu.VMEM((2, length, PAIR), jnp.bfloat16),
                pltpu.VMEM((2, length, PAIR), jnp.bfloat16),
                pltpu.VMEM((PAIR, length), jnp.bfloat16),
                pltpu.VMEM((PAIR, length), jnp.float32),
                pltpu.VMEM((2, SLAB, lanes), jnp.float32),
                pltpu.VMEM((16, length), jnp.float32),
                pltpu.VMEM((width, TRIPLE), jnp.bfloat16),
                pltpu.VMEM((width, length), jnp.bfloat16),
                pltpu.VMEM((width, TRIPLE), jnp.bfloat16),
                pltpu.SemaphoreType.DMA((2,)),
            ],
        ),
        out_shape=[
            in_hbm((length, TRIPLE), jnp.bfloat16),
            in_hbm(piece, jnp.bfloat16),
            in_hbm((2, lanes), jnp.float32),
            in_hbm((1, width), jnp.float32),
        ],
        compiler_params=pltpu.CompilerParams(vmem_limit_bytes=40 * MIB),
        cost_estimate=pl.CostEstimate(
            flops=1, bytes_accessed=1, transcendentals=0
        ),
        name="attend_backward",
    )(meta, *from_hbm(qkv, out, grad), ends, logs, *from_hbm(table, turned, matrices))


def feed_kernel(
    meta_ref, x_ref, cot_ref, att0_ref, att1_ref, att2_ref, gain_ref, mix_ref, up0_ref, up1_ref, down_ref,
    out_ref, sgrad_ref, agrad_ref, later_ref, rest_ref, own_ref, other_ref,
    state, scale, normed, turned, total, upstream, act, pre, mixing, attended, branch, up, down,
):
    block = pl.program_id(0)
    blocks = pl.num_programs(0)
    me = meta_ref[0]
    length, width = x_ref.shape
    half = width // 2
    shards, _, rows, _ = mix_ref.shape
    count = length // ROWS

    @pl.when(block == 0)
    def _():
        for c in range(2):
            mixing[:, c * half : (c + 1) * half] = mix_ref[:, c].reshape(width, half)
        for i, ref in enumerate((att0_ref, att1_ref, att2_ref)):
            for p in range(2):
                spot = pl.multiple_of((i + CHUNKS * ((p + me) % 2)) * PAIR, PAIR)
                attended[:, pl.ds(spot, PAIR)] = ref[p]

        def start(n, carry):
            spot = pl.ds(pl.multiple_of(n * ROWS, ROWS), ROWS)
            held = wide(x_ref[spot, :]) + nn(attended[spot, :], mixing[...])
            state[spot, :] = held
            found = lax.rsqrt(jnp.mean(held * held, axis=1, keepdims=True) + EPS)
            scale[spot, :] = jnp.broadcast_to(found, (ROWS, SLAB))
            normed[spot, :] = low(held * found * gain_ref[...])
            return carry

        lax.fori_loop(0, count, start, 0)
        turned[...] = normed[...].T
        total[...] = jnp.zeros_like(total)
        upstream[...] = jnp.zeros_like(upstream)

    for c, ref in enumerate((up0_ref, up1_ref)):
        up[:, c * half : (c + 1) * half] = ref[...].reshape(width, half)
        down[:, c * half : (c + 1) * half] = down_ref[:, c].reshape(width, half)

    def middle(n, carry):
        spot = pl.ds(n * ROWS, ROWS)
        v = nn(normed[spot, :], up[...])
        square = v * v
        bent = jnp.tanh(v * (CURVE + (CURVE * CUBE) * square))
        gate = 0.5 + 0.5 * bent
        slope = gate + (0.5 * v) * (1.0 - bent * bent) * (CURVE + (3 * CURVE * CUBE) * square)
        active = low(v * gate)
        act[spot, :] = active
        total[spot, :] += nn(active, down[...])
        changed = low(nt(cot_ref[spot, :], down[...]) * slope)
        pre[spot, :] = changed
        upstream[spot, :] += nt(changed, up[...])
        return carry

    for n in range(count):
        middle(n, 0)
    long = down_ref.shape[2]
    per = width // long
    steps = blocks // 2

    def halves(values):
        left, right = values[:, :half], values[:, half:]
        first = me == 0
        return jnp.where(first, left, right), jnp.where(first, right, left)

    kept, sent = halves(low(tn(act[...], cot_ref[...])))
    for s in range(per):
        own_ref[s] = kept[s * long : (s + 1) * long]
        other_ref[s] = sent[s * long : (s + 1) * long]
    dup = low(nn(turned[...], pre[...]))
    for c in range(2):
        start = pl.multiple_of(rows + (block % steps * 2 + c) * rows, rows)
        for s in range(shards):
            rest_ref[s, block // steps, pl.ds(start, rows)] = dup[
                s * rows : (s + 1) * rows, c * half : (c + 1) * half
            ]

    @pl.when(block == blocks - 1)
    def _():
        gain = gain_ref[...]

        def finish(n, parts):
            spot = pl.ds(pl.multiple_of(n * ROWS, ROWS), ROWS)
            held = state[spot, :]
            found = scale[spot, :][:, :1]
            out_ref[spot, :] = low(held + total[spot, :])
            grads = upstream[spot, :]
            parts = parts + jnp.sum(grads * held * found, axis=0, keepdims=True)
            scaled = grads * gain
            mean = jnp.mean(scaled * held, axis=1, keepdims=True)
            result = wide(cot_ref[spot, :]) + found * (scaled - held * (found * found * mean))
            sgrad_ref[spot, :] = result
            rounded = low(result)
            branch[spot, :] = rounded
            back = low(nt(rounded, mixing[...]))
            for pair in range(width // PAIR):
                agrad_ref[pair % CHUNKS, (pair // CHUNKS + me) % 2, spot, :] = back[
                    :, pair * PAIR : (pair + 1) * PAIR
                ]
            return parts

        later_ref[...] = lax.fori_loop(0, count, finish, jnp.zeros((1, width), jnp.float32))
        dmix = low(tn(attended[...], branch[...]))
        for s in range(shards):
            for c in range(2):
                rest_ref[s, c, :rows] = dmix[s * rows : (s + 1) * rows, c * half : (c + 1) * half]


def feed_forward(meta, inputs, cotangent, attended, gain, gathered):
    length, width = inputs.shape
    half = width // 2
    shards, _, every, _ = gathered.shape
    rows = width // shards
    groups = (every - rows) // (2 * rows)
    long = groups * rows
    per = width // long
    steps = groups // 2
    blocks = 2 * steps
    same = lambda b, m: (0, 0)
    full = pl.BlockSpec((length, width), same)
    pair = pl.BlockSpec((2, length, PAIR), lambda b, m: (0, 0, 0))
    return pl.pallas_call(
        feed_kernel,
        grid_spec=pltpu.PrefetchScalarGridSpec(
            num_scalar_prefetch=1,
            grid=(blocks,),
            in_specs=[
                full, full, pair, pair, pair,
                pl.BlockSpec((1, width), same),
                pl.BlockSpec((shards, 2, rows, half), lambda b, m: (0, 0, groups, 0)),
                pl.BlockSpec((shards, 1, rows, half), lambda b, m: (0, b // steps, groups + 1 + 2 * (b % steps), 0)),
                pl.BlockSpec((shards, 1, rows, half), lambda b, m: (0, b // steps, groups + 2 + 2 * (b % steps), 0)),
                pl.BlockSpec((per, 2, long, half), lambda b, m: (b, 0, 0, 0)),
            ],
            out_specs=[
                full, full,
                pl.BlockSpec((CHUNKS, 2, length, PAIR), lambda b, m: (0, 0, 0, 0)),
                pl.BlockSpec((1, width), same),
                pl.BlockSpec((shards, 2, every - long, half), lambda b, m: (0, 0, 0, 0)),
                pl.BlockSpec((per, long, half), lambda b, m: (b, 0, 0)),
                pl.BlockSpec((per, long, half), lambda b, m: (b, 0, 0)),
            ],
            scratch_shapes=[
                pltpu.VMEM((length, width), jnp.float32),
                pltpu.VMEM((length, SLAB), jnp.float32),
                pltpu.VMEM((length, width), jnp.bfloat16),
                pltpu.VMEM((width, length), jnp.bfloat16),
                pltpu.VMEM((length, width), jnp.float32),
                pltpu.VMEM((length, width), jnp.float32),
                pltpu.VMEM((length, width), jnp.bfloat16),
                pltpu.VMEM((length, width), jnp.bfloat16),
                pltpu.VMEM((width, width), jnp.bfloat16),
                pltpu.VMEM((length, width), jnp.bfloat16),
                pltpu.VMEM((length, width), jnp.bfloat16),
                pltpu.VMEM((width, width), jnp.bfloat16),
                pltpu.VMEM((width, width), jnp.bfloat16),
            ],
        ),
        out_shape=[
            in_hbm((length, width), jnp.bfloat16),
            in_hbm((length, width), jnp.float32),
            in_hbm((CHUNKS, 2, length, PAIR), jnp.bfloat16),
            in_hbm((1, width), jnp.float32),
            in_hbm((shards, 2, every - long, half), jnp.bfloat16),
            in_hbm((shards, long, half), jnp.bfloat16),
            in_hbm((shards, long, half), jnp.bfloat16),
        ],
        compiler_params=pltpu.CompilerParams(vmem_limit_bytes=60 * MIB),
        cost_estimate=pl.CostEstimate(
            flops=12 * length * width * width * blocks + 6 * length * width * width,
            bytes_accessed=14 * length * width + 8 * width * width * blocks,
            transcendentals=length * width * blocks,
        ),
        name="feed_forward",
    )(meta, inputs, cotangent, *attended, gain.reshape(1, width), *[gathered] * 4)


def last_kernel(x_ref, scale_ref, gain_ref, sgrad_ref, *refs):
    grads, weights = refs[: 2 * CHUNKS], refs[2 * CHUNKS : 3 * CHUNKS]
    out_ref = refs[3 * CHUNKS]
    x = wide(x_ref[...])
    found = scale_ref[...]
    upstream = jnp.zeros(x.shape, jnp.float32)
    for i in range(CHUNKS):
        for side in range(2):
            upstream = upstream + nt(grads[2 * i + side][...], weights[i][side])
    scaled = upstream * gain_ref[...]
    mean = jnp.mean(scaled * x, axis=1, keepdims=True)
    out_ref[...] = low(sgrad_ref[...] + found * (scaled - x * (found * found * mean)))


def last(inputs, scale, gain, state_grad, grads, weights):
    length, width = inputs.shape
    step = lambda i: (i, 0)
    same = lambda i: (0, 0)
    return pl.pallas_call(
        last_kernel,
        grid=(length // ROWS,),
        in_specs=[
            pl.BlockSpec((ROWS, width), step),
            pl.BlockSpec((ROWS, 1), step),
            pl.BlockSpec((1, width), same),
            pl.BlockSpec((ROWS, width), step),
        ]
        + [pl.BlockSpec((ROWS, TRIPLE), step)] * (2 * CHUNKS)
        + [pl.BlockSpec((2, width, TRIPLE), lambda i: (0, 0, 0))] * CHUNKS,
        out_specs=pl.BlockSpec((ROWS, width), step),
        out_shape=in_hbm((length, width), jnp.bfloat16),
        compiler_params=pltpu.CompilerParams(vmem_limit_bytes=48 * MIB),
        cost_estimate=pl.CostEstimate(
            flops=1, bytes_accessed=1, transcendentals=0
        ),
        name="last",
    )(inputs, scale, gain.reshape(1, width), state_grad, *from_hbm(*grads, *weights))


def swap(values):
    return lax.ppermute(values, "replica", [(0, 1), (1, 0)])


def shift(values, shards, distance):
    return lax.ppermute(values, "shard", [(i, i ^ distance) for i in range(shards)])


def tie(values, *before):
    return lax.optimization_barrier((values,) + before)[0]


def gather_relative(own, shards, *before):
    line = jnp.stack([own] + [shift(own, shards, k * INNER) for k in range(1, shards // INNER)])
    came = [shift(line, shards, m) for m in range(1, INNER)]
    return jnp.stack([line] + [tie(c, *before) for c in came])


def cross(own, came):
    return [low(wide(own[m]) + wide(came[m])) for m in range(INNER)]


def plane(places, shards):
    return [places[0]] + [shift(places[m], shards, m) for m in range(1, INNER)]


def column(line, shards):
    return [line[0]] + [shift(line[k], shards, k * INNER) for k in range(1, shards // INNER)]


def total_of(parts):
    total = wide(parts[0])
    for part in parts[1:]:
        total = total + wide(part)
    return total


def inner_first(places, shards):
    return jnp.swapaxes(places.reshape((shards // INNER, INNER) + places.shape[1:]), 0, 1)


def exchange(pieces, groups):
    return lax.all_to_all(pieces, "shard", 0, 0, axis_index_groups=groups)


def inner_groups(shards):
    return [[o * INNER + i for i in range(INNER)] for o in range(shards // INNER)]


def outer_groups(shards):
    return [[o * INNER + i for o in range(shards // INNER)] for i in range(INNER)]


def natural_halves(own):
    other = swap(own)
    first = lax.axis_index("replica") == 0
    return jnp.where(first, own, other), jnp.where(first, other, own)


def scatter_halves(own, other):
    halves = []
    for part in (own, other):
        whole = jnp.swapaxes(part, 0, 1).reshape((-1,) + part.shape[2:])
        halves.append(wide(lax.psum_scatter(whole, "shard", scatter_dimension=0, tiled=True))[0])
    return lax.psum(tuple(halves), "replica")


def body(
    copies,
    shards,
    inputs,
    cotangent,
    block_ids,
    buckets,
    early_gain,
    query_weight,
    key_weight,
    value_weight,
    mixing_weight,
    relative_table,
    later_gain,
    up_weight,
    down_weight,
):
    length, width = inputs.shape
    half = width // 2
    bucket_count, heads = relative_table.shape
    hidden = up_weight.shape[1]
    offsets = buckets.shape[0]
    relative = copies == 2 and width // shards % 16 == 0 and shards & (shards - 1) == 0
    me = lax.axis_index("replica") if relative else jnp.int32(0)
    spot = lax.axis_index("shard") if relative else jnp.int32(0)

    def parts_of(h):
        column = lambda w, c: lax.dynamic_slice_in_dim(w, c, half, 1)
        groups = up_weight.shape[1] // width
        return jnp.concatenate(
            [column(down_weight, h * half), column(mixing_weight, h * half)]
            + [column(up_weight, (h * groups + j) * half) for j in range(groups)],
            axis=0,
        )

    def triples_of(h):
        weights = (query_weight, key_weight, value_weight)
        starts = [(chunk + CHUNKS * h) * PAIR for chunk in range(CHUNKS)]
        return jnp.stack(
            [
                jnp.concatenate([lax.dynamic_slice_in_dim(w, at, PAIR, 1) for w in weights], axis=1)
                for at in starts
            ]
        )

    outer = shards // INNER
    if relative:
        gathered = lax.all_gather(parts_of(me), ("shard", "replica"), axis=0, tiled=True)
    else:
        gathered = lax.all_gather(jnp.stack([parts_of(0), parts_of(1)]), "shard", axis=0, tiled=True)
    gathered = gathered.reshape(shards, 2, -1, half)

    ids = block_ids.reshape(length)
    ends = jnp.sum((ids[None, :] <= ids[:, None]).astype(jnp.int32), axis=1)
    tiles = length // TILE
    final = ends.reshape(tiles, TILE)[:, TILE - 1]
    counts = (final + TILE - 1) // TILE
    starts = jnp.arange(tiles, dtype=jnp.int32) * TILE
    uses = jnp.sum((starts[:, None] < final[None, :]).astype(jnp.int32), axis=1)
    place_of = jnp.stack([me, spot % INNER, spot // INNER])
    meta = jnp.concatenate([place_of, counts, uses]).astype(jnp.int32)
    early_meta = jnp.where(jnp.arange(meta.shape[0], dtype=jnp.int32) == 2, 0, meta)

    onehot = (buckets[:, None] == jnp.arange(bucket_count, dtype=jnp.int32)[None, :]).astype(jnp.float32)
    mirrored = (buckets[::-1][:, None] == jnp.arange(bucket_count, dtype=jnp.int32)[None, :]).astype(jnp.float32)
    spare = ((0, 0), (0, 2 * length - offsets))
    forward_table, backward_table = [
        skew(jnp.pad(jnp.dot(hot, relative_table, precision=HIGH).T, spare), length) for hot in (onehot, mirrored)
    ]

    def natural(values):
        every = lax.all_gather(values, "shard", axis=0)
        return jnp.swapaxes(every.reshape((outer, INNER) + values.shape), 0, 1)

    if relative:
        own = gather_relative(triples_of(me), shards, forward_table, backward_table)
        other = swap(own)
    else:
        own, other = natural(triples_of(0)), natural(triples_of(1))

    values = wide(inputs)
    early_scale = lax.rsqrt(jnp.mean(values * values, axis=1, keepdims=True) + EPS)
    normed = low(values * early_scale * early_gain)
    turned = normed.T

    held = [
        attend_forward(c, relative, meta, normed, own, other, ends[:, None], forward_table)
        for c in range(CHUNKS)
    ]
    layer_output, state_grad, attended_grad, later_part, rest, down_own, down_other = feed_forward(
        meta, inputs, cotangent, [h[1] for h in held], later_gain, gathered
    )

    grads, diagonals, gains = {}, {}, {}

    def backward(c, side, *before):
        qkv, attended, logs, matrices = held[c]
        grad = tie(attended_grad, *before) if before else attended_grad
        grads[c, side], weight, diagonals[c, side], gains[c, side] = attend_backward(
            c, side, relative, shards, meta if c else early_meta, qkv, attended, grad, ends[None, :], logs, backward_table, turned,
            matrices,
        )
        return weight, diagonals[c, side]

    def finish(*before):
        scale = tie(early_scale, *before) if before else early_scale
        ordered = [grads[c, side] for c in range(CHUNKS) for side in range(2)]
        return last(inputs, scale, early_gain, state_grad, ordered, [h[3] for h in held])

    rows = width // shards

    def vector_of():
        early_part = sum(gains.values()).reshape(-1) / early_gain
        sides = [jnp.concatenate([diagonals[c, side] for c in range(CHUNKS)], axis=0) for side in range(2)]
        first = me == 0
        stacked = jnp.concatenate([jnp.where(first, *sides), jnp.where(first, *sides[::-1])], axis=0)[:, :offsets]
        table_part = lax.dot_general(mirrored, stacked, (((0,), (1,)), ((), ())), precision=HIGH)
        return jnp.concatenate([early_part, later_part.reshape(-1), table_part.reshape(-1)])

    def small_sums():
        vector = vector_of()
        vector = jnp.pad(vector, (0, SMALL * half - vector.shape[0])).reshape(SMALL, half)
        high = low(vector)
        return jnp.concatenate([high, low(vector - wide(high))], axis=0)

    def halve(sums):
        vector = sums[:, :SMALL] + sums[:, SMALL:]
        high = low(vector)
        return jnp.concatenate([high, low(vector - wide(high))], axis=1)

    if relative:
        share = lax.psum_scatter(
            rest.reshape((2 * shards,) + rest.shape[2:]), ("shard", "replica"), scatter_dimension=0, tiled=True
        )[0]
        down_came = swap(down_other)
        other, done = backward(0, 1)
        came = swap(other)
        down_came = tie(down_came, done)
        down_pieces = exchange(
            inner_first(low(wide(down_own) + wide(down_came)), shards), inner_groups(shards)
        )
        own, done = backward(0, 0, done, down_came)
        places = cross(own, tie(came, done))
        plane0 = plane(places, shards)
        other, done = backward(1, 1, done, *places)
        came1 = swap(other)
        own1, done = backward(1, 0, done)
        down_line = low(jnp.sum(wide(tie(down_pieces, done)), axis=0))
        line0 = low(total_of([tie(p, done) for p in plane0]))
        early = jnp.concatenate([down_line, line0], axis=1)
        pieces = exchange(early, outer_groups(shards))
        other, done = backward(2, 1, done, early)
        came1 = tie(came1, done)
        came2 = swap(other)
        own2, done = backward(2, 0, done)
        came2 = tie(came2, done)
        places = [jnp.concatenate(p, axis=1) for p in zip(cross(own1, came1), cross(own2, came2), strict=True)]
        small = small_sums()
        late = [jnp.concatenate([p, jnp.broadcast_to(small, p.shape[:1] + small.shape)], axis=1) for p in places]
        late_plane = plane(late, shards)
        early = jnp.sum(wide(tie(pieces, done)), axis=0)
        input_gradient = finish(*late, early)
        late = wide(late[0])
        for p in late_plane[1:]:
            late = late + wide(tie(p, input_gradient))
        late = jnp.concatenate([low(late[:, : 2 * rows]), halve(late[:, 2 * rows :])], axis=1)
        late = natural_halves(total_of(column(late, shards)))
        early = natural_halves(early)
        share = [wide(h) for h in natural_halves(tie(share, input_gradient))]
        small = late[0][2 * rows :] + late[1][2 * rows :]
        small = (small[:SMALL] + small[SMALL:]).reshape(-1)
        down_share = [h[:-rows] for h in early]
        shares = [[h[-rows:] for h in early], [h[:rows] for h in late], [h[rows : 2 * rows] for h in late]]
    else:
        shares = []
        for c in range(CHUNKS):
            other, _ = backward(c, 1)
            own, _ = backward(c, 0)
            shares.append(scatter_halves(own, other))
        input_gradient = finish()
        both = lax.psum_scatter(rest, "shard", scatter_dimension=0, tiled=True)[0]
        share = lax.psum((wide(both[0]), wide(both[1])), "replica")
        down_share = [
            lax.psum(wide(lax.psum_scatter(d, "shard", scatter_dimension=0, tiled=True))[0], "replica")
            for d in (down_own, down_other)
        ]
        small = lax.psum(vector_of(), ("replica", "shard"))

    early_total, later_total = small[:width], small[width : 2 * width]
    table_total = small[2 * width : 2 * width + relative_table.size].reshape(bucket_count, heads)

    groups = hidden // width
    down_share = jnp.concatenate(down_share, axis=1)
    mixing_share = jnp.concatenate([share[0][:rows], share[1][:rows]], axis=1)
    up_share = jnp.concatenate(
        [share[h][rows * (1 + j) : rows * (2 + j)] for h in range(2) for j in range(groups)], axis=1
    )
    triples = [
        jnp.concatenate(
            [shares[c][h][:, n * PAIR : (n + 1) * PAIR] for h in range(2) for c in range(CHUNKS)], axis=1
        )
        for n in range(3)
    ]
    return (
        layer_output,
        input_gradient,
        early_total,
        triples[0],
        triples[1],
        triples[2],
        mixing_share,
        table_total,
        later_total,
        up_share,
        down_share,
    )


def solution(mesh):
    rows = P(("replica", "shard"), None)
    split = P("shard", None)
    same = P()
    return jax.shard_map(
        functools.partial(body, mesh.shape["replica"], mesh.shape["shard"]),
        mesh=mesh,
        in_specs=(rows, rows, rows, same, same, split, split, split, split, same, same, split, split),
        out_specs=(rows, rows, same, split, split, split, split, same, same, split, split),
        check_vma=False,
    )
```

```python
import functools
import math

import jax
import jax.numpy as jnp
from jax import lax
from jax.experimental import pallas as pl
from jax.experimental.pallas import tpu as pltpu
from jax.sharding import PartitionSpec as P

EPS = 1e-06
HIGH = lax.Precision.HIGHEST
HEAD_DIM = 64
PAIR = 2 * HEAD_DIM
TRIPLE = 3 * PAIR
SLAB = 128
TILE = 256
CHUNKS = 3
INNER = 4
ROWS = 512
SMALL = 8
NEG = -1e30
CURVE = math.sqrt(2 / math.pi)
CUBE = 0.044715
MIB = 1 << 20


def nt(left, right):
    return lax.dot_general(left, right, (((1,), (1,)), ((), ())), preferred_element_type=jnp.float32)


def nn(left, right):
    return lax.dot_general(left, right, (((1,), (0,)), ((), ())), preferred_element_type=jnp.float32)


def tn(left, right):
    return lax.dot_general(left, right, (((0,), (0,)), ((), ())), preferred_element_type=jnp.float32)


def low(values):
    return values.astype(jnp.bfloat16)


def wide(values):
    return values.astype(jnp.float32)


def in_hbm(shape, dtype):
    return pltpu.HBM(shape, dtype)


def from_hbm(*arrays):
    return [pltpu.with_memory_space_constraint(a, pltpu.HBM) for a in arrays]


def skew_kernel(rows_ref, out_ref):
    width = rows_ref.shape[-1]
    keep = out_ref.shape[-1]
    for k in range(rows_ref.shape[0]):
        spread = jnp.broadcast_to(rows_ref[k], (SLAB, width))
        moved = pltpu.roll(spread, width - SLAB + 1, 1, stride=1, stride_axis=0)
        out_ref[k] = moved[:, :keep]


def skew(rows, length):
    count, width = rows.shape
    keep = 2 * length - SLAB
    return pl.pallas_call(
        skew_kernel,
        grid=(count // 2,),
        in_specs=[pl.BlockSpec((2, 1, width), lambda i: (i, 0, 0))],
        out_specs=pl.BlockSpec((2, SLAB, keep), lambda i: (i, 0, 0)),
        out_shape=in_hbm((count, SLAB, keep), jnp.float32),
        compiler_params=pltpu.CompilerParams(vmem_limit_bytes=32 * MIB),
        cost_estimate=pl.CostEstimate(
            flops=count * SLAB * width, bytes_accessed=count * SLAB * keep * 4, transcendentals=0
        ),
        name="skew",
    )(rows.reshape(count, 1, width))


def prepare_kernel(x_ref, gain_ref, row_ref, column_ref, normed_ref, turned_ref, scale_ref, across_ref, upright_ref):
    length = x_ref.shape[0]
    ids = row_ref[...]

    def part(n, ends):
        spot = pl.ds(pl.multiple_of(n * TILE, TILE), TILE)
        x = wide(x_ref[spot, :])
        found = lax.rsqrt(jnp.mean(x * x, axis=1, keepdims=True) + EPS)
        scale_ref[spot, :] = found
        normed_ref[spot, :] = low(x * found * gain_ref[...])
        mine = column_ref[spot, :]
        upright_ref[spot, :] = jnp.sum(jnp.where(ids <= mine, 1, 0), axis=1, keepdims=True)
        return ends + jnp.sum(jnp.where(mine <= ids, 1, 0), axis=0, keepdims=True)

    across_ref[...] = lax.fori_loop(0, length // TILE, part, jnp.zeros((1, length), jnp.int32))
    turned_ref[...] = normed_ref[...].T


def prepare(inputs, gain, ids):
    length, width = inputs.shape
    return pl.pallas_call(
        prepare_kernel,
        out_shape=[
            in_hbm((length, width), jnp.bfloat16),
            in_hbm((width, length), jnp.bfloat16),
            in_hbm((length, 1), jnp.float32),
            in_hbm((1, length), jnp.int32),
            in_hbm((length, 1), jnp.int32),
        ],
        compiler_params=pltpu.CompilerParams(vmem_limit_bytes=32 * MIB),
        cost_estimate=pl.CostEstimate(flops=1, bytes_accessed=1, transcendentals=0),
        name="prepare",
    )(inputs, gain.reshape(1, width), ids.reshape(1, length), ids.reshape(length, 1))


def shard_at(relative, meta_ref, m, k):
    return (meta_ref[2] ^ k) * INNER + (meta_ref[1] ^ m) if relative else k * INNER + m


def row_span(relative, shard, rows):
    return pl.ds(pl.multiple_of(shard * rows, 16) if relative else shard * rows, rows)


def forward_kernel(
    relative, meta_ref, normed_ref, pieces_ref, ends_ref, table_ref, qkv_ref, out_ref, log_ref, weight_ref
):
    length = normed_ref.shape[0]
    tiles = length // TILE
    inner, outer, rows, _ = pieces_ref.shape
    for m in range(inner):
        for k in range(outer):
            span = row_span(relative, shard_at(relative, meta_ref, m, k), rows)
            weight_ref[0, span, :] = pieces_ref[m, k]
    qkv_ref[0] = low(nn(normed_ref[...], weight_ref[0]))
    left = lax.broadcasted_iota(jnp.int32, (TILE, PAIR), 1) < HEAD_DIM

    def block(i, n):
        first = pl.multiple_of(i * TILE, TILE)
        query = qkv_ref[0, pl.ds(first, TILE), :PAIR]
        keys = qkv_ref[0, : n * TILE, PAIR : 2 * PAIR]
        values = qkv_ref[0, : n * TILE, 2 * PAIR :]
        ends = ends_ref[pl.ds(first, TILE), :]
        columns = lax.broadcasted_iota(jnp.int32, (TILE, n * TILE), 1)
        allowed = columns < ends
        outs = []
        zero = jnp.zeros_like(query)
        offset = pl.multiple_of((tiles - 1 - i) * TILE + SLAB, SLAB)
        before = pl.multiple_of(offset - SLAB, SLAB)
        for k in range(2):
            mine = jnp.where(left, query, zero) if k == 0 else jnp.where(left, zero, query)
            bias = jnp.concatenate(
                [table_ref[k, :, pl.ds(offset, n * TILE)], table_ref[k, :, pl.ds(before, n * TILE)]], axis=0
            )
            scores = jnp.where(allowed, nt(mine, keys) + bias, NEG)
            peak = jnp.max(scores, axis=1, keepdims=True)
            weights = jnp.exp(scores - peak)
            total = jnp.sum(weights, axis=1, keepdims=True)
            outs.append(nn(low(weights), values) / total)
            logs = jnp.broadcast_to(peak + jnp.log(total), (TILE, SLAB))
            log_ref[0, k : k + 1, pl.ds(first, TILE)] = logs.T[0:1, :]
        out_ref[0, pl.ds(first, TILE), :] = low(jnp.where(left, outs[0], outs[1]))

    def step(i, carry):
        count = meta_ref[3 + i]
        for n in range(1, tiles + 1):
            @pl.when(count == n)
            def _():
                block(i, n)
        return carry

    lax.fori_loop(0, tiles, step, 0)


def attend_forward(side, relative, meta, normed, pieces, ends, table):
    length, width = normed.shape
    keep = table.shape[-1]
    turn = lambda p, m: (p, 0, 0)
    same = lambda p, m: (0, 0)
    return pl.pallas_call(
        functools.partial(forward_kernel, relative),
        grid_spec=pltpu.PrefetchScalarGridSpec(
            num_scalar_prefetch=1,
            grid=(CHUNKS,),
            in_specs=[
                pl.BlockSpec((length, width), same),
                pl.BlockSpec(pieces.shape[:2] + (None,) + pieces.shape[3:], lambda p, m: (0, 0, p, 0, 0)),
                pl.BlockSpec((length, 1), same),
                pl.BlockSpec((2, SLAB, keep), lambda p, m: (p + CHUNKS * ((side + m[0]) % 2), 0, 0)),
            ],
            out_specs=[
                pl.BlockSpec((1, length, TRIPLE), turn),
                pl.BlockSpec((1, length, PAIR), turn),
                pl.BlockSpec((1, 2, length), turn),
                pl.BlockSpec((1, width, TRIPLE), turn),
            ],
        ),
        out_shape=[
            in_hbm((CHUNKS, length, TRIPLE), jnp.bfloat16),
            in_hbm((CHUNKS, length, PAIR), jnp.bfloat16),
            in_hbm((CHUNKS, 2, length), jnp.float32),
            in_hbm((CHUNKS, width, TRIPLE), jnp.bfloat16),
        ],
        compiler_params=pltpu.CompilerParams(vmem_limit_bytes=48 * MIB),
        cost_estimate=pl.CostEstimate(
            flops=24 * length * length * HEAD_DIM * 2,
            bytes_accessed=3 * length * (width + 2 * TRIPLE) + 6 * SLAB * keep * 4,
            transcendentals=6 * length * length,
        ),
        name="attend_forward",
    )(meta, *from_hbm(normed), pieces, *from_hbm(ends, table))


def backward_kernel(
    relative, chunk, meta_ref, qkv_ref, out_ref, grad_ref, ends_ref, log_ref, table_ref, turned_ref, matrix_ref,
    dqkv_ref, weight_ref, diag_ref, gain_ref,
    qm, gm, kt, dq_acc, skewed, delta, summed, turned, matrix, sems,
):
    fetches = [
        pltpu.make_async_copy(turned_ref, turned, sems.at[0]),
        pltpu.make_async_copy(matrix_ref.at[chunk], matrix, sems.at[1]),
    ]
    for fetch in fetches:
        fetch.start()
    length = qkv_ref.shape[1]
    tiles = length // TILE
    left = lax.broadcasted_iota(jnp.int32, (length, PAIR), 1) < HEAD_DIM
    query, grads = qkv_ref[0, :, :PAIR], grad_ref[0, 0]
    zero = jnp.zeros_like(query)
    for k in range(2):
        pick = left if k == 0 else jnp.logical_not(left)
        qm[k] = jnp.where(pick, query, zero)
        gm[k] = jnp.where(pick, grads, zero)
    kt[...] = qkv_ref[0, :, PAIR : 2 * PAIR].T
    dq_acc[...] = jnp.zeros_like(dq_acc)
    skewed[...] = jnp.zeros_like(skewed)
    product = wide(grads) * wide(out_ref[0])
    high = low(product)
    rest = low(product - wide(high))
    lane = lax.broadcasted_iota(jnp.int32, (16, PAIR), 1)
    row = lax.broadcasted_iota(jnp.int32, (16, PAIR), 0)
    chooser = low(jnp.where(lane // HEAD_DIM == row, 1.0, 0.0))
    delta[...] = nt(chooser, high) + nt(chooser, rest)

    def block(kb, n):
        kf = pl.multiple_of(kb * TILE, TILE)
        qf = length - n * TILE
        span = n * TILE
        offset = pl.multiple_of((2 * tiles - 1 - n - kb) * TILE + SLAB, SLAB)
        before = pl.multiple_of(offset - SLAB, SLAB)
        rows = lax.broadcasted_iota(jnp.int32, (TILE, span), 0) + kf
        allowed = rows < ends_ref[:, qf:]
        k_tile = qkv_ref[0, pl.ds(kf, TILE), PAIR : 2 * PAIR]
        v_tile = qkv_ref[0, pl.ds(kf, TILE), 2 * PAIR :]
        dk = jnp.zeros((TILE, PAIR), jnp.float32)
        dv = jnp.zeros((TILE, PAIR), jnp.float32)
        for k in range(2):
            q_part = qm[k, qf:, :]
            g_part = gm[k, qf:, :]
            bias = jnp.concatenate(
                [table_ref[k, :, pl.ds(offset, span)], table_ref[k, :, pl.ds(before, span)]], axis=0
            )
            scores = nt(k_tile, q_part) + bias - log_ref[0, k : k + 1, qf:]
            probs = jnp.where(allowed, jnp.exp(scores), 0.0)
            above = nt(v_tile, g_part) - delta[k : k + 1, qf:]
            grad = probs * above
            skewed[k, :, pl.ds(offset, span)] += grad[:SLAB]
            skewed[k, :, pl.ds(before, span)] += grad[SLAB:]
            grad_low = low(grad)
            dv = dv + nn(low(probs), g_part)
            dk = dk + nn(grad_low, q_part)
            head = slice(k * HEAD_DIM, (k + 1) * HEAD_DIM)
            dq_acc[head, qf:] += nn(kt[head, pl.ds(kf, TILE)], grad_low)
        dqkv_ref[pl.ds(kf, TILE), PAIR : 2 * PAIR] = low(dk)
        dqkv_ref[pl.ds(kf, TILE), 2 * PAIR :] = low(dv)

    def step(kb, carry):
        count = meta_ref[3 + tiles + kb]
        for n in range(1, tiles + 1):
            @pl.when(count == n)
            def _():
                block(kb, n)
        return carry

    lax.fori_loop(0, tiles, step, 0)
    dqkv_ref[:, :PAIR] = low(dq_acc[...].T)
    for fetch in fetches:
        fetch.wait()
    exact = nn(turned[...], dqkv_ref[...])
    summed[...] = low(exact)
    by_row = jnp.sum(exact * wide(matrix[...]), axis=1, keepdims=True)
    gain_ref[...] = jnp.broadcast_to(by_row, (by_row.shape[0], SLAB)).T[0:1, :]
    inner, outer, rows, _ = weight_ref.shape
    for m in range(inner):
        for k in range(outer):
            weight_ref[m, k] = summed[row_span(relative, shard_at(relative, meta_ref, m, k), rows), :]

    group = lax.broadcasted_iota(jnp.int32, (8, skewed.shape[-1]), 0)
    for k in range(2):
        held = skewed[k, SLAB - 8 :, :]
        for a in range(SLAB // 8 - 1):
            held = held + pltpu.roll(skewed[k, a * 8 : (a + 1) * 8, :], SLAB - 8 * (a + 1), 1)
        for bit in (1, 2, 4):
            held = jnp.where(((7 - group) & bit) != 0, pltpu.roll(held, bit, 1), held)
        diag_ref[k : k + 1, :] = jnp.sum(held, axis=0, keepdims=True)


def attend_backward(chunk, side, relative, shards, meta, qkv, out, grad, ends, logs, table, turned, matrices):
    length = qkv.shape[1]
    width = turned.shape[0]
    keep = table.shape[-1]
    lanes = 2 * length
    turn = lambda i, m: (chunk, 0, 0)
    same = lambda i, m: (0, 0)
    piece = (INNER, shards // INNER, width // shards, TRIPLE)
    return pl.pallas_call(
        functools.partial(backward_kernel, relative, chunk),
        grid_spec=pltpu.PrefetchScalarGridSpec(
            num_scalar_prefetch=1,
            grid=(1,),
            in_specs=[
                pl.BlockSpec((1, length, TRIPLE), turn),
                pl.BlockSpec((1, length, PAIR), turn),
                pl.BlockSpec((1, 1, length, PAIR), lambda i, m: (chunk, side, 0, 0)),
                pl.BlockSpec((1, length), same),
                pl.BlockSpec((1, 2, length), turn),
                pl.BlockSpec((2, SLAB, keep), lambda i, m: (chunk + CHUNKS * ((side + m[0]) % 2), 0, 0)),
                pl.BlockSpec(memory_space=pl.ANY),
                pl.BlockSpec(memory_space=pl.ANY),
            ],
            out_specs=[
                pl.BlockSpec((length, TRIPLE), same),
                pl.BlockSpec(piece, lambda i, m: (0, 0, 0, 0)),
                pl.BlockSpec((2, lanes), same),
                pl.BlockSpec((1, width), same),
            ],
            scratch_shapes=[
                pltpu.VMEM((2, length, PAIR), jnp.bfloat16),
                pltpu.VMEM((2, length, PAIR), jnp.bfloat16),
                pltpu.VMEM((PAIR, length), jnp.bfloat16),
                pltpu.VMEM((PAIR, length), jnp.float32),
                pltpu.VMEM((2, SLAB, lanes), jnp.float32),
                pltpu.VMEM((16, length), jnp.float32),
                pltpu.VMEM((width, TRIPLE), jnp.bfloat16),
                pltpu.VMEM((width, length), jnp.bfloat16),
                pltpu.VMEM((width, TRIPLE), jnp.bfloat16),
                pltpu.SemaphoreType.DMA((2,)),
            ],
        ),
        out_shape=[
            in_hbm((length, TRIPLE), jnp.bfloat16),
            in_hbm(piece, jnp.bfloat16),
            in_hbm((2, lanes), jnp.float32),
            in_hbm((1, width), jnp.float32),
        ],
        compiler_params=pltpu.CompilerParams(vmem_limit_bytes=40 * MIB),
        cost_estimate=pl.CostEstimate(
            flops=1, bytes_accessed=1, transcendentals=0
        ),
        name="attend_backward",
    )(meta, *from_hbm(qkv, out, grad), ends, logs, *from_hbm(table, turned, matrices))


def feed_kernel(
    meta_ref, x_ref, cot_ref, own_att_ref, other_att_ref, gain_ref, mix_ref, up0_ref, up1_ref, down_ref,
    out_ref, sgrad_ref, agrad_ref, later_ref, rest_ref, own_ref, other_ref,
    state, scale, normed, turned, total, upstream, act, pre, mixing, attended, branch, up, down,
):
    block = pl.program_id(0)
    blocks = pl.num_programs(0)
    me = meta_ref[0]
    length, width = x_ref.shape
    half = width // 2
    shards, _, rows, _ = mix_ref.shape
    count = length // ROWS

    @pl.when(block == 0)
    def _():
        for c in range(2):
            mixing[:, c * half : (c + 1) * half] = mix_ref[:, c].reshape(width, half)
        for p, ref in enumerate((own_att_ref, other_att_ref)):
            for i in range(CHUNKS):
                spot = pl.multiple_of((i + CHUNKS * ((p + me) % 2)) * PAIR, PAIR)
                attended[:, pl.ds(spot, PAIR)] = ref[i]

        def start(n, carry):
            spot = pl.ds(pl.multiple_of(n * ROWS, ROWS), ROWS)
            held = wide(x_ref[spot, :]) + nn(attended[spot, :], mixing[...])
            state[spot, :] = held
            found = lax.rsqrt(jnp.mean(held * held, axis=1, keepdims=True) + EPS)
            scale[spot, :] = jnp.broadcast_to(found, (ROWS, SLAB))
            normed[spot, :] = low(held * found * gain_ref[...])
            return carry

        lax.fori_loop(0, count, start, 0)
        turned[...] = normed[...].T
        total[...] = jnp.zeros_like(total)
        upstream[...] = jnp.zeros_like(upstream)

    for c, ref in enumerate((up0_ref, up1_ref)):
        up[:, c * half : (c + 1) * half] = ref[...].reshape(width, half)
        down[:, c * half : (c + 1) * half] = down_ref[:, c].reshape(width, half)

    def middle(n, carry):
        spot = pl.ds(n * ROWS, ROWS)
        v = nn(normed[spot, :], up[...])
        square = v * v
        bent = jnp.tanh(v * (CURVE + (CURVE * CUBE) * square))
        gate = 0.5 + 0.5 * bent
        slope = gate + (0.5 * v) * (1.0 - bent * bent) * (CURVE + (3 * CURVE * CUBE) * square)
        active = low(v * gate)
        act[spot, :] = active
        total[spot, :] += nn(active, down[...])
        changed = low(nt(cot_ref[spot, :], down[...]) * slope)
        pre[spot, :] = changed
        upstream[spot, :] += nt(changed, up[...])
        return carry

    for n in range(count):
        middle(n, 0)
    long = down_ref.shape[2]
    per = width // long
    steps = blocks // 2

    def halves(values):
        left, right = values[:, :half], values[:, half:]
        first = me == 0
        return jnp.where(first, left, right), jnp.where(first, right, left)

    kept, sent = halves(low(tn(act[...], cot_ref[...])))
    for s in range(per):
        own_ref[s % INNER, s // INNER] = kept[s * long : (s + 1) * long]
        other_ref[s % INNER, s // INNER] = sent[s * long : (s + 1) * long]
    dup = low(nn(turned[...], pre[...]))
    for c in range(2):
        start = pl.multiple_of(rows + (block % steps * 2 + c) * rows, rows)
        for s in range(shards):
            rest_ref[s, block // steps, pl.ds(start, rows)] = dup[
                s * rows : (s + 1) * rows, c * half : (c + 1) * half
            ]

    @pl.when(block == blocks - 1)
    def _():
        gain = gain_ref[...]

        def finish(n, parts):
            spot = pl.ds(pl.multiple_of(n * ROWS, ROWS), ROWS)
            held = state[spot, :]
            found = scale[spot, :][:, :1]
            out_ref[spot, :] = low(held + total[spot, :])
            grads = upstream[spot, :]
            parts = parts + jnp.sum(grads * held * found, axis=0, keepdims=True)
            scaled = grads * gain
            mean = jnp.mean(scaled * held, axis=1, keepdims=True)
            result = wide(cot_ref[spot, :]) + found * (scaled - held * (found * found * mean))
            sgrad_ref[spot, :] = result
            rounded = low(result)
            branch[spot, :] = rounded
            back = low(nt(rounded, mixing[...]))
            for pair in range(width // PAIR):
                agrad_ref[pair % CHUNKS, (pair // CHUNKS + me) % 2, spot, :] = back[
                    :, pair * PAIR : (pair + 1) * PAIR
                ]
            return parts

        later_ref[...] = lax.fori_loop(0, count, finish, jnp.zeros((1, width), jnp.float32))
        dmix = low(tn(attended[...], branch[...]))
        for s in range(shards):
            for c in range(2):
                rest_ref[s, c, :rows] = dmix[s * rows : (s + 1) * rows, c * half : (c + 1) * half]


def feed_forward(meta, inputs, cotangent, attended, gain, gathered):
    length, width = inputs.shape
    half = width // 2
    shards, _, every, _ = gathered.shape
    rows = width // shards
    groups = (every - rows) // (2 * rows)
    long = groups * rows
    per = width // long
    steps = groups // 2
    blocks = 2 * steps
    same = lambda b, m: (0, 0)
    full = pl.BlockSpec((length, width), same)
    pair = pl.BlockSpec((CHUNKS, length, PAIR), lambda b, m: (0, 0, 0))
    return pl.pallas_call(
        feed_kernel,
        grid_spec=pltpu.PrefetchScalarGridSpec(
            num_scalar_prefetch=1,
            grid=(blocks,),
            in_specs=[
                full, full, pair, pair,
                pl.BlockSpec((1, width), same),
                pl.BlockSpec((shards, 2, rows, half), lambda b, m: (0, 0, groups, 0)),
                pl.BlockSpec((shards, 1, rows, half), lambda b, m: (0, b // steps, groups + 1 + 2 * (b % steps), 0)),
                pl.BlockSpec((shards, 1, rows, half), lambda b, m: (0, b // steps, groups + 2 + 2 * (b % steps), 0)),
                pl.BlockSpec((per, 2, long, half), lambda b, m: (b, 0, 0, 0)),
            ],
            out_specs=[
                full, full,
                pl.BlockSpec((CHUNKS, 2, length, PAIR), lambda b, m: (0, 0, 0, 0)),
                pl.BlockSpec((1, width), same),
                pl.BlockSpec((shards, 2, every - long, half), lambda b, m: (0, 0, 0, 0)),
                pl.BlockSpec((INNER, per // INNER, long, half), lambda b, m: (0, b, 0, 0)),
                pl.BlockSpec((INNER, per // INNER, long, half), lambda b, m: (0, b, 0, 0)),
            ],
            scratch_shapes=[
                pltpu.VMEM((length, width), jnp.float32),
                pltpu.VMEM((length, SLAB), jnp.float32),
                pltpu.VMEM((length, width), jnp.bfloat16),
                pltpu.VMEM((width, length), jnp.bfloat16),
                pltpu.VMEM((length, width), jnp.float32),
                pltpu.VMEM((length, width), jnp.float32),
                pltpu.VMEM((length, width), jnp.bfloat16),
                pltpu.VMEM((length, width), jnp.bfloat16),
                pltpu.VMEM((width, width), jnp.bfloat16),
                pltpu.VMEM((length, width), jnp.bfloat16),
                pltpu.VMEM((length, width), jnp.bfloat16),
                pltpu.VMEM((width, width), jnp.bfloat16),
                pltpu.VMEM((width, width), jnp.bfloat16),
            ],
        ),
        out_shape=[
            in_hbm((length, width), jnp.bfloat16),
            in_hbm((length, width), jnp.float32),
            in_hbm((CHUNKS, 2, length, PAIR), jnp.bfloat16),
            in_hbm((1, width), jnp.float32),
            in_hbm((shards, 2, every - long, half), jnp.bfloat16),
            in_hbm((INNER, shards // INNER, long, half), jnp.bfloat16),
            in_hbm((INNER, shards // INNER, long, half), jnp.bfloat16),
        ],
        compiler_params=pltpu.CompilerParams(vmem_limit_bytes=60 * MIB),
        cost_estimate=pl.CostEstimate(
            flops=12 * length * width * width * blocks + 6 * length * width * width,
            bytes_accessed=14 * length * width + 8 * width * width * blocks,
            transcendentals=length * width * blocks,
        ),
        name="feed_forward",
    )(meta, inputs, cotangent, *attended, gain.reshape(1, width), *[gathered] * 4)


def last_kernel(x_ref, scale_ref, gain_ref, sgrad_ref, *refs):
    grads, weights = refs[: 2 * CHUNKS], refs[2 * CHUNKS : 2 * CHUNKS + 2]
    out_ref = refs[2 * CHUNKS + 2]
    x = wide(x_ref[...])
    found = scale_ref[...]
    upstream = jnp.zeros(x.shape, jnp.float32)
    for i in range(CHUNKS):
        for side in range(2):
            upstream = upstream + nt(grads[2 * i + side][...], weights[side][i])
    scaled = upstream * gain_ref[...]
    mean = jnp.mean(scaled * x, axis=1, keepdims=True)
    out_ref[...] = low(sgrad_ref[...] + found * (scaled - x * (found * found * mean)))


def last(inputs, scale, gain, state_grad, grads, weights):
    length, width = inputs.shape
    step = lambda i: (i, 0)
    same = lambda i: (0, 0)
    return pl.pallas_call(
        last_kernel,
        grid=(length // ROWS,),
        in_specs=[
            pl.BlockSpec((ROWS, width), step),
            pl.BlockSpec((ROWS, 1), step),
            pl.BlockSpec((1, width), same),
            pl.BlockSpec((ROWS, width), step),
        ]
        + [pl.BlockSpec((ROWS, TRIPLE), step)] * (2 * CHUNKS)
        + [pl.BlockSpec((CHUNKS, width, TRIPLE), lambda i: (0, 0, 0))] * 2,
        out_specs=pl.BlockSpec((ROWS, width), step),
        out_shape=in_hbm((length, width), jnp.bfloat16),
        compiler_params=pltpu.CompilerParams(vmem_limit_bytes=48 * MIB),
        cost_estimate=pl.CostEstimate(
            flops=1, bytes_accessed=1, transcendentals=0
        ),
        name="last",
    )(inputs, scale, gain.reshape(1, width), state_grad, *from_hbm(*grads, *weights))


def swap(values):
    return lax.ppermute(values, "replica", [(0, 1), (1, 0)])


def shift(values, shards, distance):
    return lax.ppermute(values, "shard", [(i, i ^ distance) for i in range(shards)])


def tie(values, *before):
    return lax.optimization_barrier((values,) + before)[0]


def gather_relative(own, shards, *before):
    line = jnp.stack([own] + [shift(own, shards, k * INNER) for k in range(1, shards // INNER)])
    came = [shift(line, shards, m) for m in range(1, INNER)]
    return jnp.stack([line] + [tie(c, *before) for c in came])


def cross(own, came):
    return [low(wide(own[m]) + wide(came[m])) for m in range(INNER)]


def plane(places, shards):
    return [places[0]] + [shift(places[m], shards, m) for m in range(1, INNER)]


def column(line, shards):
    return [line[0]] + [shift(line[k], shards, k * INNER) for k in range(1, shards // INNER)]


def total_of(parts):
    total = wide(parts[0])
    for part in parts[1:]:
        total = total + wide(part)
    return total


def exchange(pieces, groups):
    return lax.all_to_all(pieces, "shard", 0, 0, axis_index_groups=groups)


def inner_groups(shards):
    return [[o * INNER + i for i in range(INNER)] for o in range(shards // INNER)]


def outer_groups(shards):
    return [[o * INNER + i for o in range(shards // INNER)] for i in range(INNER)]


def natural_halves(own):
    other = swap(own)
    first = lax.axis_index("replica") == 0
    return jnp.where(first, own, other), jnp.where(first, other, own)


def scatter_halves(own, other):
    halves = []
    for part in (own, other):
        whole = jnp.swapaxes(part, 0, 1).reshape((-1,) + part.shape[2:])
        halves.append(wide(lax.psum_scatter(whole, "shard", scatter_dimension=0, tiled=True))[0])
    return lax.psum(tuple(halves), "replica")


def body(
    copies,
    shards,
    inputs,
    cotangent,
    block_ids,
    buckets,
    early_gain,
    query_weight,
    key_weight,
    value_weight,
    mixing_weight,
    relative_table,
    later_gain,
    up_weight,
    down_weight,
):
    length, width = inputs.shape
    half = width // 2
    bucket_count, heads = relative_table.shape
    hidden = up_weight.shape[1]
    offsets = buckets.shape[0]
    relative = copies == 2 and width // shards % 16 == 0 and shards & (shards - 1) == 0
    me = lax.axis_index("replica") if relative else jnp.int32(0)
    spot = lax.axis_index("shard") if relative else jnp.int32(0)

    def parts_of(h):
        column = lambda w, c: lax.dynamic_slice_in_dim(w, c, half, 1)
        groups = up_weight.shape[1] // width
        return jnp.concatenate(
            [column(down_weight, h * half), column(mixing_weight, h * half)]
            + [column(up_weight, (h * groups + j) * half) for j in range(groups)],
            axis=0,
        )

    def triples_of(h):
        weights = (query_weight, key_weight, value_weight)
        starts = [(chunk + CHUNKS * h) * PAIR for chunk in range(CHUNKS)]
        return jnp.stack(
            [
                jnp.concatenate([lax.dynamic_slice_in_dim(w, at, PAIR, 1) for w in weights], axis=1)
                for at in starts
            ]
        )

    outer = shards // INNER
    if relative:
        gathered = lax.all_gather(parts_of(me), ("shard", "replica"), axis=0, tiled=True)
    else:
        gathered = lax.all_gather(jnp.stack([parts_of(0), parts_of(1)]), "shard", axis=0, tiled=True)
    gathered = gathered.reshape(shards, 2, -1, half)

    normed, turned, early_scale, across, upright = prepare(inputs, early_gain, block_ids)
    tiles = length // TILE
    final = across.reshape(tiles, TILE)[:, TILE - 1]
    counts = (final + TILE - 1) // TILE
    starts = jnp.arange(tiles, dtype=jnp.int32) * TILE
    uses = jnp.sum((starts[:, None] < final[None, :]).astype(jnp.int32), axis=1)
    place_of = jnp.stack([me, spot % INNER, spot // INNER])
    meta = jnp.concatenate([place_of, counts, uses]).astype(jnp.int32)
    early_meta = jnp.where(jnp.arange(meta.shape[0], dtype=jnp.int32) == 2, 0, meta)

    onehot = (buckets[:, None] == jnp.arange(bucket_count, dtype=jnp.int32)[None, :]).astype(jnp.float32)
    mirrored = (buckets[::-1][:, None] == jnp.arange(bucket_count, dtype=jnp.int32)[None, :]).astype(jnp.float32)
    spare = ((0, 0), (0, 2 * length - offsets))
    forward_table, backward_table = [
        skew(jnp.pad(jnp.dot(hot, relative_table, precision=HIGH).T, spare), length) for hot in (onehot, mirrored)
    ]

    def natural(values):
        every = lax.all_gather(values, "shard", axis=0)
        return jnp.swapaxes(every.reshape((outer, INNER) + values.shape), 0, 1)

    if relative:
        own = gather_relative(triples_of(me), shards, forward_table, backward_table, normed, turned, upright, meta)
        other = swap(own)
    else:
        own, other = natural(triples_of(0)), natural(triples_of(1))

    held = [attend_forward(0, relative, meta, normed, own, upright, forward_table)]
    other = tie(other, held[0][2])
    held.append(attend_forward(1, relative, meta, normed, other, upright, forward_table))
    layer_output, state_grad, attended_grad, later_part, rest, down_own, down_other = feed_forward(
        meta, inputs, cotangent, [h[1] for h in held], later_gain, gathered
    )

    grads, diagonals, gains = {}, {}, {}

    def backward(c, side, *before):
        qkv, attended, logs, matrices = held[side]
        grad = tie(attended_grad, *before) if before else attended_grad
        grads[c, side], weight, diagonals[c, side], gains[c, side] = attend_backward(
            c, side, relative, shards, meta if c else early_meta, qkv, attended, grad, across, logs, backward_table, turned,
            matrices,
        )
        return weight, diagonals[c, side]

    def finish(*before):
        scale = tie(early_scale, *before) if before else early_scale
        ordered = [grads[c, side] for c in range(CHUNKS) for side in range(2)]
        return last(inputs, scale, early_gain, state_grad, ordered, [h[3] for h in held])

    rows = width // shards

    def vector_of():
        early_part = sum(gains.values()).reshape(-1) / early_gain
        sides = [jnp.concatenate([diagonals[c, side] for c in range(CHUNKS)], axis=0) for side in range(2)]
        first = me == 0
        stacked = jnp.concatenate([jnp.where(first, *sides), jnp.where(first, *sides[::-1])], axis=0)[:, :offsets]
        table_part = lax.dot_general(mirrored, stacked, (((0,), (1,)), ((), ())), precision=HIGH)
        return jnp.concatenate([early_part, later_part.reshape(-1), table_part.reshape(-1)])

    def small_sums():
        vector = vector_of()
        vector = jnp.pad(vector, (0, SMALL * half - vector.shape[0])).reshape(SMALL, half)
        high = low(vector)
        return jnp.concatenate([high, low(vector - wide(high))], axis=0)

    def halve(sums):
        vector = sums[:, :SMALL] + sums[:, SMALL:]
        high = low(vector)
        return jnp.concatenate([high, low(vector - wide(high))], axis=1)

    if relative:
        share = lax.psum_scatter(
            rest.reshape((2 * shards,) + rest.shape[2:]), ("shard", "replica"), scatter_dimension=0, tiled=True
        )[0]
        down_came = swap(down_other)
        other, done = backward(0, 1)
        came = swap(other)
        down_came = tie(down_came, done)
        down_pieces = exchange(
            low(wide(down_own) + wide(down_came)), inner_groups(shards)
        )
        own, done = backward(0, 0, done, down_came)
        places = cross(own, tie(came, done))
        plane0 = plane(places, shards)
        other, done = backward(1, 1, done, *places)
        came1 = swap(other)
        own1, done = backward(1, 0, done)
        down_line = low(jnp.sum(wide(tie(down_pieces, done)), axis=0))
        line0 = low(total_of([tie(p, done) for p in plane0]))
        early = jnp.concatenate([down_line, line0], axis=1)
        pieces = exchange(early, outer_groups(shards))
        other, done = backward(2, 1, done, early)
        came1 = tie(came1, done)
        came2 = swap(other)
        own2, done = backward(2, 0, done)
        came2 = tie(came2, done)
        places = [jnp.concatenate(p, axis=1) for p in zip(cross(own1, came1), cross(own2, came2), strict=True)]
        small = small_sums()
        late = [jnp.concatenate([p, jnp.broadcast_to(small, p.shape[:1] + small.shape)], axis=1) for p in places]
        late_plane = plane(late, shards)
        early = jnp.sum(wide(tie(pieces, done)), axis=0)
        input_gradient = finish(*late, early)
        late = wide(late[0])
        for p in late_plane[1:]:
            late = late + wide(tie(p, input_gradient))
        late = jnp.concatenate([low(late[:, : 2 * rows]), halve(late[:, 2 * rows :])], axis=1)
        late = natural_halves(total_of(column(late, shards)))
        early = natural_halves(early)
        share = [wide(h) for h in natural_halves(tie(share, input_gradient))]
        small = late[0][2 * rows :] + late[1][2 * rows :]
        small = (small[:SMALL] + small[SMALL:]).reshape(-1)
        down_share = [h[:-rows] for h in early]
        shares = [[h[-rows:] for h in early], [h[:rows] for h in late], [h[rows : 2 * rows] for h in late]]
    else:
        shares = []
        for c in range(CHUNKS):
            other, _ = backward(c, 1)
            own, _ = backward(c, 0)
            shares.append(scatter_halves(own, other))
        input_gradient = finish()
        both = lax.psum_scatter(rest, "shard", scatter_dimension=0, tiled=True)[0]
        share = lax.psum((wide(both[0]), wide(both[1])), "replica")
        down_share = [
            lax.psum(
                wide(
                    lax.psum_scatter(
                        jnp.swapaxes(d, 0, 1).reshape((shards,) + d.shape[2:]), "shard", scatter_dimension=0, tiled=True
                    )
                )[0],
                "replica",
            )
            for d in (down_own, down_other)
        ]
        small = lax.psum(vector_of(), ("replica", "shard"))

    early_total, later_total = small[:width], small[width : 2 * width]
    table_total = small[2 * width : 2 * width + relative_table.size].reshape(bucket_count, heads)

    groups = hidden // width
    down_share = jnp.concatenate(down_share, axis=1)
    mixing_share = jnp.concatenate([share[0][:rows], share[1][:rows]], axis=1)
    up_share = jnp.concatenate(
        [share[h][rows * (1 + j) : rows * (2 + j)] for h in range(2) for j in range(groups)], axis=1
    )
    triples = [
        jnp.concatenate(
            [shares[c][h][:, n * PAIR : (n + 1) * PAIR] for h in range(2) for c in range(CHUNKS)], axis=1
        )
        for n in range(3)
    ]
    return (
        layer_output,
        input_gradient,
        early_total,
        triples[0],
        triples[1],
        triples[2],
        mixing_share,
        table_total,
        later_total,
        up_share,
        down_share,
    )


def solution(mesh):
    rows = P(("replica", "shard"), None)
    split = P("shard", None)
    same = P()
    return jax.shard_map(
        functools.partial(body, mesh.shape["replica"], mesh.shape["shard"]),
        mesh=mesh,
        in_specs=(rows, rows, rows, same, same, split, split, split, split, same, same, split, split),
        out_specs=(rows, rows, same, split, split, split, split, same, same, split, split),
        check_vma=False,
    )
```

```python
import functools
import math

import jax
import jax.numpy as jnp
from jax import lax
from jax.experimental import pallas as pl
from jax.experimental.pallas import tpu as pltpu
from jax.sharding import PartitionSpec as P

EPS = 1e-06
HIGH = lax.Precision.HIGHEST
HEAD_DIM = 64
PAIR = 2 * HEAD_DIM
TRIPLE = 3 * PAIR
SLAB = 128
TILE = 256
CHUNKS = 3
INNER = 4
ROWS = 512
SMALL = 8
NEG = -1e30
CURVE = math.sqrt(2 / math.pi)
CUBE = 0.044715
MIB = 1 << 20


def nt(left, right):
    return lax.dot_general(left, right, (((1,), (1,)), ((), ())), preferred_element_type=jnp.float32)


def nn(left, right):
    return lax.dot_general(left, right, (((1,), (0,)), ((), ())), preferred_element_type=jnp.float32)


def tn(left, right):
    return lax.dot_general(left, right, (((0,), (0,)), ((), ())), preferred_element_type=jnp.float32)


def low(values):
    return values.astype(jnp.bfloat16)


def wide(values):
    return values.astype(jnp.float32)


def in_hbm(shape, dtype):
    return pltpu.HBM(shape, dtype)


def from_hbm(*arrays):
    return [pltpu.with_memory_space_constraint(a, pltpu.HBM) for a in arrays]


def skew_kernel(rows_ref, out_ref):
    width = rows_ref.shape[-1]
    keep = out_ref.shape[-1]
    for k in range(rows_ref.shape[0]):
        spread = jnp.broadcast_to(rows_ref[k], (SLAB, width))
        moved = pltpu.roll(spread, width - SLAB + 1, 1, stride=1, stride_axis=0)
        out_ref[k] = moved[:, :keep]


def skew(rows, length):
    count, width = rows.shape
    keep = 2 * length - SLAB
    return pl.pallas_call(
        skew_kernel,
        grid=(count // 2,),
        in_specs=[pl.BlockSpec((2, 1, width), lambda i: (i, 0, 0))],
        out_specs=pl.BlockSpec((2, SLAB, keep), lambda i: (i, 0, 0)),
        out_shape=in_hbm((count, SLAB, keep), jnp.float32),
        compiler_params=pltpu.CompilerParams(vmem_limit_bytes=32 * MIB),
        cost_estimate=pl.CostEstimate(
            flops=count * SLAB * width, bytes_accessed=count * SLAB * keep * 4, transcendentals=0
        ),
        name="skew",
    )(rows.reshape(count, 1, width))


def prepare_kernel(x_ref, gain_ref, row_ref, column_ref, normed_ref, turned_ref, scale_ref, across_ref, upright_ref):
    length = x_ref.shape[0]
    ids = row_ref[...]

    def part(n, ends):
        spot = pl.ds(pl.multiple_of(n * TILE, TILE), TILE)
        x = wide(x_ref[spot, :])
        found = lax.rsqrt(jnp.mean(x * x, axis=1, keepdims=True) + EPS)
        scale_ref[spot, :] = found
        normed_ref[spot, :] = low(x * found * gain_ref[...])
        mine = column_ref[spot, :]
        upright_ref[spot, :] = jnp.sum(jnp.where(ids <= mine, 1, 0), axis=1, keepdims=True)
        return ends + jnp.sum(jnp.where(mine <= ids, 1, 0), axis=0, keepdims=True)

    across_ref[...] = lax.fori_loop(0, length // TILE, part, jnp.zeros((1, length), jnp.int32))
    turned_ref[...] = normed_ref[...].T


def prepare(inputs, gain, ids):
    length, width = inputs.shape
    return pl.pallas_call(
        prepare_kernel,
        out_shape=[
            in_hbm((length, width), jnp.bfloat16),
            in_hbm((width, length), jnp.bfloat16),
            in_hbm((length, 1), jnp.float32),
            in_hbm((1, length), jnp.int32),
            in_hbm((length, 1), jnp.int32),
        ],
        compiler_params=pltpu.CompilerParams(vmem_limit_bytes=32 * MIB),
        cost_estimate=pl.CostEstimate(flops=1, bytes_accessed=1, transcendentals=0),
        name="prepare",
    )(inputs, gain.reshape(1, width), ids.reshape(1, length), ids.reshape(length, 1))


def shard_at(relative, meta_ref, m, k):
    return (meta_ref[2] ^ k) * INNER + (meta_ref[1] ^ m) if relative else k * INNER + m


def row_span(relative, shard, rows):
    return pl.ds(pl.multiple_of(shard * rows, 16) if relative else shard * rows, rows)


def forward_kernel(
    relative, meta_ref, normed_ref, pieces_ref, ends_ref, table_ref, qkv_ref, out_ref, log_ref, weight_ref
):
    length = normed_ref.shape[0]
    tiles = length // TILE
    inner, outer, rows, _ = pieces_ref.shape
    for m in range(inner):
        for k in range(outer):
            span = row_span(relative, shard_at(relative, meta_ref, m, k), rows)
            weight_ref[0, span, :] = pieces_ref[m, k]
    qkv_ref[0] = low(nn(normed_ref[...], weight_ref[0]))
    left = lax.broadcasted_iota(jnp.int32, (TILE, PAIR), 1) < HEAD_DIM

    def block(i, n):
        first = pl.multiple_of(i * TILE, TILE)
        query = qkv_ref[0, pl.ds(first, TILE), :PAIR]
        keys = qkv_ref[0, : n * SLAB, PAIR : 2 * PAIR]
        values = qkv_ref[0, : n * SLAB, 2 * PAIR :]
        ends = ends_ref[pl.ds(first, TILE), :]
        columns = lax.broadcasted_iota(jnp.int32, (TILE, n * SLAB), 1)
        allowed = columns < ends
        outs = []
        zero = jnp.zeros_like(query)
        offset = pl.multiple_of((tiles - 1 - i) * TILE + SLAB, SLAB)
        before = pl.multiple_of(offset - SLAB, SLAB)
        for k in range(2):
            mine = jnp.where(left, query, zero) if k == 0 else jnp.where(left, zero, query)
            bias = jnp.concatenate(
                [table_ref[k, :, pl.ds(offset, n * SLAB)], table_ref[k, :, pl.ds(before, n * SLAB)]], axis=0
            )
            scores = jnp.where(allowed, nt(mine, keys) + bias, NEG)
            peak = jnp.max(scores, axis=1, keepdims=True)
            weights = jnp.exp(scores - peak)
            total = jnp.sum(weights, axis=1, keepdims=True)
            outs.append(nn(low(weights), values) / total)
            logs = jnp.broadcast_to(peak + jnp.log(total), (TILE, SLAB))
            log_ref[0, k : k + 1, pl.ds(first, TILE)] = logs.T[0:1, :]
        out_ref[0, pl.ds(first, TILE), :] = low(jnp.where(left, outs[0], outs[1]))

    def step(i, carry):
        count = meta_ref[3 + i]
        for n in range(TILE // SLAB, length // SLAB + 1):
            @pl.when(count == n)
            def _():
                block(i, n)
        return carry

    lax.fori_loop(0, tiles, step, 0)


def attend_forward(side, relative, meta, normed, pieces, ends, table):
    length, width = normed.shape
    keep = table.shape[-1]
    turn = lambda p, m: (p, 0, 0)
    same = lambda p, m: (0, 0)
    return pl.pallas_call(
        functools.partial(forward_kernel, relative),
        grid_spec=pltpu.PrefetchScalarGridSpec(
            num_scalar_prefetch=1,
            grid=(CHUNKS,),
            in_specs=[
                pl.BlockSpec((length, width), same),
                pl.BlockSpec(pieces.shape[:2] + (None,) + pieces.shape[3:], lambda p, m: (0, 0, p, 0, 0)),
                pl.BlockSpec((length, 1), same),
                pl.BlockSpec((2, SLAB, keep), lambda p, m: (p + CHUNKS * ((side + m[0]) % 2), 0, 0)),
            ],
            out_specs=[
                pl.BlockSpec((1, length, TRIPLE), turn),
                pl.BlockSpec((1, length, PAIR), turn),
                pl.BlockSpec((1, 2, length), turn),
                pl.BlockSpec((1, width, TRIPLE), turn),
            ],
        ),
        out_shape=[
            in_hbm((CHUNKS, length, TRIPLE), jnp.bfloat16),
            in_hbm((CHUNKS, length, PAIR), jnp.bfloat16),
            in_hbm((CHUNKS, 2, length), jnp.float32),
            in_hbm((CHUNKS, width, TRIPLE), jnp.bfloat16),
        ],
        compiler_params=pltpu.CompilerParams(vmem_limit_bytes=48 * MIB),
        cost_estimate=pl.CostEstimate(
            flops=24 * length * length * HEAD_DIM * 2,
            bytes_accessed=3 * length * (width + 2 * TRIPLE) + 6 * SLAB * keep * 4,
            transcendentals=6 * length * length,
        ),
        name="attend_forward",
    )(meta, *from_hbm(normed), pieces, *from_hbm(ends, table))


def backward_kernel(
    relative, chunk, meta_ref, qkv_ref, out_ref, grad_ref, ends_ref, log_ref, table_ref, turned_ref, matrix_ref,
    dqkv_ref, weight_ref, diag_ref, gain_ref,
    qm, gm, kt, dq_acc, skewed, delta, summed, turned, matrix, sems,
):
    fetches = [
        pltpu.make_async_copy(turned_ref, turned, sems.at[0]),
        pltpu.make_async_copy(matrix_ref.at[chunk], matrix, sems.at[1]),
    ]
    for fetch in fetches:
        fetch.start()
    length = qkv_ref.shape[1]
    tiles = length // TILE
    left = lax.broadcasted_iota(jnp.int32, (length, PAIR), 1) < HEAD_DIM
    query, grads = qkv_ref[0, :, :PAIR], grad_ref[0, 0]
    zero = jnp.zeros_like(query)
    for k in range(2):
        pick = left if k == 0 else jnp.logical_not(left)
        qm[k] = jnp.where(pick, query, zero)
        gm[k] = jnp.where(pick, grads, zero)
    kt[...] = qkv_ref[0, :, PAIR : 2 * PAIR].T
    dq_acc[...] = jnp.zeros_like(dq_acc)
    skewed[...] = jnp.zeros_like(skewed)
    product = wide(grads) * wide(out_ref[0])
    high = low(product)
    rest = low(product - wide(high))
    lane = lax.broadcasted_iota(jnp.int32, (16, PAIR), 1)
    row = lax.broadcasted_iota(jnp.int32, (16, PAIR), 0)
    chooser = low(jnp.where(lane // HEAD_DIM == row, 1.0, 0.0))
    delta[...] = nt(chooser, high) + nt(chooser, rest)

    def block(kb, n):
        kf = pl.multiple_of(kb * TILE, TILE)
        span = n * SLAB
        qf = length - span
        offset = pl.multiple_of((tiles - 1 - kb) * TILE + qf + SLAB, SLAB)
        before = pl.multiple_of(offset - SLAB, SLAB)
        rows = lax.broadcasted_iota(jnp.int32, (TILE, span), 0) + kf
        allowed = rows < ends_ref[:, qf:]
        k_tile = qkv_ref[0, pl.ds(kf, TILE), PAIR : 2 * PAIR]
        v_tile = qkv_ref[0, pl.ds(kf, TILE), 2 * PAIR :]
        dk = jnp.zeros((TILE, PAIR), jnp.float32)
        dv = jnp.zeros((TILE, PAIR), jnp.float32)
        for k in range(2):
            q_part = qm[k, qf:, :]
            g_part = gm[k, qf:, :]
            bias = jnp.concatenate(
                [table_ref[k, :, pl.ds(offset, span)], table_ref[k, :, pl.ds(before, span)]], axis=0
            )
            scores = nt(k_tile, q_part) + bias - log_ref[0, k : k + 1, qf:]
            probs = jnp.where(allowed, jnp.exp(scores), 0.0)
            above = nt(v_tile, g_part) - delta[k : k + 1, qf:]
            grad = probs * above
            skewed[k, :, pl.ds(offset, span)] += grad[:SLAB]
            skewed[k, :, pl.ds(before, span)] += grad[SLAB:]
            grad_low = low(grad)
            dv = dv + nn(low(probs), g_part)
            dk = dk + nn(grad_low, q_part)
            head = slice(k * HEAD_DIM, (k + 1) * HEAD_DIM)
            dq_acc[head, qf:] += nn(kt[head, pl.ds(kf, TILE)], grad_low)
        dqkv_ref[pl.ds(kf, TILE), PAIR : 2 * PAIR] = low(dk)
        dqkv_ref[pl.ds(kf, TILE), 2 * PAIR :] = low(dv)

    def step(kb, carry):
        count = meta_ref[3 + tiles + kb]
        for n in range(TILE // SLAB, length // SLAB + 1):
            @pl.when(count == n)
            def _():
                block(kb, n)
        return carry

    lax.fori_loop(0, tiles, step, 0)
    dqkv_ref[:, :PAIR] = low(dq_acc[...].T)
    for fetch in fetches:
        fetch.wait()
    exact = nn(turned[...], dqkv_ref[...])
    summed[...] = low(exact)
    by_row = jnp.sum(exact * wide(matrix[...]), axis=1, keepdims=True)
    gain_ref[...] = jnp.broadcast_to(by_row, (by_row.shape[0], SLAB)).T[0:1, :]
    inner, outer, rows, _ = weight_ref.shape
    for m in range(inner):
        for k in range(outer):
            weight_ref[m, k] = summed[row_span(relative, shard_at(relative, meta_ref, m, k), rows), :]

    group = lax.broadcasted_iota(jnp.int32, (8, skewed.shape[-1]), 0)
    for k in range(2):
        held = skewed[k, SLAB - 8 :, :]
        for a in range(SLAB // 8 - 1):
            held = held + pltpu.roll(skewed[k, a * 8 : (a + 1) * 8, :], SLAB - 8 * (a + 1), 1)
        for bit in (1, 2, 4):
            held = jnp.where(((7 - group) & bit) != 0, pltpu.roll(held, bit, 1), held)
        diag_ref[k : k + 1, :] = jnp.sum(held, axis=0, keepdims=True)


def attend_backward(chunk, side, relative, shards, meta, qkv, out, grad, ends, logs, table, turned, matrices):
    length = qkv.shape[1]
    width = turned.shape[0]
    keep = table.shape[-1]
    lanes = 2 * length
    turn = lambda i, m: (chunk, 0, 0)
    same = lambda i, m: (0, 0)
    piece = (INNER, shards // INNER, width // shards, TRIPLE)
    return pl.pallas_call(
        functools.partial(backward_kernel, relative, chunk),
        grid_spec=pltpu.PrefetchScalarGridSpec(
            num_scalar_prefetch=1,
            grid=(1,),
            in_specs=[
                pl.BlockSpec((1, length, TRIPLE), turn),
                pl.BlockSpec((1, length, PAIR), turn),
                pl.BlockSpec((1, 1, length, PAIR), lambda i, m: (chunk, side, 0, 0)),
                pl.BlockSpec((1, length), same),
                pl.BlockSpec((1, 2, length), turn),
                pl.BlockSpec((2, SLAB, keep), lambda i, m: (chunk + CHUNKS * ((side + m[0]) % 2), 0, 0)),
                pl.BlockSpec(memory_space=pl.ANY),
                pl.BlockSpec(memory_space=pl.ANY),
            ],
            out_specs=[
                pl.BlockSpec((length, TRIPLE), same),
                pl.BlockSpec(piece, lambda i, m: (0, 0, 0, 0)),
                pl.BlockSpec((2, lanes), same),
                pl.BlockSpec((1, width), same),
            ],
            scratch_shapes=[
                pltpu.VMEM((2, length, PAIR), jnp.bfloat16),
                pltpu.VMEM((2, length, PAIR), jnp.bfloat16),
                pltpu.VMEM((PAIR, length), jnp.bfloat16),
                pltpu.VMEM((PAIR, length), jnp.float32),
                pltpu.VMEM((2, SLAB, lanes), jnp.float32),
                pltpu.VMEM((16, length), jnp.float32),
                pltpu.VMEM((width, TRIPLE), jnp.bfloat16),
                pltpu.VMEM((width, length), jnp.bfloat16),
                pltpu.VMEM((width, TRIPLE), jnp.bfloat16),
                pltpu.SemaphoreType.DMA((2,)),
            ],
        ),
        out_shape=[
            in_hbm((length, TRIPLE), jnp.bfloat16),
            in_hbm(piece, jnp.bfloat16),
            in_hbm((2, lanes), jnp.float32),
            in_hbm((1, width), jnp.float32),
        ],
        compiler_params=pltpu.CompilerParams(vmem_limit_bytes=40 * MIB),
        cost_estimate=pl.CostEstimate(
            flops=1, bytes_accessed=1, transcendentals=0
        ),
        name="attend_backward",
    )(meta, *from_hbm(qkv, out, grad), ends, logs, *from_hbm(table, turned, matrices))


def feed_kernel(
    meta_ref, x_ref, cot_ref, own_att_ref, other_att_ref, gain_ref, mix_ref, up0_ref, up1_ref, down_ref,
    out_ref, sgrad_ref, agrad_ref, later_ref, rest_ref, own_ref, other_ref,
    state, scale, normed, turned, total, upstream, act, pre, mixing, attended, branch, up, down,
):
    block = pl.program_id(0)
    blocks = pl.num_programs(0)
    me = meta_ref[0]
    length, width = x_ref.shape
    half = width // 2
    shards, _, rows, _ = mix_ref.shape
    count = length // ROWS

    @pl.when(block == 0)
    def _():
        for c in range(2):
            mixing[:, c * half : (c + 1) * half] = mix_ref[:, c].reshape(width, half)
        for p, ref in enumerate((own_att_ref, other_att_ref)):
            for i in range(CHUNKS):
                spot = pl.multiple_of((i + CHUNKS * ((p + me) % 2)) * PAIR, PAIR)
                attended[:, pl.ds(spot, PAIR)] = ref[i]

        def start(n, carry):
            spot = pl.ds(pl.multiple_of(n * ROWS, ROWS), ROWS)
            held = wide(x_ref[spot, :]) + nn(attended[spot, :], mixing[...])
            state[spot, :] = held
            found = lax.rsqrt(jnp.mean(held * held, axis=1, keepdims=True) + EPS)
            scale[spot, :] = jnp.broadcast_to(found, (ROWS, SLAB))
            normed[spot, :] = low(held * found * gain_ref[...])
            return carry

        lax.fori_loop(0, count, start, 0)
        turned[...] = normed[...].T
        total[...] = jnp.zeros_like(total)
        upstream[...] = jnp.zeros_like(upstream)

    for c, ref in enumerate((up0_ref, up1_ref)):
        up[:, c * half : (c + 1) * half] = ref[...].reshape(width, half)
        down[:, c * half : (c + 1) * half] = down_ref[:, c].reshape(width, half)

    def middle(n, carry):
        spot = pl.ds(n * ROWS, ROWS)
        v = nn(normed[spot, :], up[...])
        square = v * v
        bent = jnp.tanh(v * (CURVE + (CURVE * CUBE) * square))
        gate = 0.5 + 0.5 * bent
        slope = gate + (0.5 * v) * (1.0 - bent * bent) * (CURVE + (3 * CURVE * CUBE) * square)
        active = low(v * gate)
        act[spot, :] = active
        total[spot, :] += nn(active, down[...])
        changed = low(nt(cot_ref[spot, :], down[...]) * slope)
        pre[spot, :] = changed
        upstream[spot, :] += nt(changed, up[...])
        return carry

    for n in range(count):
        middle(n, 0)
    long = down_ref.shape[2]
    per = width // long
    steps = blocks // 2

    def halves(values):
        left, right = values[:, :half], values[:, half:]
        first = me == 0
        return jnp.where(first, left, right), jnp.where(first, right, left)

    kept, sent = halves(low(tn(act[...], cot_ref[...])))
    for s in range(per):
        own_ref[s % INNER, s // INNER] = kept[s * long : (s + 1) * long]
        other_ref[s % INNER, s // INNER] = sent[s * long : (s + 1) * long]
    dup = low(nn(turned[...], pre[...]))
    for c in range(2):
        start = pl.multiple_of(rows + (block % steps * 2 + c) * rows, rows)
        for s in range(shards):
            rest_ref[s, block // steps, pl.ds(start, rows)] = dup[
                s * rows : (s + 1) * rows, c * half : (c + 1) * half
            ]

    @pl.when(block == blocks - 1)
    def _():
        gain = gain_ref[...]

        def finish(n, parts):
            spot = pl.ds(pl.multiple_of(n * ROWS, ROWS), ROWS)
            held = state[spot, :]
            found = scale[spot, :][:, :1]
            out_ref[spot, :] = low(held + total[spot, :])
            grads = upstream[spot, :]
            parts = parts + jnp.sum(grads * held * found, axis=0, keepdims=True)
            scaled = grads * gain
            mean = jnp.mean(scaled * held, axis=1, keepdims=True)
            result = wide(cot_ref[spot, :]) + found * (scaled - held * (found * found * mean))
            sgrad_ref[spot, :] = result
            rounded = low(result)
            branch[spot, :] = rounded
            back = low(nt(rounded, mixing[...]))
            for pair in range(width // PAIR):
                agrad_ref[pair % CHUNKS, (pair // CHUNKS + me) % 2, spot, :] = back[
                    :, pair * PAIR : (pair + 1) * PAIR
                ]
            return parts

        later_ref[...] = lax.fori_loop(0, count, finish, jnp.zeros((1, width), jnp.float32))
        dmix = low(tn(attended[...], branch[...]))
        for s in range(shards):
            for c in range(2):
                rest_ref[s, c, :rows] = dmix[s * rows : (s + 1) * rows, c * half : (c + 1) * half]


def feed_forward(relative, meta, inputs, cotangent, attended, gain, gathered):
    length, width = inputs.shape
    half = width // 2
    shards, _, every, _ = gathered.shape
    rows = width // shards
    groups = (every - rows) // (2 * rows)
    long = groups * rows
    per = width // long
    steps = groups // 2
    blocks = 2 * steps
    same = lambda b, m: (0, 0)
    full = pl.BlockSpec((length, width), same)
    down_piece = pl.BlockSpec(
        (INNER, per // INNER, long, half), lambda b, m: (0, b ^ m[2] if relative else b, 0, 0)
    )
    pair = pl.BlockSpec((CHUNKS, length, PAIR), lambda b, m: (0, 0, 0))
    return pl.pallas_call(
        feed_kernel,
        grid_spec=pltpu.PrefetchScalarGridSpec(
            num_scalar_prefetch=1,
            grid=(blocks,),
            in_specs=[
                full, full, pair, pair,
                pl.BlockSpec((1, width), same),
                pl.BlockSpec((shards, 2, rows, half), lambda b, m: (0, 0, groups, 0)),
                pl.BlockSpec((shards, 1, rows, half), lambda b, m: (0, b // steps, groups + 1 + 2 * (b % steps), 0)),
                pl.BlockSpec((shards, 1, rows, half), lambda b, m: (0, b // steps, groups + 2 + 2 * (b % steps), 0)),
                pl.BlockSpec((per, 2, long, half), lambda b, m: (b, 0, 0, 0)),
            ],
            out_specs=[
                full, full,
                pl.BlockSpec((CHUNKS, 2, length, PAIR), lambda b, m: (0, 0, 0, 0)),
                pl.BlockSpec((1, width), same),
                pl.BlockSpec((shards, 2, every - long, half), lambda b, m: (0, 0, 0, 0)),
                down_piece,
                down_piece,
            ],
            scratch_shapes=[
                pltpu.VMEM((length, width), jnp.float32),
                pltpu.VMEM((length, SLAB), jnp.float32),
                pltpu.VMEM((length, width), jnp.bfloat16),
                pltpu.VMEM((width, length), jnp.bfloat16),
                pltpu.VMEM((length, width), jnp.float32),
                pltpu.VMEM((length, width), jnp.float32),
                pltpu.VMEM((length, width), jnp.bfloat16),
                pltpu.VMEM((length, width), jnp.bfloat16),
                pltpu.VMEM((width, width), jnp.bfloat16),
                pltpu.VMEM((length, width), jnp.bfloat16),
                pltpu.VMEM((length, width), jnp.bfloat16),
                pltpu.VMEM((width, width), jnp.bfloat16),
                pltpu.VMEM((width, width), jnp.bfloat16),
            ],
        ),
        out_shape=[
            in_hbm((length, width), jnp.bfloat16),
            in_hbm((length, width), jnp.float32),
            in_hbm((CHUNKS, 2, length, PAIR), jnp.bfloat16),
            in_hbm((1, width), jnp.float32),
            in_hbm((shards, 2, every - long, half), jnp.bfloat16),
            in_hbm((INNER, shards // INNER, long, half), jnp.bfloat16),
            in_hbm((INNER, shards // INNER, long, half), jnp.bfloat16),
        ],
        compiler_params=pltpu.CompilerParams(vmem_limit_bytes=60 * MIB),
        cost_estimate=pl.CostEstimate(
            flops=12 * length * width * width * blocks + 6 * length * width * width,
            bytes_accessed=14 * length * width + 8 * width * width * blocks,
            transcendentals=length * width * blocks,
        ),
        name="feed_forward",
    )(meta, inputs, cotangent, *attended, gain.reshape(1, width), *[gathered] * 4)


def last_kernel(x_ref, scale_ref, gain_ref, sgrad_ref, *refs):
    grads, weights = refs[: 2 * CHUNKS], refs[2 * CHUNKS : 2 * CHUNKS + 2]
    out_ref = refs[2 * CHUNKS + 2]
    x = wide(x_ref[...])
    found = scale_ref[...]
    upstream = jnp.zeros(x.shape, jnp.float32)
    for i in range(CHUNKS):
        for side in range(2):
            upstream = upstream + nt(grads[2 * i + side][...], weights[side][i])
    scaled = upstream * gain_ref[...]
    mean = jnp.mean(scaled * x, axis=1, keepdims=True)
    out_ref[...] = low(sgrad_ref[...] + found * (scaled - x * (found * found * mean)))


def last(inputs, scale, gain, state_grad, grads, weights):
    length, width = inputs.shape
    step = lambda i: (i, 0)
    same = lambda i: (0, 0)
    return pl.pallas_call(
        last_kernel,
        grid=(length // ROWS,),
        in_specs=[
            pl.BlockSpec((ROWS, width), step),
            pl.BlockSpec((ROWS, 1), step),
            pl.BlockSpec((1, width), same),
            pl.BlockSpec((ROWS, width), step),
        ]
        + [pl.BlockSpec((ROWS, TRIPLE), step)] * (2 * CHUNKS)
        + [pl.BlockSpec((CHUNKS, width, TRIPLE), lambda i: (0, 0, 0))] * 2,
        out_specs=pl.BlockSpec((ROWS, width), step),
        out_shape=in_hbm((length, width), jnp.bfloat16),
        compiler_params=pltpu.CompilerParams(vmem_limit_bytes=48 * MIB),
        cost_estimate=pl.CostEstimate(
            flops=1, bytes_accessed=1, transcendentals=0
        ),
        name="last",
    )(inputs, scale, gain.reshape(1, width), state_grad, *from_hbm(*grads, *weights))


def swap(values):
    return lax.ppermute(values, "replica", [(0, 1), (1, 0)])


def shift(values, shards, distance):
    return lax.ppermute(values, "shard", [(i, i ^ distance) for i in range(shards)])


def tie(values, *before):
    return lax.optimization_barrier((values,) + before)[0]


def gather_relative(own, shards, *before):
    line = jnp.stack([own] + [shift(own, shards, k * INNER) for k in range(1, shards // INNER)])
    came = [shift(line, shards, m) for m in range(1, INNER)]
    return jnp.stack([line] + [tie(c, *before) for c in came])


def cross(own, came):
    return [low(wide(own[m]) + wide(came[m])) for m in range(INNER)]


def plane(places, shards):
    return [places[0]] + [shift(places[m], shards, m) for m in range(1, INNER)]


def column(line, shards):
    return [line[0]] + [shift(line[k], shards, k * INNER) for k in range(1, shards // INNER)]


def total_of(parts):
    total = wide(parts[0])
    for part in parts[1:]:
        total = total + wide(part)
    return total


def exchange(pieces, groups):
    return lax.all_to_all(pieces, "shard", 0, 0, axis_index_groups=groups)


def inner_groups(shards):
    return [[o * INNER + i for i in range(INNER)] for o in range(shards // INNER)]


def natural_halves(own):
    other = swap(own)
    first = lax.axis_index("replica") == 0
    return jnp.where(first, own, other), jnp.where(first, other, own)


def scatter_halves(own, other):
    halves = []
    for part in (own, other):
        whole = jnp.swapaxes(part, 0, 1).reshape((-1,) + part.shape[2:])
        halves.append(wide(lax.psum_scatter(whole, "shard", scatter_dimension=0, tiled=True))[0])
    return lax.psum(tuple(halves), "replica")


def body(
    copies,
    shards,
    inputs,
    cotangent,
    block_ids,
    buckets,
    early_gain,
    query_weight,
    key_weight,
    value_weight,
    mixing_weight,
    relative_table,
    later_gain,
    up_weight,
    down_weight,
):
    length, width = inputs.shape
    half = width // 2
    hidden = up_weight.shape[1]
    bucket_count, heads = relative_table.shape
    offsets = buckets.shape[0]
    relative = copies == 2 and width // shards % 16 == 0 and INNER * hidden == shards * width
    me = lax.axis_index("replica") if relative else jnp.int32(0)
    spot = lax.axis_index("shard") if relative else jnp.int32(0)

    def parts_of(h):
        column = lambda w, c: lax.dynamic_slice_in_dim(w, c, half, 1)
        groups = up_weight.shape[1] // width
        return jnp.concatenate(
            [column(down_weight, h * half), column(mixing_weight, h * half)]
            + [column(up_weight, (h * groups + j) * half) for j in range(groups)],
            axis=0,
        )

    def triples_of(h):
        weights = (query_weight, key_weight, value_weight)
        starts = [(chunk + CHUNKS * h) * PAIR for chunk in range(CHUNKS)]
        return jnp.stack(
            [
                jnp.concatenate([lax.dynamic_slice_in_dim(w, at, PAIR, 1) for w in weights], axis=1)
                for at in starts
            ]
        )

    outer = shards // INNER
    if relative:
        gathered = lax.all_gather(parts_of(me), ("shard", "replica"), axis=0, tiled=True)
    else:
        gathered = lax.all_gather(jnp.stack([parts_of(0), parts_of(1)]), "shard", axis=0, tiled=True)
    gathered = gathered.reshape(shards, 2, -1, half)

    normed, turned, early_scale, across, upright = prepare(inputs, early_gain, block_ids)
    tiles = length // TILE
    final = across.reshape(length // SLAB, SLAB)[:, SLAB - 1]
    counts = (final[TILE // SLAB - 1 :: TILE // SLAB] + SLAB - 1) // SLAB
    starts = jnp.arange(tiles, dtype=jnp.int32) * TILE
    uses = jnp.sum((starts[:, None] < final[None, :]).astype(jnp.int32), axis=1)
    place_of = jnp.stack([me, spot % INNER, spot // INNER])
    meta = jnp.concatenate([place_of, counts, uses]).astype(jnp.int32)

    onehot = (buckets[:, None] == jnp.arange(bucket_count, dtype=jnp.int32)[None, :]).astype(jnp.float32)
    mirrored = (buckets[::-1][:, None] == jnp.arange(bucket_count, dtype=jnp.int32)[None, :]).astype(jnp.float32)
    spare = ((0, 0), (0, 2 * length - offsets))
    forward_table, backward_table = [
        skew(jnp.pad(jnp.dot(hot, relative_table, precision=HIGH).T, spare), length) for hot in (onehot, mirrored)
    ]

    def natural(values):
        every = lax.all_gather(values, "shard", axis=0)
        return jnp.swapaxes(every.reshape((outer, INNER) + values.shape), 0, 1)

    if relative:
        own = gather_relative(triples_of(me), shards, forward_table, backward_table, normed, turned, upright, meta)
        other = swap(own)
    else:
        own, other = natural(triples_of(0)), natural(triples_of(1))

    held = [attend_forward(0, relative, meta, normed, own, upright, forward_table)]
    other = tie(other, held[0][2])
    held.append(attend_forward(1, relative, meta, normed, other, upright, forward_table))
    layer_output, state_grad, attended_grad, later_part, rest, down_own, down_other = feed_forward(
        relative, meta, inputs, cotangent, [h[1] for h in held], later_gain, gathered
    )

    grads, diagonals, gains = {}, {}, {}

    def backward(c, side, *before):
        qkv, attended, logs, matrices = held[side]
        grad = tie(attended_grad, *before) if before else attended_grad
        grads[c, side], weight, diagonals[c, side], gains[c, side] = attend_backward(
            c, side, relative, shards, meta, qkv, attended, grad, across, logs, backward_table, turned,
            matrices,
        )
        return weight, diagonals[c, side]

    def finish(*before):
        scale = tie(early_scale, *before) if before else early_scale
        ordered = [grads[c, side] for c in range(CHUNKS) for side in range(2)]
        return last(inputs, scale, early_gain, state_grad, ordered, [h[3] for h in held])

    rows = width // shards

    def vector_of():
        early_part = sum(gains.values()).reshape(-1) / early_gain
        sides = [jnp.concatenate([diagonals[c, side] for c in range(CHUNKS)], axis=0) for side in range(2)]
        first = me == 0
        stacked = jnp.concatenate([jnp.where(first, *sides), jnp.where(first, *sides[::-1])], axis=0)[:, :offsets]
        table_part = lax.dot_general(mirrored, stacked, (((0,), (1,)), ((), ())), precision=HIGH)
        return jnp.concatenate([early_part, later_part.reshape(-1), table_part.reshape(-1)])

    def small_sums():
        vector = vector_of()
        vector = jnp.pad(vector, (0, SMALL * half - vector.shape[0])).reshape(SMALL, half)
        high = low(vector)
        return jnp.concatenate([high, low(vector - wide(high))], axis=0)

    def halve(sums):
        vector = sums[:, :SMALL] + sums[:, SMALL:]
        high = low(vector)
        return jnp.concatenate([high, low(vector - wide(high))], axis=1)

    if relative:
        share = lax.psum_scatter(
            rest.reshape((2 * shards,) + rest.shape[2:]), ("shard", "replica"), scatter_dimension=0, tiled=True
        )[0]
        down_came = swap(down_other)
        other, done = backward(0, 1)
        came = swap(other)
        down_came = tie(down_came, done)
        down_pieces = exchange(
            low(wide(down_own) + wide(down_came)), inner_groups(shards)
        )
        own, done = backward(0, 0, done, down_came)
        places = cross(own, tie(came, done))
        plane0 = plane(places, shards)
        other, done = backward(1, 1, done, *places)
        came1 = swap(other)
        own1, done = backward(1, 0, done)
        down_line = low(jnp.sum(wide(tie(down_pieces, done)), axis=0))
        line0 = low(total_of([tie(p, done) for p in plane0]))
        early = jnp.concatenate([down_line, line0], axis=1)
        lines = lax.optimization_barrier(([early[k] for k in range(early.shape[0])], done))
        early_column = column(lines[0], shards)
        other, done = backward(2, 1, *lines[0], lines[1])
        came1 = tie(came1, done)
        came2 = swap(other)
        own2, done = backward(2, 0, done)
        came2 = tie(came2, done)
        places = [jnp.concatenate(p, axis=1) for p in zip(cross(own1, came1), cross(own2, came2), strict=True)]
        small = small_sums()
        late = [jnp.concatenate([p, jnp.broadcast_to(small, p.shape[:1] + small.shape)], axis=1) for p in places]
        late_plane = plane(late, shards)
        early = total_of([tie(p, done) for p in early_column])
        input_gradient = finish(*late, early)
        late = wide(late[0])
        for p in late_plane[1:]:
            late = late + wide(tie(p, input_gradient))
        late = jnp.concatenate([low(late[:, : 2 * rows]), halve(late[:, 2 * rows :])], axis=1)
        late = natural_halves(total_of(column(late, shards)))
        early = natural_halves(early)
        share = [wide(h) for h in natural_halves(tie(share, input_gradient))]
        small = late[0][2 * rows :] + late[1][2 * rows :]
        small = (small[:SMALL] + small[SMALL:]).reshape(-1)
        down_share = [h[:-rows] for h in early]
        shares = [[h[-rows:] for h in early], [h[:rows] for h in late], [h[rows : 2 * rows] for h in late]]
    else:
        shares = []
        for c in range(CHUNKS):
            other, _ = backward(c, 1)
            own, _ = backward(c, 0)
            shares.append(scatter_halves(own, other))
        input_gradient = finish()
        both = lax.psum_scatter(rest, "shard", scatter_dimension=0, tiled=True)[0]
        share = lax.psum((wide(both[0]), wide(both[1])), "replica")
        down_share = [
            lax.psum(
                wide(
                    lax.psum_scatter(
                        jnp.swapaxes(d, 0, 1).reshape((shards,) + d.shape[2:]), "shard", scatter_dimension=0, tiled=True
                    )
                )[0],
                "replica",
            )
            for d in (down_own, down_other)
        ]
        small = lax.psum(vector_of(), ("replica", "shard"))

    early_total, later_total = small[:width], small[width : 2 * width]
    table_total = small[2 * width : 2 * width + relative_table.size].reshape(bucket_count, heads)

    groups = hidden // width
    down_share = jnp.concatenate(down_share, axis=1)
    mixing_share = jnp.concatenate([share[0][:rows], share[1][:rows]], axis=1)
    up_share = jnp.concatenate(
        [share[h][rows * (1 + j) : rows * (2 + j)] for h in range(2) for j in range(groups)], axis=1
    )
    triples = [
        jnp.concatenate(
            [shares[c][h][:, n * PAIR : (n + 1) * PAIR] for h in range(2) for c in range(CHUNKS)], axis=1
        )
        for n in range(3)
    ]
    return (
        layer_output,
        input_gradient,
        early_total,
        triples[0],
        triples[1],
        triples[2],
        mixing_share,
        table_total,
        later_total,
        up_share,
        down_share,
    )


def solution(mesh):
    rows = P(("replica", "shard"), None)
    split = P("shard", None)
    same = P()
    return jax.shard_map(
        functools.partial(body, mesh.shape["replica"], mesh.shape["shard"]),
        mesh=mesh,
        in_specs=(rows, rows, rows, same, same, split, split, split, split, same, same, split, split),
        out_specs=(rows, rows, same, split, split, split, split, same, same, split, split),
        check_vma=False,
    )
```

```python
import functools
import math

import jax
import jax.numpy as jnp
from jax import lax
from jax.experimental import pallas as pl
from jax.experimental.pallas import tpu as pltpu
from jax.sharding import PartitionSpec as P

EPS = 1e-06
HIGH = lax.Precision.HIGHEST
HEAD_DIM = 64
PAIR = 2 * HEAD_DIM
TRIPLE = 3 * PAIR
SLAB = 128
TILE = 256
CHUNKS = 3
INNER = 4
ROWS = 512
SMALL = 8
NEG = -1e30
CURVE = math.sqrt(2 / math.pi)
CUBE = 0.044715
MIB = 1 << 20


def nt(left, right):
    return lax.dot_general(left, right, (((1,), (1,)), ((), ())), preferred_element_type=jnp.float32)


def nn(left, right):
    return lax.dot_general(left, right, (((1,), (0,)), ((), ())), preferred_element_type=jnp.float32)


def tn(left, right):
    return lax.dot_general(left, right, (((0,), (0,)), ((), ())), preferred_element_type=jnp.float32)


def low(values):
    return values.astype(jnp.bfloat16)


def wide(values):
    return values.astype(jnp.float32)


def in_hbm(shape, dtype):
    return pltpu.HBM(shape, dtype)


def from_hbm(*arrays):
    return [pltpu.with_memory_space_constraint(a, pltpu.HBM) for a in arrays]


def skew_kernel(rows_ref, out_ref):
    width = rows_ref.shape[-1]
    keep = out_ref.shape[-1]
    for k in range(rows_ref.shape[0]):
        spread = jnp.broadcast_to(rows_ref[k], (SLAB, width))
        moved = pltpu.roll(spread, width - SLAB + 1, 1, stride=1, stride_axis=0)
        out_ref[k] = moved[:, :keep]


def skew(rows, length):
    count, width = rows.shape
    keep = 2 * length - SLAB
    return pl.pallas_call(
        skew_kernel,
        grid=(count // 2,),
        in_specs=[pl.BlockSpec((2, 1, width), lambda i: (i, 0, 0))],
        out_specs=pl.BlockSpec((2, SLAB, keep), lambda i: (i, 0, 0)),
        out_shape=in_hbm((count, SLAB, keep), jnp.float32),
        compiler_params=pltpu.CompilerParams(vmem_limit_bytes=32 * MIB),
        cost_estimate=pl.CostEstimate(
            flops=count * SLAB * width, bytes_accessed=count * SLAB * keep * 4, transcendentals=0
        ),
        name="skew",
    )(rows.reshape(count, 1, width))


def pack_kernel(place_ref, query_ref, key_ref, value_ref, mix_ref, up_ref, down_ref, feed_ref, triple_ref):
    me = place_ref[0]
    long, half = down_ref.shape[0], feed_ref.shape[1]
    rows = mix_ref.shape[0]
    groups = up_ref.shape[1] // (2 * half)
    span = lambda n, size: pl.ds(pl.multiple_of(n * size, SLAB), size)
    feed_ref[:long] = down_ref[:, span(me, half)]
    feed_ref[long : long + rows] = mix_ref[:, span(me, half)]
    for j in range(groups):
        feed_ref[long + rows * (1 + j) : long + rows * (2 + j)] = up_ref[:, span(me * groups + j, half)]
    for chunk in range(CHUNKS):
        for n, ref in enumerate((query_ref, key_ref, value_ref)):
            triple_ref[chunk, :, n * PAIR : (n + 1) * PAIR] = ref[:, span(chunk + CHUNKS * me, PAIR)]


def pack(place, query, key, value, mix, up, down):
    rows, width = mix.shape
    half = width // 2
    long = down.shape[0]
    every = long + rows + rows * (up.shape[1] // width)
    whole = lambda a: pl.BlockSpec(a.shape, lambda i, m: (0, 0))
    arrays = (query, key, value, mix, up, down)
    return pl.pallas_call(
        pack_kernel,
        grid_spec=pltpu.PrefetchScalarGridSpec(
            num_scalar_prefetch=1,
            grid=(1,),
            in_specs=[whole(a) for a in arrays],
            out_specs=[
                pl.BlockSpec((every, half), lambda i, m: (0, 0)),
                pl.BlockSpec((CHUNKS, rows, TRIPLE), lambda i, m: (0, 0, 0)),
            ],
        ),
        out_shape=[in_hbm((every, half), jnp.bfloat16), in_hbm((CHUNKS, rows, TRIPLE), jnp.bfloat16)],
        cost_estimate=pl.CostEstimate(flops=1, bytes_accessed=1, transcendentals=0),
        compiler_params=pltpu.CompilerParams(vmem_limit_bytes=16 * MIB),
        name="pack",
    )(place, *from_hbm(*arrays))


def prepare_kernel(x_ref, gain_ref, row_ref, column_ref, normed_ref, turned_ref, scale_ref, across_ref, upright_ref):
    length = x_ref.shape[0]
    ids = row_ref[...]

    def part(n, ends):
        spot = pl.ds(pl.multiple_of(n * TILE, TILE), TILE)
        x = wide(x_ref[spot, :])
        found = lax.rsqrt(jnp.mean(x * x, axis=1, keepdims=True) + EPS)
        scale_ref[spot, :] = found
        normed_ref[spot, :] = low(x * found * gain_ref[...])
        mine = column_ref[spot, :]
        upright_ref[spot, :] = jnp.sum(jnp.where(ids <= mine, 1, 0), axis=1, keepdims=True)
        return ends + jnp.sum(jnp.where(mine <= ids, 1, 0), axis=0, keepdims=True)

    across_ref[...] = lax.fori_loop(0, length // TILE, part, jnp.zeros((1, length), jnp.int32))
    turned_ref[...] = normed_ref[...].T


def prepare(inputs, gain, ids):
    length, width = inputs.shape
    return pl.pallas_call(
        prepare_kernel,
        out_shape=[
            in_hbm((length, width), jnp.bfloat16),
            in_hbm((width, length), jnp.bfloat16),
            in_hbm((length, 1), jnp.float32),
            in_hbm((1, length), jnp.int32),
            in_hbm((length, 1), jnp.int32),
        ],
        compiler_params=pltpu.CompilerParams(vmem_limit_bytes=32 * MIB),
        cost_estimate=pl.CostEstimate(flops=1, bytes_accessed=1, transcendentals=0),
        name="prepare",
    )(inputs, gain.reshape(1, width), ids.reshape(1, length), ids.reshape(length, 1))


def shard_at(relative, meta_ref, m, k):
    return (meta_ref[2] ^ k) * INNER + (meta_ref[1] ^ m) if relative else k * INNER + m


def row_span(relative, shard, rows):
    return pl.ds(pl.multiple_of(shard * rows, 16) if relative else shard * rows, rows)


def forward_kernel(
    relative, meta_ref, normed_ref, pieces_ref, ends_ref, table_ref, qkv_ref, out_ref, log_ref, weight_ref
):
    length = normed_ref.shape[0]
    tiles = length // TILE
    inner, outer, rows, _ = pieces_ref.shape
    for m in range(inner):
        for k in range(outer):
            span = row_span(relative, shard_at(relative, meta_ref, m, k), rows)
            weight_ref[0, span, :] = pieces_ref[m, k]
    qkv_ref[0] = low(nn(normed_ref[...], weight_ref[0]))
    left = lax.broadcasted_iota(jnp.int32, (TILE, PAIR), 1) < HEAD_DIM

    def block(i, n):
        first = pl.multiple_of(i * TILE, TILE)
        query = qkv_ref[0, pl.ds(first, TILE), :PAIR]
        keys = qkv_ref[0, : n * SLAB, PAIR : 2 * PAIR]
        values = qkv_ref[0, : n * SLAB, 2 * PAIR :]
        ends = ends_ref[pl.ds(first, TILE), :]
        columns = lax.broadcasted_iota(jnp.int32, (TILE, n * SLAB), 1)
        allowed = columns < ends
        outs = []
        zero = jnp.zeros_like(query)
        offset = pl.multiple_of((tiles - 1 - i) * TILE + SLAB, SLAB)
        before = pl.multiple_of(offset - SLAB, SLAB)
        for k in range(2):
            mine = jnp.where(left, query, zero) if k == 0 else jnp.where(left, zero, query)
            bias = jnp.concatenate(
                [table_ref[k, :, pl.ds(offset, n * SLAB)], table_ref[k, :, pl.ds(before, n * SLAB)]], axis=0
            )
            scores = jnp.where(allowed, nt(mine, keys) + bias, NEG)
            peak = jnp.max(scores, axis=1, keepdims=True)
            weights = jnp.exp(scores - peak)
            total = jnp.sum(weights, axis=1, keepdims=True)
            outs.append(nn(low(weights), values) / total)
            logs = jnp.broadcast_to(peak + jnp.log(total), (TILE, SLAB))
            log_ref[0, k : k + 1, pl.ds(first, TILE)] = logs.T[0:1, :]
        out_ref[0, pl.ds(first, TILE), :] = low(jnp.where(left, outs[0], outs[1]))

    def step(i, carry):
        count = meta_ref[3 + i]
        for n in range(TILE // SLAB, length // SLAB + 1):
            @pl.when(count == n)
            def _():
                block(i, n)
        return carry

    lax.fori_loop(0, tiles, step, 0)


def attend_forward(side, relative, meta, normed, pieces, ends, table):
    length, width = normed.shape
    keep = table.shape[-1]
    turn = lambda p, m: (p, 0, 0)
    same = lambda p, m: (0, 0)
    return pl.pallas_call(
        functools.partial(forward_kernel, relative),
        grid_spec=pltpu.PrefetchScalarGridSpec(
            num_scalar_prefetch=1,
            grid=(CHUNKS,),
            in_specs=[
                pl.BlockSpec((length, width), same),
                pl.BlockSpec(pieces.shape[:2] + (None,) + pieces.shape[3:], lambda p, m: (0, 0, p, 0, 0)),
                pl.BlockSpec((length, 1), same),
                pl.BlockSpec((2, SLAB, keep), lambda p, m: (p + CHUNKS * ((side + m[0]) % 2), 0, 0)),
            ],
            out_specs=[
                pl.BlockSpec((1, length, TRIPLE), turn),
                pl.BlockSpec((1, length, PAIR), turn),
                pl.BlockSpec((1, 2, length), turn),
                pl.BlockSpec((1, width, TRIPLE), turn),
            ],
        ),
        out_shape=[
            in_hbm((CHUNKS, length, TRIPLE), jnp.bfloat16),
            in_hbm((CHUNKS, length, PAIR), jnp.bfloat16),
            in_hbm((CHUNKS, 2, length), jnp.float32),
            in_hbm((CHUNKS, width, TRIPLE), jnp.bfloat16),
        ],
        compiler_params=pltpu.CompilerParams(vmem_limit_bytes=48 * MIB),
        cost_estimate=pl.CostEstimate(
            flops=24 * length * length * HEAD_DIM * 2,
            bytes_accessed=3 * length * (width + 2 * TRIPLE) + 6 * SLAB * keep * 4,
            transcendentals=6 * length * length,
        ),
        name="attend_forward",
    )(meta, *from_hbm(normed), pieces, *from_hbm(ends, table))


def backward_kernel(
    relative, chunk, meta_ref, qkv_ref, out_ref, grad_ref, ends_ref, log_ref, table_ref, turned_ref, matrix_ref,
    dqkv_ref, weight_ref, diag_ref, gain_ref,
    qm, gm, kt, dq_acc, skewed, delta, summed, turned, matrix, sems,
):
    fetches = [
        pltpu.make_async_copy(turned_ref, turned, sems.at[0]),
        pltpu.make_async_copy(matrix_ref.at[chunk], matrix, sems.at[1]),
    ]
    for fetch in fetches:
        fetch.start()
    length = qkv_ref.shape[1]
    tiles = length // TILE
    left = lax.broadcasted_iota(jnp.int32, (length, PAIR), 1) < HEAD_DIM
    query, grads = qkv_ref[0, :, :PAIR], grad_ref[0, 0]
    zero = jnp.zeros_like(query)
    for k in range(2):
        pick = left if k == 0 else jnp.logical_not(left)
        qm[k] = jnp.where(pick, query, zero)
        gm[k] = jnp.where(pick, grads, zero)
    kt[...] = qkv_ref[0, :, PAIR : 2 * PAIR].T
    dq_acc[...] = jnp.zeros_like(dq_acc)
    skewed[...] = jnp.zeros_like(skewed)
    product = wide(grads) * wide(out_ref[0])
    high = low(product)
    rest = low(product - wide(high))
    lane = lax.broadcasted_iota(jnp.int32, (16, PAIR), 1)
    row = lax.broadcasted_iota(jnp.int32, (16, PAIR), 0)
    chooser = low(jnp.where(lane // HEAD_DIM == row, 1.0, 0.0))
    delta[...] = nt(chooser, high) + nt(chooser, rest)

    def block(kb, n):
        kf = pl.multiple_of(kb * TILE, TILE)
        span = n * SLAB
        qf = length - span
        offset = pl.multiple_of((tiles - 1 - kb) * TILE + qf + SLAB, SLAB)
        before = pl.multiple_of(offset - SLAB, SLAB)
        rows = lax.broadcasted_iota(jnp.int32, (TILE, span), 0) + kf
        allowed = rows < ends_ref[:, qf:]
        k_tile = qkv_ref[0, pl.ds(kf, TILE), PAIR : 2 * PAIR]
        v_tile = qkv_ref[0, pl.ds(kf, TILE), 2 * PAIR :]
        dk = jnp.zeros((TILE, PAIR), jnp.float32)
        dv = jnp.zeros((TILE, PAIR), jnp.float32)
        for k in range(2):
            q_part = qm[k, qf:, :]
            g_part = gm[k, qf:, :]
            bias = jnp.concatenate(
                [table_ref[k, :, pl.ds(offset, span)], table_ref[k, :, pl.ds(before, span)]], axis=0
            )
            scores = nt(k_tile, q_part) + bias - log_ref[0, k : k + 1, qf:]
            probs = jnp.where(allowed, jnp.exp(scores), 0.0)
            above = nt(v_tile, g_part) - delta[k : k + 1, qf:]
            grad = probs * above
            skewed[k, :, pl.ds(offset, span)] += grad[:SLAB]
            skewed[k, :, pl.ds(before, span)] += grad[SLAB:]
            grad_low = low(grad)
            dv = dv + nn(low(probs), g_part)
            dk = dk + nn(grad_low, q_part)
            head = slice(k * HEAD_DIM, (k + 1) * HEAD_DIM)
            dq_acc[head, qf:] += nn(kt[head, pl.ds(kf, TILE)], grad_low)
        dqkv_ref[pl.ds(kf, TILE), PAIR : 2 * PAIR] = low(dk)
        dqkv_ref[pl.ds(kf, TILE), 2 * PAIR :] = low(dv)

    def step(kb, carry):
        count = meta_ref[3 + tiles + kb]
        for n in range(TILE // SLAB, length // SLAB + 1):
            @pl.when(count == n)
            def _():
                block(kb, n)
        return carry

    lax.fori_loop(0, tiles, step, 0)
    dqkv_ref[:, :PAIR] = low(dq_acc[...].T)
    for fetch in fetches:
        fetch.wait()
    exact = nn(turned[...], dqkv_ref[...])
    summed[...] = low(exact)
    by_row = jnp.sum(exact * wide(matrix[...]), axis=1, keepdims=True)
    gain_ref[...] = jnp.broadcast_to(by_row, (by_row.shape[0], SLAB)).T[0:1, :]
    inner, outer, rows, _ = weight_ref.shape
    for m in range(inner):
        for k in range(outer):
            weight_ref[m, k] = summed[row_span(relative, shard_at(relative, meta_ref, m, k), rows), :]

    group = lax.broadcasted_iota(jnp.int32, (8, skewed.shape[-1]), 0)
    for k in range(2):
        held = skewed[k, SLAB - 8 :, :]
        for a in range(SLAB // 8 - 1):
            held = held + pltpu.roll(skewed[k, a * 8 : (a + 1) * 8, :], SLAB - 8 * (a + 1), 1)
        for bit in (1, 2, 4):
            held = jnp.where(((7 - group) & bit) != 0, pltpu.roll(held, bit, 1), held)
        diag_ref[k : k + 1, :] = jnp.sum(held, axis=0, keepdims=True)


def attend_backward(chunk, side, relative, shards, meta, qkv, out, grad, ends, logs, table, turned, matrices):
    length = qkv.shape[1]
    width = turned.shape[0]
    keep = table.shape[-1]
    lanes = 2 * length
    turn = lambda i, m: (chunk, 0, 0)
    same = lambda i, m: (0, 0)
    piece = (INNER, shards // INNER, width // shards, TRIPLE)
    return pl.pallas_call(
        functools.partial(backward_kernel, relative, chunk),
        grid_spec=pltpu.PrefetchScalarGridSpec(
            num_scalar_prefetch=1,
            grid=(1,),
            in_specs=[
                pl.BlockSpec((1, length, TRIPLE), turn),
                pl.BlockSpec((1, length, PAIR), turn),
                pl.BlockSpec((1, 1, length, PAIR), lambda i, m: (chunk, side, 0, 0)),
                pl.BlockSpec((1, length), same),
                pl.BlockSpec((1, 2, length), turn),
                pl.BlockSpec((2, SLAB, keep), lambda i, m: (chunk + CHUNKS * ((side + m[0]) % 2), 0, 0)),
                pl.BlockSpec(memory_space=pl.ANY),
                pl.BlockSpec(memory_space=pl.ANY),
            ],
            out_specs=[
                pl.BlockSpec((length, TRIPLE), same),
                pl.BlockSpec(piece, lambda i, m: (0, 0, 0, 0)),
                pl.BlockSpec((2, lanes), same),
                pl.BlockSpec((1, width), same),
            ],
            scratch_shapes=[
                pltpu.VMEM((2, length, PAIR), jnp.bfloat16),
                pltpu.VMEM((2, length, PAIR), jnp.bfloat16),
                pltpu.VMEM((PAIR, length), jnp.bfloat16),
                pltpu.VMEM((PAIR, length), jnp.float32),
                pltpu.VMEM((2, SLAB, lanes), jnp.float32),
                pltpu.VMEM((16, length), jnp.float32),
                pltpu.VMEM((width, TRIPLE), jnp.bfloat16),
                pltpu.VMEM((width, length), jnp.bfloat16),
                pltpu.VMEM((width, TRIPLE), jnp.bfloat16),
                pltpu.SemaphoreType.DMA((2,)),
            ],
        ),
        out_shape=[
            in_hbm((length, TRIPLE), jnp.bfloat16),
            in_hbm(piece, jnp.bfloat16),
            in_hbm((2, lanes), jnp.float32),
            in_hbm((1, width), jnp.float32),
        ],
        compiler_params=pltpu.CompilerParams(vmem_limit_bytes=40 * MIB),
        cost_estimate=pl.CostEstimate(
            flops=1, bytes_accessed=1, transcendentals=0
        ),
        name="attend_backward",
    )(meta, *from_hbm(qkv, out, grad), ends, logs, *from_hbm(table, turned, matrices))


def feed_kernel(
    meta_ref, x_ref, cot_ref, own_att_ref, other_att_ref, gain_ref, mix_ref, up0_ref, up1_ref, down_ref,
    out_ref, sgrad_ref, agrad_ref, later_ref, rest_ref, own_ref, other_ref,
    state, scale, normed, turned, total, upstream, act, pre, mixing, attended, branch, up, down,
):
    block = pl.program_id(0)
    blocks = pl.num_programs(0)
    me = meta_ref[0]
    length, width = x_ref.shape
    half = width // 2
    shards, _, rows, _ = mix_ref.shape
    count = length // ROWS

    @pl.when(block == 0)
    def _():
        for c in range(2):
            mixing[:, c * half : (c + 1) * half] = mix_ref[:, c].reshape(width, half)
        for p, ref in enumerate((own_att_ref, other_att_ref)):
            for i in range(CHUNKS):
                spot = pl.multiple_of((i + CHUNKS * ((p + me) % 2)) * PAIR, PAIR)
                attended[:, pl.ds(spot, PAIR)] = ref[i]

        def start(n, carry):
            spot = pl.ds(pl.multiple_of(n * ROWS, ROWS), ROWS)
            held = wide(x_ref[spot, :]) + nn(attended[spot, :], mixing[...])
            state[spot, :] = held
            found = lax.rsqrt(jnp.mean(held * held, axis=1, keepdims=True) + EPS)
            scale[spot, :] = jnp.broadcast_to(found, (ROWS, SLAB))
            normed[spot, :] = low(held * found * gain_ref[...])
            return carry

        lax.fori_loop(0, count, start, 0)
        turned[...] = normed[...].T
        total[...] = jnp.zeros_like(total)
        upstream[...] = jnp.zeros_like(upstream)

    for c, ref in enumerate((up0_ref, up1_ref)):
        up[:, c * half : (c + 1) * half] = ref[...].reshape(width, half)
        down[:, c * half : (c + 1) * half] = down_ref[:, c].reshape(width, half)

    def middle(n, carry):
        spot = pl.ds(n * ROWS, ROWS)
        v = nn(normed[spot, :], up[...])
        square = v * v
        bent = jnp.tanh(v * (CURVE + (CURVE * CUBE) * square))
        gate = 0.5 + 0.5 * bent
        slope = gate + (0.5 * v) * (1.0 - bent * bent) * (CURVE + (3 * CURVE * CUBE) * square)
        active = low(v * gate)
        act[spot, :] = active
        total[spot, :] += nn(active, down[...])
        changed = low(nt(cot_ref[spot, :], down[...]) * slope)
        pre[spot, :] = changed
        upstream[spot, :] += nt(changed, up[...])
        return carry

    for n in range(count):
        middle(n, 0)
    long = down_ref.shape[2]
    per = width // long
    steps = blocks // 2

    def halves(values):
        left, right = values[:, :half], values[:, half:]
        first = me == 0
        return jnp.where(first, left, right), jnp.where(first, right, left)

    kept, sent = halves(low(tn(act[...], cot_ref[...])))
    for s in range(per):
        own_ref[s % INNER, s // INNER] = kept[s * long : (s + 1) * long]
        other_ref[s % INNER, s // INNER] = sent[s * long : (s + 1) * long]
    dup = low(nn(turned[...], pre[...]))
    for c in range(2):
        start = pl.multiple_of(rows + (block % steps * 2 + c) * rows, rows)
        for s in range(shards):
            rest_ref[s, block // steps, pl.ds(start, rows)] = dup[
                s * rows : (s + 1) * rows, c * half : (c + 1) * half
            ]

    @pl.when(block == blocks - 1)
    def _():
        gain = gain_ref[...]

        def finish(n, parts):
            spot = pl.ds(pl.multiple_of(n * ROWS, ROWS), ROWS)
            held = state[spot, :]
            found = scale[spot, :][:, :1]
            out_ref[spot, :] = low(held + total[spot, :])
            grads = upstream[spot, :]
            parts = parts + jnp.sum(grads * held * found, axis=0, keepdims=True)
            scaled = grads * gain
            mean = jnp.mean(scaled * held, axis=1, keepdims=True)
            result = wide(cot_ref[spot, :]) + found * (scaled - held * (found * found * mean))
            sgrad_ref[spot, :] = result
            rounded = low(result)
            branch[spot, :] = rounded
            back = low(nt(rounded, mixing[...]))
            for pair in range(width // PAIR):
                agrad_ref[pair % CHUNKS, (pair // CHUNKS + me) % 2, spot, :] = back[
                    :, pair * PAIR : (pair + 1) * PAIR
                ]
            return parts

        later_ref[...] = lax.fori_loop(0, count, finish, jnp.zeros((1, width), jnp.float32))
        dmix = low(tn(attended[...], branch[...]))
        for s in range(shards):
            for c in range(2):
                rest_ref[s, c, :rows] = dmix[s * rows : (s + 1) * rows, c * half : (c + 1) * half]


def feed_forward(relative, meta, inputs, cotangent, attended, gain, gathered):
    length, width = inputs.shape
    half = width // 2
    shards, _, every, _ = gathered.shape
    rows = width // shards
    groups = (every - rows) // (2 * rows)
    long = groups * rows
    per = width // long
    steps = groups // 2
    blocks = 2 * steps
    same = lambda b, m: (0, 0)
    full = pl.BlockSpec((length, width), same)
    down_piece = pl.BlockSpec(
        (INNER, per // INNER, long, half), lambda b, m: (0, b ^ m[2] if relative else b, 0, 0)
    )
    pair = pl.BlockSpec((CHUNKS, length, PAIR), lambda b, m: (0, 0, 0))
    return pl.pallas_call(
        feed_kernel,
        grid_spec=pltpu.PrefetchScalarGridSpec(
            num_scalar_prefetch=1,
            grid=(blocks,),
            in_specs=[
                full, full, pair, pair,
                pl.BlockSpec((1, width), same),
                pl.BlockSpec((shards, 2, rows, half), lambda b, m: (0, 0, groups, 0)),
                pl.BlockSpec((shards, 1, rows, half), lambda b, m: (0, b // steps, groups + 1 + 2 * (b % steps), 0)),
                pl.BlockSpec((shards, 1, rows, half), lambda b, m: (0, b // steps, groups + 2 + 2 * (b % steps), 0)),
                pl.BlockSpec((per, 2, long, half), lambda b, m: (b, 0, 0, 0)),
            ],
            out_specs=[
                full, full,
                pl.BlockSpec((CHUNKS, 2, length, PAIR), lambda b, m: (0, 0, 0, 0)),
                pl.BlockSpec((1, width), same),
                pl.BlockSpec((shards, 2, every - long, half), lambda b, m: (0, 0, 0, 0)),
                down_piece,
                down_piece,
            ],
            scratch_shapes=[
                pltpu.VMEM((length, width), jnp.float32),
                pltpu.VMEM((length, SLAB), jnp.float32),
                pltpu.VMEM((length, width), jnp.bfloat16),
                pltpu.VMEM((width, length), jnp.bfloat16),
                pltpu.VMEM((length, width), jnp.float32),
                pltpu.VMEM((length, width), jnp.float32),
                pltpu.VMEM((length, width), jnp.bfloat16),
                pltpu.VMEM((length, width), jnp.bfloat16),
                pltpu.VMEM((width, width), jnp.bfloat16),
                pltpu.VMEM((length, width), jnp.bfloat16),
                pltpu.VMEM((length, width), jnp.bfloat16),
                pltpu.VMEM((width, width), jnp.bfloat16),
                pltpu.VMEM((width, width), jnp.bfloat16),
            ],
        ),
        out_shape=[
            in_hbm((length, width), jnp.bfloat16),
            in_hbm((length, width), jnp.float32),
            in_hbm((CHUNKS, 2, length, PAIR), jnp.bfloat16),
            in_hbm((1, width), jnp.float32),
            in_hbm((shards, 2, every - long, half), jnp.bfloat16),
            in_hbm((INNER, shards // INNER, long, half), jnp.bfloat16),
            in_hbm((INNER, shards // INNER, long, half), jnp.bfloat16),
        ],
        compiler_params=pltpu.CompilerParams(vmem_limit_bytes=60 * MIB),
        cost_estimate=pl.CostEstimate(
            flops=12 * length * width * width * blocks + 6 * length * width * width,
            bytes_accessed=14 * length * width + 8 * width * width * blocks,
            transcendentals=length * width * blocks,
        ),
        name="feed_forward",
    )(meta, inputs, cotangent, *attended, gain.reshape(1, width), *[gathered] * 4)


def last_kernel(x_ref, scale_ref, gain_ref, sgrad_ref, *refs):
    grads, weights = refs[: 2 * CHUNKS], refs[2 * CHUNKS : 2 * CHUNKS + 2]
    out_ref = refs[2 * CHUNKS + 2]
    x = wide(x_ref[...])
    found = scale_ref[...]
    upstream = jnp.zeros(x.shape, jnp.float32)
    for i in range(CHUNKS):
        for side in range(2):
            upstream = upstream + nt(grads[2 * i + side][...], weights[side][i])
    scaled = upstream * gain_ref[...]
    mean = jnp.mean(scaled * x, axis=1, keepdims=True)
    out_ref[...] = low(sgrad_ref[...] + found * (scaled - x * (found * found * mean)))


def last(inputs, scale, gain, state_grad, grads, weights):
    length, width = inputs.shape
    step = lambda i: (i, 0)
    same = lambda i: (0, 0)
    return pl.pallas_call(
        last_kernel,
        grid=(length // ROWS,),
        in_specs=[
            pl.BlockSpec((ROWS, width), step),
            pl.BlockSpec((ROWS, 1), step),
            pl.BlockSpec((1, width), same),
            pl.BlockSpec((ROWS, width), step),
        ]
        + [pl.BlockSpec((ROWS, TRIPLE), step)] * (2 * CHUNKS)
        + [pl.BlockSpec((CHUNKS, width, TRIPLE), lambda i: (0, 0, 0))] * 2,
        out_specs=pl.BlockSpec((ROWS, width), step),
        out_shape=in_hbm((length, width), jnp.bfloat16),
        compiler_params=pltpu.CompilerParams(vmem_limit_bytes=48 * MIB),
        cost_estimate=pl.CostEstimate(
            flops=1, bytes_accessed=1, transcendentals=0
        ),
        name="last",
    )(inputs, scale, gain.reshape(1, width), state_grad, *from_hbm(*grads, *weights))


def swap(values):
    return lax.ppermute(values, "replica", [(0, 1), (1, 0)])


def shift(values, shards, distance):
    return lax.ppermute(values, "shard", [(i, i ^ distance) for i in range(shards)])


def tie(values, *before):
    return lax.optimization_barrier((values,) + before)[0]


def gather_relative(own, shards, *before):
    line = jnp.stack([own] + [shift(own, shards, k * INNER) for k in range(1, shards // INNER)])
    came = [shift(line, shards, m) for m in range(1, INNER)]
    return jnp.stack([line] + [tie(c, *before) for c in came])


def cross(own, came):
    return [low(wide(own[m]) + wide(came[m])) for m in range(INNER)]


def plane(places, shards):
    return [places[0]] + [shift(places[m], shards, m) for m in range(1, INNER)]


def column(line, shards):
    return [line[0]] + [shift(line[k], shards, k * INNER) for k in range(1, shards // INNER)]


def total_of(parts):
    total = wide(parts[0])
    for part in parts[1:]:
        total = total + wide(part)
    return total


def exchange(pieces, groups):
    return lax.all_to_all(pieces, "shard", 0, 0, axis_index_groups=groups)


def inner_groups(shards):
    return [[o * INNER + i for i in range(INNER)] for o in range(shards // INNER)]


def natural_halves(own):
    other = swap(own)
    first = lax.axis_index("replica") == 0
    return jnp.where(first, own, other), jnp.where(first, other, own)


def scatter_halves(own, other):
    halves = []
    for part in (own, other):
        whole = jnp.swapaxes(part, 0, 1).reshape((-1,) + part.shape[2:])
        halves.append(wide(lax.psum_scatter(whole, "shard", scatter_dimension=0, tiled=True))[0])
    return lax.psum(tuple(halves), "replica")


def body(
    copies,
    shards,
    inputs,
    cotangent,
    block_ids,
    buckets,
    early_gain,
    query_weight,
    key_weight,
    value_weight,
    mixing_weight,
    relative_table,
    later_gain,
    up_weight,
    down_weight,
):
    length, width = inputs.shape
    half = width // 2
    hidden = up_weight.shape[1]
    bucket_count, heads = relative_table.shape
    offsets = buckets.shape[0]
    relative = copies == 2 and width // shards % 16 == 0 and INNER * hidden == shards * width
    me = lax.axis_index("replica") if relative else jnp.int32(0)
    spot = lax.axis_index("shard") if relative else jnp.int32(0)

    def parts_of(h):
        column = lambda w, c: lax.dynamic_slice_in_dim(w, c, half, 1)
        groups = up_weight.shape[1] // width
        return jnp.concatenate(
            [column(down_weight, h * half), column(mixing_weight, h * half)]
            + [column(up_weight, (h * groups + j) * half) for j in range(groups)],
            axis=0,
        )

    def triples_of(h):
        weights = (query_weight, key_weight, value_weight)
        starts = [(chunk + CHUNKS * h) * PAIR for chunk in range(CHUNKS)]
        return jnp.stack(
            [
                jnp.concatenate([lax.dynamic_slice_in_dim(w, at, PAIR, 1) for w in weights], axis=1)
                for at in starts
            ]
        )

    outer = shards // INNER
    if relative:
        feed_part, triple_part = pack(
            me.astype(jnp.int32).reshape(1), query_weight, key_weight, value_weight, mixing_weight, up_weight, down_weight
        )
        gathered = lax.all_gather(feed_part, ("shard", "replica"), axis=0, tiled=True)
    else:
        gathered = lax.all_gather(jnp.stack([parts_of(0), parts_of(1)]), "shard", axis=0, tiled=True)
    gathered = gathered.reshape(shards, 2, -1, half)

    normed, turned, early_scale, across, upright = prepare(inputs, early_gain, block_ids)
    tiles = length // TILE
    final = across.reshape(length // SLAB, SLAB)[:, SLAB - 1]
    counts = (final[TILE // SLAB - 1 :: TILE // SLAB] + SLAB - 1) // SLAB
    starts = jnp.arange(tiles, dtype=jnp.int32) * TILE
    uses = jnp.sum((starts[:, None] < final[None, :]).astype(jnp.int32), axis=1)
    place_of = jnp.stack([me, spot % INNER, spot // INNER])
    meta = jnp.concatenate([place_of, counts, uses]).astype(jnp.int32)

    onehot = (buckets[:, None] == jnp.arange(bucket_count, dtype=jnp.int32)[None, :]).astype(jnp.float32)
    mirrored = (buckets[::-1][:, None] == jnp.arange(bucket_count, dtype=jnp.int32)[None, :]).astype(jnp.float32)
    spare = ((0, 0), (0, 2 * length - offsets))
    forward_table, backward_table = [
        skew(jnp.pad(jnp.dot(hot, relative_table, precision=HIGH).T, spare), length) for hot in (onehot, mirrored)
    ]

    def natural(values):
        every = lax.all_gather(values, "shard", axis=0)
        return jnp.swapaxes(every.reshape((outer, INNER) + values.shape), 0, 1)

    if relative:
        own = gather_relative(triple_part, shards, forward_table, backward_table, normed, turned, upright, meta)
        other = swap(own)
    else:
        own, other = natural(triples_of(0)), natural(triples_of(1))

    held = [attend_forward(0, relative, meta, normed, own, upright, forward_table)]
    other = tie(other, held[0][2])
    held.append(attend_forward(1, relative, meta, normed, other, upright, forward_table))
    layer_output, state_grad, attended_grad, later_part, rest, down_own, down_other = feed_forward(
        relative, meta, inputs, cotangent, [h[1] for h in held], later_gain, gathered
    )

    grads, diagonals, gains = {}, {}, {}

    def backward(c, side, *before):
        qkv, attended, logs, matrices = held[side]
        grad = tie(attended_grad, *before) if before else attended_grad
        grads[c, side], weight, diagonals[c, side], gains[c, side] = attend_backward(
            c, side, relative, shards, meta, qkv, attended, grad, across, logs, backward_table, turned,
            matrices,
        )
        return weight, diagonals[c, side]

    def finish(*before):
        scale = tie(early_scale, *before) if before else early_scale
        ordered = [grads[c, side] for c in range(CHUNKS) for side in range(2)]
        return last(inputs, scale, early_gain, state_grad, ordered, [h[3] for h in held])

    rows = width // shards

    def vector_of():
        early_part = sum(gains.values()).reshape(-1) / early_gain
        sides = [jnp.concatenate([diagonals[c, side] for c in range(CHUNKS)], axis=0) for side in range(2)]
        first = me == 0
        stacked = jnp.concatenate([jnp.where(first, *sides), jnp.where(first, *sides[::-1])], axis=0)[:, :offsets]
        table_part = lax.dot_general(mirrored, stacked, (((0,), (1,)), ((), ())), precision=HIGH)
        return jnp.concatenate([early_part, later_part.reshape(-1), table_part.reshape(-1)])

    def small_sums():
        vector = vector_of()
        vector = jnp.pad(vector, (0, SMALL * half - vector.shape[0])).reshape(SMALL, half)
        high = low(vector)
        return jnp.concatenate([high, low(vector - wide(high))], axis=0)

    def halve(sums):
        vector = sums[:, :SMALL] + sums[:, SMALL:]
        high = low(vector)
        return jnp.concatenate([high, low(vector - wide(high))], axis=1)

    if relative:
        share = lax.psum_scatter(
            rest.reshape((2 * shards,) + rest.shape[2:]), ("shard", "replica"), scatter_dimension=0, tiled=True
        )[0]
        down_came = swap(down_other)
        other, done = backward(0, 1)
        came = swap(other)
        down_came = tie(down_came, done)
        down_pieces = exchange(
            low(wide(down_own) + wide(down_came)), inner_groups(shards)
        )
        own, done = backward(0, 0, done, down_came)
        places = cross(own, tie(came, done))
        plane0 = plane(places, shards)
        other, done = backward(1, 1, done, *places)
        came1 = swap(other)
        own1, done = backward(1, 0, done)
        down_line = low(jnp.sum(wide(tie(down_pieces, done)), axis=0))
        line0 = low(total_of([tie(p, done) for p in plane0]))
        early = jnp.concatenate([down_line, line0], axis=1)
        lines = lax.optimization_barrier(([early[k] for k in range(early.shape[0])], done))
        early_column = column(lines[0], shards)
        other, done = backward(2, 1, *lines[0], lines[1])
        came1 = tie(came1, done)
        came2 = swap(other)
        own2, done = backward(2, 0, done)
        came2 = tie(came2, done)
        places = [jnp.concatenate(p, axis=1) for p in zip(cross(own1, came1), cross(own2, came2), strict=True)]
        small = small_sums()
        late = [jnp.concatenate([p, jnp.broadcast_to(small, p.shape[:1] + small.shape)], axis=1) for p in places]
        late_plane = plane(late, shards)
        early = total_of([tie(p, done) for p in early_column])
        input_gradient = finish(*late, early)
        late = wide(late[0])
        for p in late_plane[1:]:
            late = late + wide(tie(p, input_gradient))
        late = jnp.concatenate([low(late[:, : 2 * rows]), halve(late[:, 2 * rows :])], axis=1)
        late = natural_halves(total_of(column(late, shards)))
        early = natural_halves(early)
        share = [wide(h) for h in natural_halves(tie(share, input_gradient))]
        small = late[0][2 * rows :] + late[1][2 * rows :]
        small = (small[:SMALL] + small[SMALL:]).reshape(-1)
        down_share = [h[:-rows] for h in early]
        shares = [[h[-rows:] for h in early], [h[:rows] for h in late], [h[rows : 2 * rows] for h in late]]
    else:
        shares = []
        for c in range(CHUNKS):
            other, _ = backward(c, 1)
            own, _ = backward(c, 0)
            shares.append(scatter_halves(own, other))
        input_gradient = finish()
        both = lax.psum_scatter(rest, "shard", scatter_dimension=0, tiled=True)[0]
        share = lax.psum((wide(both[0]), wide(both[1])), "replica")
        down_share = [
            lax.psum(
                wide(
                    lax.psum_scatter(
                        jnp.swapaxes(d, 0, 1).reshape((shards,) + d.shape[2:]), "shard", scatter_dimension=0, tiled=True
                    )
                )[0],
                "replica",
            )
            for d in (down_own, down_other)
        ]
        small = lax.psum(vector_of(), ("replica", "shard"))

    early_total, later_total = small[:width], small[width : 2 * width]
    table_total = small[2 * width : 2 * width + relative_table.size].reshape(bucket_count, heads)

    groups = hidden // width
    down_share = jnp.concatenate(down_share, axis=1)
    mixing_share = jnp.concatenate([share[0][:rows], share[1][:rows]], axis=1)
    up_share = jnp.concatenate(
        [share[h][rows * (1 + j) : rows * (2 + j)] for h in range(2) for j in range(groups)], axis=1
    )
    triples = [
        jnp.concatenate(
            [shares[c][h][:, n * PAIR : (n + 1) * PAIR] for h in range(2) for c in range(CHUNKS)], axis=1
        )
        for n in range(3)
    ]
    return (
        layer_output,
        input_gradient,
        early_total,
        triples[0],
        triples[1],
        triples[2],
        mixing_share,
        table_total,
        later_total,
        up_share,
        down_share,
    )


def solution(mesh):
    rows = P(("replica", "shard"), None)
    split = P("shard", None)
    same = P()
    return jax.shard_map(
        functools.partial(body, mesh.shape["replica"], mesh.shape["shard"]),
        mesh=mesh,
        in_specs=(rows, rows, rows, same, same, split, split, split, split, same, same, split, split),
        out_specs=(rows, rows, same, split, split, split, split, same, same, split, split),
        check_vma=False,
    )
```

```python
import functools
import math

import jax
import jax.numpy as jnp
from jax import lax
from jax.experimental import pallas as pl
from jax.experimental.pallas import tpu as pltpu
from jax.sharding import PartitionSpec as P

EPS = 1e-06
HIGH = lax.Precision.HIGHEST
HEAD_DIM = 64
PAIR = 2 * HEAD_DIM
TRIPLE = 3 * PAIR
SLAB = 128
TILE = 256
CHUNKS = 3
INNER = 4
ROWS = 512
SMALL = 8
NEG = -1e30
CURVE = math.sqrt(2 / math.pi)
CUBE = 0.044715
MIB = 1 << 20


def nt(left, right):
    return lax.dot_general(left, right, (((1,), (1,)), ((), ())), preferred_element_type=jnp.float32)


def nn(left, right):
    return lax.dot_general(left, right, (((1,), (0,)), ((), ())), preferred_element_type=jnp.float32)


def tn(left, right):
    return lax.dot_general(left, right, (((0,), (0,)), ((), ())), preferred_element_type=jnp.float32)


def low(values):
    return values.astype(jnp.bfloat16)


def wide(values):
    return values.astype(jnp.float32)


def in_hbm(shape, dtype):
    return pltpu.HBM(shape, dtype)


def from_hbm(*arrays):
    return [pltpu.with_memory_space_constraint(a, pltpu.HBM) for a in arrays]


def skew_kernel(rows_ref, out_ref):
    width = rows_ref.shape[-1]
    keep = out_ref.shape[-1]
    for k in range(rows_ref.shape[0]):
        spread = jnp.broadcast_to(rows_ref[k], (SLAB, width))
        moved = pltpu.roll(spread, width - SLAB + 1, 1, stride=1, stride_axis=0)
        out_ref[k] = moved[:, :keep]


def skew(rows, length):
    count, width = rows.shape
    keep = 2 * length - SLAB
    return pl.pallas_call(
        skew_kernel,
        grid=(count // 2,),
        in_specs=[pl.BlockSpec((2, 1, width), lambda i: (i, 0, 0))],
        out_specs=pl.BlockSpec((2, SLAB, keep), lambda i: (i, 0, 0)),
        out_shape=in_hbm((count, SLAB, keep), jnp.float32),
        compiler_params=pltpu.CompilerParams(vmem_limit_bytes=32 * MIB),
        cost_estimate=pl.CostEstimate(
            flops=count * SLAB * width, bytes_accessed=count * SLAB * keep * 4, transcendentals=0
        ),
        name="skew",
    )(rows.reshape(count, 1, width))


def pack_kernel(place_ref, query_ref, key_ref, value_ref, mix_ref, up_ref, down_ref, feed_ref, triple_ref):
    me = place_ref[0]
    long, half = down_ref.shape[0], feed_ref.shape[1]
    rows = mix_ref.shape[0]
    groups = up_ref.shape[1] // (2 * half)
    span = lambda n, size: pl.ds(pl.multiple_of(n * size, SLAB), size)
    feed_ref[:long] = down_ref[:, span(me, half)]
    feed_ref[long : long + rows] = mix_ref[:, span(me, half)]
    for j in range(groups):
        feed_ref[long + rows * (1 + j) : long + rows * (2 + j)] = up_ref[:, span(me * groups + j, half)]
    for chunk in range(CHUNKS):
        for n, ref in enumerate((query_ref, key_ref, value_ref)):
            triple_ref[chunk, :, n * PAIR : (n + 1) * PAIR] = ref[:, span(chunk + CHUNKS * me, PAIR)]


def pack(place, query, key, value, mix, up, down):
    rows, width = mix.shape
    half = width // 2
    long = down.shape[0]
    every = long + rows + rows * (up.shape[1] // width)
    whole = lambda a: pl.BlockSpec(a.shape, lambda i, m: (0, 0))
    arrays = (query, key, value, mix, up, down)
    return pl.pallas_call(
        pack_kernel,
        grid_spec=pltpu.PrefetchScalarGridSpec(
            num_scalar_prefetch=1,
            grid=(1,),
            in_specs=[whole(a) for a in arrays],
            out_specs=[
                pl.BlockSpec((every, half), lambda i, m: (0, 0)),
                pl.BlockSpec((CHUNKS, rows, TRIPLE), lambda i, m: (0, 0, 0)),
            ],
        ),
        out_shape=[in_hbm((every, half), jnp.bfloat16), in_hbm((CHUNKS, rows, TRIPLE), jnp.bfloat16)],
        cost_estimate=pl.CostEstimate(flops=1, bytes_accessed=1, transcendentals=0),
        compiler_params=pltpu.CompilerParams(vmem_limit_bytes=16 * MIB),
        name="pack",
    )(place, *from_hbm(*arrays))


def prepare_kernel(x_ref, gain_ref, row_ref, column_ref, normed_ref, turned_ref, scale_ref, across_ref, upright_ref):
    length = x_ref.shape[0]
    ids = row_ref[...]

    def part(n, ends):
        spot = pl.ds(pl.multiple_of(n * TILE, TILE), TILE)
        x = wide(x_ref[spot, :])
        found = lax.rsqrt(jnp.mean(x * x, axis=1, keepdims=True) + EPS)
        scale_ref[spot, :] = found
        normed_ref[spot, :] = low(x * found * gain_ref[...])
        mine = column_ref[spot, :]
        upright_ref[spot, :] = jnp.sum(jnp.where(ids <= mine, 1, 0), axis=1, keepdims=True)
        return ends + jnp.sum(jnp.where(mine <= ids, 1, 0), axis=0, keepdims=True)

    across_ref[...] = lax.fori_loop(0, length // TILE, part, jnp.zeros((1, length), jnp.int32))
    turned_ref[...] = normed_ref[...].T


def prepare(inputs, gain, ids):
    length, width = inputs.shape
    return pl.pallas_call(
        prepare_kernel,
        out_shape=[
            in_hbm((length, width), jnp.bfloat16),
            in_hbm((width, length), jnp.bfloat16),
            in_hbm((length, 1), jnp.float32),
            in_hbm((1, length), jnp.int32),
            in_hbm((length, 1), jnp.int32),
        ],
        compiler_params=pltpu.CompilerParams(vmem_limit_bytes=32 * MIB),
        cost_estimate=pl.CostEstimate(flops=1, bytes_accessed=1, transcendentals=0),
        name="prepare",
    )(inputs, gain.reshape(1, width), ids.reshape(1, length), ids.reshape(length, 1))


def shard_at(relative, meta_ref, m, k):
    return (meta_ref[2] ^ k) * INNER + (meta_ref[1] ^ m) if relative else k * INNER + m


def row_span(relative, shard, rows):
    return pl.ds(pl.multiple_of(shard * rows, 16) if relative else shard * rows, rows)


def forward_kernel(
    relative, meta_ref, normed_ref, pieces_ref, ends_ref, table_ref, qkv_ref, out_ref, log_ref, weight_ref
):
    length = normed_ref.shape[0]
    tiles = length // TILE
    inner, outer, rows, _ = pieces_ref.shape
    for m in range(inner):
        for k in range(outer):
            span = row_span(relative, shard_at(relative, meta_ref, m, k), rows)
            weight_ref[0, span, :] = pieces_ref[m, k]
    qkv_ref[0] = low(nn(normed_ref[...], weight_ref[0]))
    left = lax.broadcasted_iota(jnp.int32, (TILE, PAIR), 1) < HEAD_DIM

    def block(i, n):
        first = pl.multiple_of(i * TILE, TILE)
        query = qkv_ref[0, pl.ds(first, TILE), :PAIR]
        keys = qkv_ref[0, : n * SLAB, PAIR : 2 * PAIR]
        values = qkv_ref[0, : n * SLAB, 2 * PAIR :]
        ends = ends_ref[pl.ds(first, TILE), :]
        columns = lax.broadcasted_iota(jnp.int32, (TILE, n * SLAB), 1)
        allowed = columns < ends
        outs = []
        zero = jnp.zeros_like(query)
        offset = pl.multiple_of((tiles - 1 - i) * TILE + SLAB, SLAB)
        before = pl.multiple_of(offset - SLAB, SLAB)
        for k in range(2):
            mine = jnp.where(left, query, zero) if k == 0 else jnp.where(left, zero, query)
            bias = jnp.concatenate(
                [table_ref[k, :, pl.ds(offset, n * SLAB)], table_ref[k, :, pl.ds(before, n * SLAB)]], axis=0
            )
            scores = jnp.where(allowed, nt(mine, keys) + bias, NEG)
            peak = jnp.max(scores, axis=1, keepdims=True)
            weights = jnp.exp(scores - peak)
            total = jnp.sum(weights, axis=1, keepdims=True)
            outs.append(nn(low(weights), values) / total)
            logs = jnp.broadcast_to(peak + jnp.log(total), (TILE, SLAB))
            log_ref[0, k : k + 1, pl.ds(first, TILE)] = logs.T[0:1, :]
        out_ref[0, pl.ds(first, TILE), :] = low(jnp.where(left, outs[0], outs[1]))

    def step(i, carry):
        count = meta_ref[3 + i]
        for n in range(TILE // SLAB, length // SLAB + 1):
            @pl.when(count == n)
            def _():
                block(i, n)
        return carry

    lax.fori_loop(0, tiles, step, 0)


def attend_forward(side, relative, meta, normed, pieces, ends, table):
    length, width = normed.shape
    keep = table.shape[-1]
    turn = lambda p, m: (p, 0, 0)
    same = lambda p, m: (0, 0)
    return pl.pallas_call(
        functools.partial(forward_kernel, relative),
        grid_spec=pltpu.PrefetchScalarGridSpec(
            num_scalar_prefetch=1,
            grid=(CHUNKS,),
            in_specs=[
                pl.BlockSpec((length, width), same),
                pl.BlockSpec(pieces.shape[:2] + (None,) + pieces.shape[3:], lambda p, m: (0, 0, p, 0, 0)),
                pl.BlockSpec((length, 1), same),
                pl.BlockSpec((2, SLAB, keep), lambda p, m: (p + CHUNKS * ((side + m[0]) % 2), 0, 0)),
            ],
            out_specs=[
                pl.BlockSpec((1, length, TRIPLE), turn),
                pl.BlockSpec((1, length, PAIR), turn),
                pl.BlockSpec((1, 2, length), turn),
                pl.BlockSpec((1, width, TRIPLE), turn),
            ],
        ),
        out_shape=[
            in_hbm((CHUNKS, length, TRIPLE), jnp.bfloat16),
            in_hbm((CHUNKS, length, PAIR), jnp.bfloat16),
            in_hbm((CHUNKS, 2, length), jnp.float32),
            in_hbm((CHUNKS, width, TRIPLE), jnp.bfloat16),
        ],
        compiler_params=pltpu.CompilerParams(vmem_limit_bytes=48 * MIB),
        cost_estimate=pl.CostEstimate(
            flops=24 * length * length * HEAD_DIM * 2,
            bytes_accessed=3 * length * (width + 2 * TRIPLE) + 6 * SLAB * keep * 4,
            transcendentals=6 * length * length,
        ),
        name="attend_forward",
    )(meta, *from_hbm(normed), pieces, *from_hbm(ends, table))


def backward_kernel(
    relative, chunk, meta_ref, qkv_ref, out_ref, grad_ref, ends_ref, log_ref, table_ref, turned_ref, matrix_ref,
    dqkv_ref, weight_ref, diag_ref, gain_ref,
    qm, gm, kt, dq_acc, skewed, delta, summed, turned, matrix, sems,
):
    fetches = [
        pltpu.make_async_copy(turned_ref, turned, sems.at[0]),
        pltpu.make_async_copy(matrix_ref.at[chunk], matrix, sems.at[1]),
    ]
    for fetch in fetches:
        fetch.start()
    length = qkv_ref.shape[1]
    tiles = length // TILE
    left = lax.broadcasted_iota(jnp.int32, (length, PAIR), 1) < HEAD_DIM
    query, grads = qkv_ref[0, :, :PAIR], grad_ref[0, 0]
    zero = jnp.zeros_like(query)
    for k in range(2):
        pick = left if k == 0 else jnp.logical_not(left)
        qm[k] = jnp.where(pick, query, zero)
        gm[k] = jnp.where(pick, grads, zero)
    kt[...] = qkv_ref[0, :, PAIR : 2 * PAIR].T
    dq_acc[...] = jnp.zeros_like(dq_acc)
    skewed[...] = jnp.zeros_like(skewed)
    product = wide(grads) * wide(out_ref[0])
    high = low(product)
    rest = low(product - wide(high))
    lane = lax.broadcasted_iota(jnp.int32, (16, PAIR), 1)
    row = lax.broadcasted_iota(jnp.int32, (16, PAIR), 0)
    chooser = low(jnp.where(lane // HEAD_DIM == row, 1.0, 0.0))
    delta[...] = nt(chooser, high) + nt(chooser, rest)

    def block(kb, n):
        kf = pl.multiple_of(kb * TILE, TILE)
        span = n * SLAB
        qf = length - span
        offset = pl.multiple_of((tiles - 1 - kb) * TILE + qf + SLAB, SLAB)
        before = pl.multiple_of(offset - SLAB, SLAB)
        rows = lax.broadcasted_iota(jnp.int32, (TILE, span), 0) + kf
        allowed = rows < ends_ref[:, qf:]
        k_tile = qkv_ref[0, pl.ds(kf, TILE), PAIR : 2 * PAIR]
        v_tile = qkv_ref[0, pl.ds(kf, TILE), 2 * PAIR :]
        dk = jnp.zeros((TILE, PAIR), jnp.float32)
        dv = jnp.zeros((TILE, PAIR), jnp.float32)
        for k in range(2):
            q_part = qm[k, qf:, :]
            g_part = gm[k, qf:, :]
            bias = jnp.concatenate(
                [table_ref[k, :, pl.ds(offset, span)], table_ref[k, :, pl.ds(before, span)]], axis=0
            )
            scores = nt(k_tile, q_part) + bias - log_ref[0, k : k + 1, qf:]
            probs = jnp.where(allowed, jnp.exp(scores), 0.0)
            above = nt(v_tile, g_part) - delta[k : k + 1, qf:]
            grad = probs * above
            skewed[k, :, pl.ds(offset, span)] += grad[:SLAB]
            skewed[k, :, pl.ds(before, span)] += grad[SLAB:]
            grad_low = low(grad)
            dv = dv + nn(low(probs), g_part)
            dk = dk + nn(grad_low, q_part)
            head = slice(k * HEAD_DIM, (k + 1) * HEAD_DIM)
            dq_acc[head, qf:] += nn(kt[head, pl.ds(kf, TILE)], grad_low)
        dqkv_ref[pl.ds(kf, TILE), PAIR : 2 * PAIR] = low(dk)
        dqkv_ref[pl.ds(kf, TILE), 2 * PAIR :] = low(dv)

    def step(kb, carry):
        count = meta_ref[3 + tiles + kb]
        for n in range(TILE // SLAB, length // SLAB + 1):
            @pl.when(count == n)
            def _():
                block(kb, n)
        return carry

    lax.fori_loop(0, tiles, step, 0)
    dqkv_ref[:, :PAIR] = low(dq_acc[...].T)
    for fetch in fetches:
        fetch.wait()
    exact = nn(turned[...], dqkv_ref[...])
    summed[...] = low(exact)
    by_row = jnp.sum(exact * wide(matrix[...]), axis=1, keepdims=True)
    gain_ref[...] = jnp.broadcast_to(by_row, (by_row.shape[0], SLAB)).T[0:1, :]
    inner, outer, rows, _ = weight_ref.shape
    for m in range(inner):
        for k in range(outer):
            weight_ref[m, k] = summed[row_span(relative, shard_at(relative, meta_ref, m, k), rows), :]

    group = lax.broadcasted_iota(jnp.int32, (8, skewed.shape[-1]), 0)
    for k in range(2):
        held = skewed[k, SLAB - 8 :, :]
        for a in range(SLAB // 8 - 1):
            held = held + pltpu.roll(skewed[k, a * 8 : (a + 1) * 8, :], SLAB - 8 * (a + 1), 1)
        for bit in (1, 2, 4):
            held = jnp.where(((7 - group) & bit) != 0, pltpu.roll(held, bit, 1), held)
        diag_ref[k : k + 1, :] = jnp.sum(held, axis=0, keepdims=True)


def attend_backward(chunk, side, relative, shards, meta, qkv, out, grad, ends, logs, table, turned, matrices):
    length = qkv.shape[1]
    width = turned.shape[0]
    keep = table.shape[-1]
    lanes = 2 * length
    turn = lambda i, m: (chunk, 0, 0)
    same = lambda i, m: (0, 0)
    piece = (INNER, shards // INNER, width // shards, TRIPLE)
    return pl.pallas_call(
        functools.partial(backward_kernel, relative, chunk),
        grid_spec=pltpu.PrefetchScalarGridSpec(
            num_scalar_prefetch=1,
            grid=(1,),
            in_specs=[
                pl.BlockSpec((1, length, TRIPLE), turn),
                pl.BlockSpec((1, length, PAIR), turn),
                pl.BlockSpec((1, 1, length, PAIR), lambda i, m: (chunk, side, 0, 0)),
                pl.BlockSpec((1, length), same),
                pl.BlockSpec((1, 2, length), turn),
                pl.BlockSpec((2, SLAB, keep), lambda i, m: (chunk + CHUNKS * ((side + m[0]) % 2), 0, 0)),
                pl.BlockSpec(memory_space=pl.ANY),
                pl.BlockSpec(memory_space=pl.ANY),
            ],
            out_specs=[
                pl.BlockSpec((length, TRIPLE), same),
                pl.BlockSpec(piece, lambda i, m: (0, 0, 0, 0)),
                pl.BlockSpec((2, lanes), same),
                pl.BlockSpec((1, width), same),
            ],
            scratch_shapes=[
                pltpu.VMEM((2, length, PAIR), jnp.bfloat16),
                pltpu.VMEM((2, length, PAIR), jnp.bfloat16),
                pltpu.VMEM((PAIR, length), jnp.bfloat16),
                pltpu.VMEM((PAIR, length), jnp.float32),
                pltpu.VMEM((2, SLAB, lanes), jnp.float32),
                pltpu.VMEM((16, length), jnp.float32),
                pltpu.VMEM((width, TRIPLE), jnp.bfloat16),
                pltpu.VMEM((width, length), jnp.bfloat16),
                pltpu.VMEM((width, TRIPLE), jnp.bfloat16),
                pltpu.SemaphoreType.DMA((2,)),
            ],
        ),
        out_shape=[
            in_hbm((length, TRIPLE), jnp.bfloat16),
            in_hbm(piece, jnp.bfloat16),
            in_hbm((2, lanes), jnp.float32),
            in_hbm((1, width), jnp.float32),
        ],
        compiler_params=pltpu.CompilerParams(vmem_limit_bytes=40 * MIB),
        cost_estimate=pl.CostEstimate(
            flops=1, bytes_accessed=1, transcendentals=0
        ),
        name="attend_backward",
    )(meta, *from_hbm(qkv, out, grad), ends, logs, *from_hbm(table, turned, matrices))


def feed_kernel(
    meta_ref, x_ref, cots_ref, own_att_ref, other_att_ref, gain_ref, mix_ref, up0_ref, up1_ref, down_ref,
    out_ref, sgrad_ref, agrad_ref, later_ref, rest_ref, own_ref, other_ref,
    state, scale, normed, turned, total, upstream, act, pre, mixing, attended, branch, up, down, parts, mixed, cot_ref, sems,
):
    block = pl.program_id(0)
    blocks = pl.num_programs(0)
    me = meta_ref[0]
    length, width = x_ref.shape
    half = width // 2
    shards, _, rows, _ = mix_ref.shape
    count = length // ROWS
    fetch = pltpu.make_async_copy(cots_ref, cot_ref, sems.at[0])

    @pl.when(block == 0)
    def _():
        fetch.start()
        for c in range(2):
            mixing[:, c * half : (c + 1) * half] = mix_ref[:, c].reshape(width, half)
        for p, ref in enumerate((own_att_ref, other_att_ref)):
            for i in range(CHUNKS):
                spot = pl.multiple_of((i + CHUNKS * ((p + me) % 2)) * PAIR, PAIR)
                attended[:, pl.ds(spot, PAIR)] = ref[i]

        def start(n, carry):
            spot = pl.ds(pl.multiple_of(n * ROWS, ROWS), ROWS)
            held = wide(x_ref[spot, :]) + nn(attended[spot, :], mixing[...])
            state[spot, :] = held
            found = lax.rsqrt(jnp.mean(held * held, axis=1, keepdims=True) + EPS)
            scale[spot, :] = jnp.broadcast_to(found, (ROWS, SLAB))
            normed[spot, :] = low(held * found * gain_ref[...])
            return carry

        lax.fori_loop(0, count, start, 0)
        turned[...] = normed[...].T
        total[...] = jnp.zeros_like(total)
        upstream[...] = jnp.zeros_like(upstream)
        fetch.wait()

    for c, ref in enumerate((up0_ref, up1_ref)):
        up[:, c * half : (c + 1) * half] = ref[...].reshape(width, half)
        down[:, c * half : (c + 1) * half] = down_ref[:, c].reshape(width, half)

    def middle(n, carry):
        spot = pl.ds(n * ROWS, ROWS)
        v = nn(normed[spot, :], up[...])
        square = v * v
        bent = jnp.tanh(v * (CURVE + (CURVE * CUBE) * square))
        gate = 0.5 + 0.5 * bent
        slope = gate + (0.5 * v) * (1.0 - bent * bent) * (CURVE + (3 * CURVE * CUBE) * square)
        active = low(v * gate)
        act[spot, :] = active
        total[spot, :] += nn(active, down[...])
        changed = low(nt(cot_ref[spot, :], down[...]) * slope)
        pre[spot, :] = changed
        upstream[spot, :] += nt(changed, up[...])
        return carry

    for n in range(count):
        middle(n, 0)
    long = down_ref.shape[2]
    per = width // long
    steps = blocks // 2

    def halves(values):
        left, right = values[:, :half], values[:, half:]
        first = me == 0
        return jnp.where(first, left, right), jnp.where(first, right, left)

    kept, sent = halves(low(tn(act[...], cot_ref[...])))
    for s in range(per):
        own_ref[s % INNER, s // INNER] = kept[s * long : (s + 1) * long]
        other_ref[s % INNER, s // INNER] = sent[s * long : (s + 1) * long]
    dup = low(nn(turned[...], pre[...]))

    def sends(at):
        return [
            pltpu.make_async_copy(
                parts.at[c],
                rest_ref.at[:, at // steps, pl.ds(pl.multiple_of((1 + at % steps * 2 + c) * rows, rows), rows), :],
                sems.at[1 + c],
            )
            for c in range(2)
        ]

    @pl.when(block > 0)
    def _():
        for send in sends(block - 1):
            send.wait()

    for c in range(2):
        for s in range(shards):
            parts[c, s] = dup[s * rows : (s + 1) * rows, c * half : (c + 1) * half]
    for send in sends(block):
        send.start()

    @pl.when(block == blocks - 1)
    def _():
        gain = gain_ref[...]

        def finish(n, parts):
            spot = pl.ds(pl.multiple_of(n * ROWS, ROWS), ROWS)
            held = state[spot, :]
            found = scale[spot, :][:, :1]
            out_ref[spot, :] = low(held + total[spot, :])
            grads = upstream[spot, :]
            parts = parts + jnp.sum(grads * held * found, axis=0, keepdims=True)
            scaled = grads * gain
            mean = jnp.mean(scaled * held, axis=1, keepdims=True)
            result = wide(cot_ref[spot, :]) + found * (scaled - held * (found * found * mean))
            sgrad_ref[spot, :] = result
            rounded = low(result)
            branch[spot, :] = rounded
            back = low(nt(rounded, mixing[...]))
            for pair in range(width // PAIR):
                agrad_ref[pair % CHUNKS, (pair // CHUNKS + me) % 2, spot, :] = back[
                    :, pair * PAIR : (pair + 1) * PAIR
                ]
            return parts

        later_ref[...] = lax.fori_loop(0, count, finish, jnp.zeros((1, width), jnp.float32))
        dmix = low(tn(attended[...], branch[...]))
        for c in range(2):
            for s in range(shards):
                mixed[c, s] = dmix[s * rows : (s + 1) * rows, c * half : (c + 1) * half]
        leave = [pltpu.make_async_copy(mixed.at[c], rest_ref.at[:, c, :rows, :], sems.at[3 + c]) for c in range(2)]
        for send in leave:
            send.start()
        for send in leave + sends(block):
            send.wait()


def feed_forward(relative, meta, inputs, cotangent, attended, gain, gathered):
    length, width = inputs.shape
    half = width // 2
    shards, _, every, _ = gathered.shape
    rows = width // shards
    groups = (every - rows) // (2 * rows)
    long = groups * rows
    per = width // long
    steps = groups // 2
    blocks = 2 * steps
    same = lambda b, m: (0, 0)
    full = pl.BlockSpec((length, width), same)
    down_piece = pl.BlockSpec(
        (INNER, per // INNER, long, half), lambda b, m: (0, b ^ m[2] if relative else b, 0, 0)
    )
    pair = pl.BlockSpec((CHUNKS, length, PAIR), lambda b, m: (0, 0, 0))
    return pl.pallas_call(
        feed_kernel,
        grid_spec=pltpu.PrefetchScalarGridSpec(
            num_scalar_prefetch=1,
            grid=(blocks,),
            in_specs=[
                full, pl.BlockSpec(memory_space=pl.ANY), pair, pair,
                pl.BlockSpec((1, width), same),
                pl.BlockSpec((shards, 2, rows, half), lambda b, m: (0, 0, groups, 0)),
                pl.BlockSpec((shards, 1, rows, half), lambda b, m: (0, b // steps, groups + 1 + 2 * (b % steps), 0)),
                pl.BlockSpec((shards, 1, rows, half), lambda b, m: (0, b // steps, groups + 2 + 2 * (b % steps), 0)),
                pl.BlockSpec((per, 2, long, half), lambda b, m: (b, 0, 0, 0)),
            ],
            out_specs=[
                full, full,
                pl.BlockSpec((CHUNKS, 2, length, PAIR), lambda b, m: (0, 0, 0, 0)),
                pl.BlockSpec((1, width), same),
                pl.BlockSpec(memory_space=pl.ANY),
                down_piece,
                down_piece,
            ],
            scratch_shapes=[
                pltpu.VMEM((length, width), jnp.float32),
                pltpu.VMEM((length, SLAB), jnp.float32),
                pltpu.VMEM((length, width), jnp.bfloat16),
                pltpu.VMEM((width, length), jnp.bfloat16),
                pltpu.VMEM((length, width), jnp.float32),
                pltpu.VMEM((length, width), jnp.float32),
                pltpu.VMEM((length, width), jnp.bfloat16),
                pltpu.VMEM((length, width), jnp.bfloat16),
                pltpu.VMEM((width, width), jnp.bfloat16),
                pltpu.VMEM((length, width), jnp.bfloat16),
                pltpu.VMEM((length, width), jnp.bfloat16),
                pltpu.VMEM((width, width), jnp.bfloat16),
                pltpu.VMEM((width, width), jnp.bfloat16),
                pltpu.VMEM((2, shards, rows, half), jnp.bfloat16),
                pltpu.VMEM((2, shards, rows, half), jnp.bfloat16),
                pltpu.VMEM((length, width), jnp.bfloat16),
                pltpu.SemaphoreType.DMA((5,)),
            ],
        ),
        out_shape=[
            in_hbm((length, width), jnp.bfloat16),
            in_hbm((length, width), jnp.float32),
            in_hbm((CHUNKS, 2, length, PAIR), jnp.bfloat16),
            in_hbm((1, width), jnp.float32),
            in_hbm((shards, 2, every - long, half), jnp.bfloat16),
            in_hbm((INNER, shards // INNER, long, half), jnp.bfloat16),
            in_hbm((INNER, shards // INNER, long, half), jnp.bfloat16),
        ],
        compiler_params=pltpu.CompilerParams(vmem_limit_bytes=60 * MIB),
        cost_estimate=pl.CostEstimate(
            flops=12 * length * width * width * blocks + 6 * length * width * width,
            bytes_accessed=14 * length * width + 8 * width * width * blocks,
            transcendentals=length * width * blocks,
        ),
        name="feed_forward",
    )(meta, inputs, *from_hbm(cotangent), *attended, gain.reshape(1, width), *[gathered] * 4)


def last_kernel(x_ref, scale_ref, gain_ref, sgrad_ref, *refs):
    grads, weights = refs[: 2 * CHUNKS], refs[2 * CHUNKS : 2 * CHUNKS + 2]
    out_ref = refs[2 * CHUNKS + 2]
    x = wide(x_ref[...])
    found = scale_ref[...]
    upstream = jnp.zeros(x.shape, jnp.float32)
    for i in range(CHUNKS):
        for side in range(2):
            upstream = upstream + nt(grads[2 * i + side][...], weights[side][i])
    scaled = upstream * gain_ref[...]
    mean = jnp.mean(scaled * x, axis=1, keepdims=True)
    out_ref[...] = low(sgrad_ref[...] + found * (scaled - x * (found * found * mean)))


def last(inputs, scale, gain, state_grad, grads, weights):
    length, width = inputs.shape
    step = lambda i: (i, 0)
    same = lambda i: (0, 0)
    return pl.pallas_call(
        last_kernel,
        grid=(length // ROWS,),
        in_specs=[
            pl.BlockSpec((ROWS, width), step),
            pl.BlockSpec((ROWS, 1), step),
            pl.BlockSpec((1, width), same),
            pl.BlockSpec((ROWS, width), step),
        ]
        + [pl.BlockSpec((ROWS, TRIPLE), step)] * (2 * CHUNKS)
        + [pl.BlockSpec((CHUNKS, width, TRIPLE), lambda i: (0, 0, 0))] * 2,
        out_specs=pl.BlockSpec((ROWS, width), step),
        out_shape=in_hbm((length, width), jnp.bfloat16),
        compiler_params=pltpu.CompilerParams(vmem_limit_bytes=48 * MIB),
        cost_estimate=pl.CostEstimate(
            flops=1, bytes_accessed=1, transcendentals=0
        ),
        name="last",
    )(inputs, scale, gain.reshape(1, width), *from_hbm(state_grad), *from_hbm(*grads, *weights))


def swap(values):
    return lax.ppermute(values, "replica", [(0, 1), (1, 0)])


def shift(values, shards, distance):
    return lax.ppermute(values, "shard", [(i, i ^ distance) for i in range(shards)])


def tie(values, *before):
    return lax.optimization_barrier((values,) + before)[0]


def gather_relative(own, shards, *before):
    line = jnp.stack([own] + [shift(own, shards, k * INNER) for k in range(1, shards // INNER)])
    came = [shift(line, shards, m) for m in range(1, INNER)]
    return jnp.stack([line] + [tie(c, *before) for c in came])


def cross(own, came):
    return [low(wide(own[m]) + wide(came[m])) for m in range(INNER)]


def plane(places, shards):
    return [places[0]] + [shift(places[m], shards, m) for m in range(1, INNER)]


def column(line, shards):
    return [line[0]] + [shift(line[k], shards, k * INNER) for k in range(1, shards // INNER)]


def total_of(parts):
    total = wide(parts[0])
    for part in parts[1:]:
        total = total + wide(part)
    return total


def exchange(pieces, groups):
    return lax.all_to_all(pieces, "shard", 0, 0, axis_index_groups=groups)


def inner_groups(shards):
    return [[o * INNER + i for i in range(INNER)] for o in range(shards // INNER)]


def natural_halves(own):
    other = swap(own)
    first = lax.axis_index("replica") == 0
    return jnp.where(first, own, other), jnp.where(first, other, own)


def scatter_halves(own, other):
    halves = []
    for part in (own, other):
        whole = jnp.swapaxes(part, 0, 1).reshape((-1,) + part.shape[2:])
        halves.append(wide(lax.psum_scatter(whole, "shard", scatter_dimension=0, tiled=True))[0])
    return lax.psum(tuple(halves), "replica")


def body(
    copies,
    shards,
    inputs,
    cotangent,
    block_ids,
    buckets,
    early_gain,
    query_weight,
    key_weight,
    value_weight,
    mixing_weight,
    relative_table,
    later_gain,
    up_weight,
    down_weight,
):
    length, width = inputs.shape
    half = width // 2
    hidden = up_weight.shape[1]
    bucket_count, heads = relative_table.shape
    offsets = buckets.shape[0]
    relative = copies == 2 and width // shards % 16 == 0 and INNER * hidden == shards * width
    me = lax.axis_index("replica") if relative else jnp.int32(0)
    spot = lax.axis_index("shard") if relative else jnp.int32(0)

    def parts_of(h):
        column = lambda w, c: lax.dynamic_slice_in_dim(w, c, half, 1)
        groups = up_weight.shape[1] // width
        return jnp.concatenate(
            [column(down_weight, h * half), column(mixing_weight, h * half)]
            + [column(up_weight, (h * groups + j) * half) for j in range(groups)],
            axis=0,
        )

    def triples_of(h):
        weights = (query_weight, key_weight, value_weight)
        starts = [(chunk + CHUNKS * h) * PAIR for chunk in range(CHUNKS)]
        return jnp.stack(
            [
                jnp.concatenate([lax.dynamic_slice_in_dim(w, at, PAIR, 1) for w in weights], axis=1)
                for at in starts
            ]
        )

    outer = shards // INNER
    if relative:
        feed_part, triple_part = pack(
            me.astype(jnp.int32).reshape(1), query_weight, key_weight, value_weight, mixing_weight, up_weight, down_weight
        )
        gathered = lax.all_gather(feed_part, ("shard", "replica"), axis=0, tiled=True)
    else:
        gathered = lax.all_gather(jnp.stack([parts_of(0), parts_of(1)]), "shard", axis=0, tiled=True)
    gathered = gathered.reshape(shards, 2, -1, half)

    normed, turned, early_scale, across, upright = prepare(inputs, early_gain, block_ids)
    tiles = length // TILE
    final = across.reshape(length // SLAB, SLAB)[:, SLAB - 1]
    counts = (final[TILE // SLAB - 1 :: TILE // SLAB] + SLAB - 1) // SLAB
    starts = jnp.arange(tiles, dtype=jnp.int32) * TILE
    uses = jnp.sum((starts[:, None] < final[None, :]).astype(jnp.int32), axis=1)
    place_of = jnp.stack([me, spot % INNER, spot // INNER])
    meta = jnp.concatenate([place_of, counts, uses]).astype(jnp.int32)

    onehot = (buckets[:, None] == jnp.arange(bucket_count, dtype=jnp.int32)[None, :]).astype(jnp.float32)
    mirrored = (buckets[::-1][:, None] == jnp.arange(bucket_count, dtype=jnp.int32)[None, :]).astype(jnp.float32)
    spare = ((0, 0), (0, 2 * length - offsets))
    forward_table, backward_table = [
        skew(jnp.pad(jnp.dot(hot, relative_table, precision=HIGH).T, spare), length) for hot in (onehot, mirrored)
    ]

    def natural(values):
        every = lax.all_gather(values, "shard", axis=0)
        return jnp.swapaxes(every.reshape((outer, INNER) + values.shape), 0, 1)

    if relative:
        own = gather_relative(triple_part, shards, forward_table, backward_table, normed, turned, upright, meta)
        other = swap(own)
    else:
        own, other = natural(triples_of(0)), natural(triples_of(1))

    held = [attend_forward(0, relative, meta, normed, own, upright, forward_table)]
    other = tie(other, held[0][2])
    held.append(attend_forward(1, relative, meta, normed, other, upright, forward_table))
    layer_output, state_grad, attended_grad, later_part, rest, down_own, down_other = feed_forward(
        relative, meta, inputs, cotangent, [h[1] for h in held], later_gain, gathered
    )

    grads, diagonals, gains = {}, {}, {}

    def backward(c, side, *before):
        qkv, attended, logs, matrices = held[side]
        grad = tie(attended_grad, *before) if before else attended_grad
        grads[c, side], weight, diagonals[c, side], gains[c, side] = attend_backward(
            c, side, relative, shards, meta, qkv, attended, grad, across, logs, backward_table, turned,
            matrices,
        )
        return weight, diagonals[c, side]

    def finish(*before):
        scale = tie(early_scale, *before) if before else early_scale
        ordered = [grads[c, side] for c in range(CHUNKS) for side in range(2)]
        return last(inputs, scale, early_gain, state_grad, ordered, [h[3] for h in held])

    rows = width // shards

    def vector_of():
        early_part = sum(gains.values()).reshape(-1) / early_gain
        sides = [jnp.concatenate([diagonals[c, side] for c in range(CHUNKS)], axis=0) for side in range(2)]
        first = me == 0
        stacked = jnp.concatenate([jnp.where(first, *sides), jnp.where(first, *sides[::-1])], axis=0)[:, :offsets]
        table_part = lax.dot_general(mirrored, stacked, (((0,), (1,)), ((), ())), precision=HIGH)
        return jnp.concatenate([early_part, later_part.reshape(-1), table_part.reshape(-1)])

    def small_sums():
        vector = vector_of()
        vector = jnp.pad(vector, (0, SMALL * half - vector.shape[0])).reshape(SMALL, half)
        high = low(vector)
        return jnp.concatenate([high, low(vector - wide(high))], axis=0)

    def halve(sums):
        vector = sums[:, :SMALL] + sums[:, SMALL:]
        high = low(vector)
        return jnp.concatenate([high, low(vector - wide(high))], axis=1)

    if relative:
        share = lax.psum_scatter(
            rest.reshape((2 * shards,) + rest.shape[2:]), ("shard", "replica"), scatter_dimension=0, tiled=True
        )[0]
        down_came = swap(down_other)
        other, done = backward(0, 1)
        came = swap(other)
        down_came = tie(down_came, done)
        down_pieces = exchange(
            low(wide(down_own) + wide(down_came)), inner_groups(shards)
        )
        own, done = backward(0, 0, done, down_came)
        places = cross(own, tie(came, done))
        plane0 = plane(places, shards)
        other, done = backward(1, 1, done, *places)
        came1 = swap(other)
        own1, done = backward(1, 0, done)
        down_line = low(jnp.sum(wide(tie(down_pieces, done)), axis=0))
        line0 = low(total_of([tie(p, done) for p in plane0]))
        early = jnp.concatenate([down_line, line0], axis=1)
        lines = lax.optimization_barrier(([early[k] for k in range(early.shape[0])], done))
        early_column = column(lines[0], shards)
        other, done = backward(2, 1, *lines[0], lines[1])
        came1 = tie(came1, done)
        came2 = swap(other)
        own2, done = backward(2, 0, done)
        came2 = tie(came2, done)
        places = [jnp.concatenate(p, axis=1) for p in zip(cross(own1, came1), cross(own2, came2), strict=True)]
        small = small_sums()
        late = [jnp.concatenate([p, jnp.broadcast_to(small, p.shape[:1] + small.shape)], axis=1) for p in places]
        late_plane = plane(late, shards)
        early = total_of([tie(p, done) for p in early_column])
        input_gradient = finish(*late, early)
        late = wide(late[0])
        for p in late_plane[1:]:
            late = late + wide(tie(p, input_gradient))
        late = jnp.concatenate([low(late[:, : 2 * rows]), halve(late[:, 2 * rows :])], axis=1)
        late = natural_halves(total_of(column(late, shards)))
        early = natural_halves(early)
        share = [wide(h) for h in natural_halves(tie(share, input_gradient))]
        small = late[0][2 * rows :] + late[1][2 * rows :]
        small = (small[:SMALL] + small[SMALL:]).reshape(-1)
        down_share = [h[:-rows] for h in early]
        shares = [[h[-rows:] for h in early], [h[:rows] for h in late], [h[rows : 2 * rows] for h in late]]
    else:
        shares = []
        for c in range(CHUNKS):
            other, _ = backward(c, 1)
            own, _ = backward(c, 0)
            shares.append(scatter_halves(own, other))
        input_gradient = finish()
        both = lax.psum_scatter(rest, "shard", scatter_dimension=0, tiled=True)[0]
        share = lax.psum((wide(both[0]), wide(both[1])), "replica")
        down_share = [
            lax.psum(
                wide(
                    lax.psum_scatter(
                        jnp.swapaxes(d, 0, 1).reshape((shards,) + d.shape[2:]), "shard", scatter_dimension=0, tiled=True
                    )
                )[0],
                "replica",
            )
            for d in (down_own, down_other)
        ]
        small = lax.psum(vector_of(), ("replica", "shard"))

    early_total, later_total = small[:width], small[width : 2 * width]
    table_total = small[2 * width : 2 * width + relative_table.size].reshape(bucket_count, heads)

    groups = hidden // width
    down_share = jnp.concatenate(down_share, axis=1)
    mixing_share = jnp.concatenate([share[0][:rows], share[1][:rows]], axis=1)
    up_share = jnp.concatenate(
        [share[h][rows * (1 + j) : rows * (2 + j)] for h in range(2) for j in range(groups)], axis=1
    )
    triples = [
        jnp.concatenate(
            [shares[c][h][:, n * PAIR : (n + 1) * PAIR] for h in range(2) for c in range(CHUNKS)], axis=1
        )
        for n in range(3)
    ]
    return (
        layer_output,
        input_gradient,
        early_total,
        triples[0],
        triples[1],
        triples[2],
        mixing_share,
        table_total,
        later_total,
        up_share,
        down_share,
    )


def solution(mesh):
    rows = P(("replica", "shard"), None)
    split = P("shard", None)
    same = P()
    return jax.shard_map(
        functools.partial(body, mesh.shape["replica"], mesh.shape["shard"]),
        mesh=mesh,
        in_specs=(rows, rows, rows, same, same, split, split, split, split, same, same, split, split),
        out_specs=(rows, rows, same, split, split, split, split, same, same, split, split),
        check_vma=False,
    )
```
